512 devices in a mesh: leaf: 128 (over z, y, core), sep: 4 (over x).
Axes of the slice: x: 4, y: 8, z: 8, core: 2. Of those that a mesh axis runs over, the one named last changes fastest.
Arguments:
- leaf_source: float32 [128, 640, 256], P('leaf', 'sep'), may hold values from -6 to 6
- leaf_inverse: float32 [128, 640, 640], P('leaf', 'sep'), as said below
- leaf_update: float32 [128, 896, 640], P('leaf', None, 'sep'), as said below
- row_lists: int32 [128, 896], P('leaf'), may hold values from 0 to 255
- row_counts: int32 [128, 7], P('leaf'), may hold values from 1 to 128, as said below
- separator_source: float32 [128, 256, 256], P('leaf', 'sep'), may hold values from -6 to 6
- separator_inverse: float32 [128, 256, 256], P('leaf'), as said below
- separator_coupling: float32 [128, 256, 256], P('leaf'), may hold values from -0.1875 to 0.1875
Outputs:
- leaf_solution: float32 [128, 640, 256], P('leaf', 'sep')
- separator_solution: float32 [128, 256, 256], P('leaf', 'sep')
The draws below stay inside these ranges and needn't reach their ends.
Inputs may be any that keep to these rules, and one draw needn't show every extreme that they name: `leaf_inverse`: each leaf's block is lower triangular, zero above the diagonal, with diagonal entries between 0.6 and 1.4. `separator_inverse`: each block is lower triangular, zero above the diagonal, with diagonal entries between 0.6 and 1.4. `leaf_update`: row r of a leaf's block belongs to the leaf's ancestor of level 1 + r // 128. `row_lists`: entry r names a row of the leaf's ancestor of level 1 + r // 128. `row_counts`: at every level some leaf has 128 live rows.
All inputs are finite; a program needn't handle non-finite values.
Results may differ from the reference program's by a relative error of at most 0.00011.
Values sent between devices are 32-bit elements; how exact they have to be, the bound alone decides.
A program may use at most 64 MiB of HBM per device.

```python
import jax
import jax.numpy as jnp
import numpy as np
from jax import lax

NRHS = 256
LR = 640
W = 256
P_SIZE = 128
NLEAF = 128
LEV = 7
UROWS = 896


def triangle(key, order, spread):
    entries = jax.random.normal(key, (NLEAF, order, order), jnp.float32) * spread
    diagonal = jax.random.uniform(jax.random.fold_in(key, 11), (NLEAF, order, 1), jnp.float32, 0.6, 1.4)
    row_ids = lax.broadcasted_iota(jnp.int32, (order, order), 0)
    col_ids = lax.broadcasted_iota(jnp.int32, (order, order), 1)
    return jnp.where(row_ids > col_ids, entries, jnp.where(row_ids == col_ids, diagonal, 0.0))


def draw_leaf_inverse(key, part):
    return triangle(key, LR, LR ** (-0.5))


def draw_separator_inverse(key, part):
    return triangle(key, W, (0.5 / W) ** 0.5)


def draw_leaf_update(key, part):
    entries = jax.random.normal(key, (NLEAF, UROWS, LR), jnp.float32)
    height_index = (lax.broadcasted_iota(jnp.int32, (UROWS, 1), 0) // P_SIZE).astype(jnp.float32)
    return entries * jnp.exp2(-0.5 * height_index) * LR ** (-0.5)


def draw_row_counts(key, part):
    counts = jax.random.randint(key, (NLEAF, LEV), 1, P_SIZE + 1)
    chosen = jax.random.randint(jax.random.fold_in(key, 7), (LEV,), 0, NLEAF)
    return jnp.where(jnp.arange(NLEAF)[:, None] == chosen[None, :], P_SIZE, counts).astype(jnp.int32)


def plant(result, key, low, top_value):
    dims = result.shape
    place = [jax.random.randint(jax.random.fold_in(key, axis), (), 0, dims[axis]) for axis in range(len(dims))]
    result = result.at[tuple(place)].set(low)
    longest = dims.index(max(dims))
    place[longest] = (place[longest] + 1) % dims[longest]
    return result.at[tuple(place)].set(top_value)


def level_of(stream_key, shape, cuts, low, top_value):
    def one(position, blocks):
        draws = jax.random.uniform(jax.random.fold_in(jax.random.fold_in(stream_key, 6), position), (blocks,), jnp.float32, low / len(cuts), top_value / len(cuts))
        return jnp.repeat(jnp.exp(draws), shape[position] // blocks).reshape((-1,) + (1,) * (len(shape) - position - 1))

    level = one(*cuts[0])
    for cut in cuts[1:]:
        level = level * one(*cut)
    return level


def centred(own_key, dims, width, limit, split=(), held_as=jnp.bfloat16):
    array = width * jax.random.normal(own_key, dims, jnp.float32)
    if split:
        array = array * level_of(own_key, dims, split, -0.22, 0.18)
    return jnp.clip(array, -limit, limit).astype(held_as)


def setup_inputs(seed: int = 0) -> dict:
    streams_of = jax.random.split(jax.random.key(seed), 9)
    leaf_source = centred(streams_of[0], (NLEAF, LR, NRHS), 1.0, 6.0, ((0, 128), (1, 4)), jnp.float32)
    leaf_inverse = draw_leaf_inverse(jax.random.fold_in(streams_of[8], 71), 0)
    leaf_update = draw_leaf_update(jax.random.fold_in(streams_of[8], 71), 0)
    row_lists = plant(jax.random.randint(streams_of[3], (NLEAF, UROWS), 0, W), jax.random.fold_in(streams_of[3], 1), 0, W - 1).astype(jnp.int32)
    row_counts = draw_row_counts(jax.random.fold_in(streams_of[8], 71), 0)
    separator_source = centred(streams_of[5], (NLEAF, W, NRHS), 1.0, 6.0, ((0, 128), (1, 4)), jnp.float32)
    separator_inverse = draw_separator_inverse(jax.random.fold_in(streams_of[8], 71), 0)
    separator_coupling = centred(streams_of[7], (NLEAF, W, W), (4 * W) ** -0.5, 0.1875, ((0, 128),), jnp.float32)
    return {"leaf_source": leaf_source, "leaf_inverse": leaf_inverse, "leaf_update": leaf_update, "row_lists": row_lists, "row_counts": row_counts, "separator_source": separator_source, "separator_inverse": separator_inverse, "separator_coupling": separator_coupling}


highest = lax.Precision.HIGHEST


def reference(leaf_source, leaf_inverse, leaf_update, row_lists, row_counts, separator_source, separator_inverse, separator_coupling):
    leaf_y = jnp.einsum("lij,ljn->lin", leaf_inverse, leaf_source, precision=highest)
    slot_index = np.arange(UROWS) % P_SIZE
    block_index = np.arange(UROWS) // P_SIZE
    live_rows = slot_index[None, :] < row_counts[:, block_index]
    update_terms = jnp.einsum("lrj,ljn->lrn", leaf_update, leaf_y, precision=highest)
    update_terms = jnp.where(live_rows[:, :, None], update_terms, 0.0)
    targets = row_lists.reshape(NLEAF, LEV, P_SIZE)
    picker = (jnp.arange(W, dtype=jnp.int32)[None, None, :, None] == targets[:, :, None, :]).astype(jnp.float32)
    densified = jnp.einsum("lkwp,lkpn->lkwn", picker, update_terms.reshape(NLEAF, LEV, P_SIZE, NRHS), precision=highest)
    solved_levels = []
    previous_owners = None
    for height in range(1, LEV + 1):
        groups = NLEAF >> height
        owners = np.arange(groups) * 2 ** height + 2 ** (height - 1)
        gathered = densified[:, height - 1].reshape(groups, 2 ** height, W, NRHS).sum(axis=1)
        residual = separator_source[owners] - gathered
        if height > 1:
            pushed = jnp.einsum("gvw,gwn->gvn", separator_coupling[previous_owners], solved_levels[-1], precision=highest)
            residual = residual - pushed.reshape(groups, 2, W, NRHS).sum(axis=1)
        solved_levels.append(jnp.einsum("gvw,gwn->gvn", separator_inverse[owners], residual, precision=highest))
        previous_owners = owners
    separator_solution = jnp.zeros((NLEAF, W, NRHS), jnp.float32)
    solution_levels = [None] * LEV
    above_x = None
    for height in range(LEV, 0, -1):
        owners = np.arange(NLEAF >> height) * 2 ** height + 2 ** (height - 1)
        target = solved_levels[height - 1]
        if height < LEV:
            parents = jnp.repeat(above_x, 2, axis=0)
            target = target - jnp.einsum("gvw,gvn->gwn", separator_coupling[owners], parents, precision=highest)
        above_x = jnp.einsum("gvw,gvn->gwn", separator_inverse[owners], target, precision=highest)
        solution_levels[height - 1] = above_x
        separator_solution = separator_solution.at[owners].set(above_x)
    ancestors = jnp.stack([solution_levels[height - 1][np.arange(NLEAF) >> height] for height in range(1, LEV + 1)], axis=1)
    picked = jnp.einsum("lkwp,lkwn->lkpn", picker, ancestors, precision=highest).reshape(NLEAF, UROWS, NRHS)
    picked = jnp.where(live_rows[:, :, None], picked, 0.0)
    leaf_w = leaf_y - jnp.einsum("lrj,lrn->ljn", leaf_update, picked, precision=highest)
    leaf_solution = jnp.einsum("lij,lin->ljn", leaf_inverse, leaf_w, precision=highest)
    return leaf_solution, separator_solution
```

```python
import functools

import jax
import jax.numpy as jnp
from jax import lax
from jax.experimental import pallas as pl
from jax.experimental.pallas import tpu as pltpu
from jax.sharding import PartitionSpec as P

MESH = pl.DeviceIdType.MESH
F32 = jnp.float32
BF16 = jnp.bfloat16


def split(x):
    high = x.astype(BF16)
    return high, (x - high.astype(F32)).astype(BF16)


def mm(a, b, ca=1, cb=0):
    return lax.dot_general(a, b, (((ca,), (cb,)), ((), ())), preferred_element_type=F32)


def mm3(a, b, ca=1, cb=0):
    ah, al = split(a)
    bh, bl = split(b)
    return mm(ah, bh, ca, cb) + (mm(al, bh, ca, cb) + mm(ah, bl, ca, cb))


def stacked(matrix):
    high, low = split(matrix)
    return jnp.concatenate([high, high, low], axis=0)


def chain(rows, stack):
    high, low = split(rows)
    return mm(jnp.concatenate([high, low, high], axis=1), stack)


def level_of(index, depth):
    level = jnp.int32(1)
    half = jnp.int32(1)
    for k in range(1, depth + 1):
        hit = (lax.rem(index, 2**k) == 0).astype(jnp.int32)
        level = level + hit
        half = half + hit * 2 ** (k - 1)
    return level, half


def kernel(
    depth,
    counts,
    src,
    inv,
    upd,
    lists,
    ssrc,
    sinv,
    cpl,
    out,
    sol,
    S,
    sp,
    ssb,
    MT3,
    M3,
    N3,
    pick,
    yT,
    updh,
    updl,
    TT,
    rsb,
    D,
    up,
    uo,
    R,
    U,
    V,
    dn,
    pkb,
    XB,
    fb,
    xp,
    xob,
    agS,
    agR,
    ssS,
    ssR,
    rsS,
    rsR,
    eS,
    pS,
    upR,
    dS,
    dnR,
    pkS,
    pkR,
    fS,
    fR,
    xS,
    xR,
):
    l = lax.axis_index("leaf")
    q = lax.axis_index("sep")
    nsep = 4
    rows = src.shape[0]
    cols = ssrc.shape[0]
    cap = lists.shape[1] // depth
    lam, half = level_of(l, depth)
    even = lax.rem(l, 2) == 0
    odd = lax.rem(l, 2) == 1
    lam_pair, _ = level_of(l - 1, depth)
    low_half = lax.div(half, 2)
    right = (lax.rem(l, 4 * half) >= 2 * half).astype(jnp.int32)
    parent = l + half - 2 * half * right
    is_owner = l > 0
    has_parent = lam < depth
    even_owner = jnp.logical_and(even, is_owner)
    pair = l + 1 - 2 * lax.rem(l, 2)

    def at_sep(d):
        return (l, lax.rem(q + d, nsep))

    def hello(device):
        pl.semaphore_signal(barrier, inc=1, device_id=device, device_id_type=MESH)

    def rcopy(a, b, ss, rs, device):
        return pltpu.make_async_remote_copy(
            src_ref=a, dst_ref=b, send_sem=ss, recv_sem=rs, device_id=device, device_id_type=MESH
        )

    barrier = pltpu.get_barrier_semaphore()
    for d in range(1, nsep):
        hello(at_sep(d))
    hello((pair, q))

    @pl.when(has_parent)
    def _():
        hello((parent, q))

    @pl.when(even_owner)
    def _():
        hello((l - low_half, q))
        hello((l + low_half, q))

    own = pl.ds(pl.multiple_of(q * rows, 8), rows)
    mine = pl.ds(pl.multiple_of(q * cols, 8), cols)
    S[own, :] = src[...]
    for j in range(1, nsep):

        @pl.when(j > q)
        def _():
            S[j * rows : (j + 1) * rows, :] = jnp.zeros((rows, S.shape[1]), F32)

    sp[...] = jnp.zeros_like(sp)
    sp[:, :cols] = ssrc[...].T
    ssb[q] = sp[mine, :]

    peers = 4 + has_parent.astype(jnp.int32) + 2 * even_owner.astype(jnp.int32)
    pl.semaphore_wait(barrier, peers)

    def ag(d):
        return rcopy(S.at[own, :], S.at[own, :], agS.at[d], agR.at[d], at_sep(d))

    for d in (2, 1, 3):

        @pl.when(q + d < nsep)
        def _():
            ag(d).start()

    def ssx(d):
        to = lax.rem(q + d, nsep)
        return rcopy(
            sp.at[pl.ds(pl.multiple_of(to * cols, 8), cols), :],
            ssb.at[q],
            ssS.at[d],
            ssR.at[d],
            at_sep(d),
        )

    for d in range(1, nsep):
        ssx(d).start()

    wi = lax.broadcasted_iota(jnp.int32, (pick.shape[1], cap), 0)
    pi = lax.broadcasted_iota(jnp.int32, (pick.shape[1], cap), 1)
    for j in range(depth):
        hit = jnp.logical_and(wi == lists[0:1, j * cap : (j + 1) * cap], pi < counts[0, j])
        pick[j] = jnp.where(hit, 1.0, 0.0).astype(BF16)
    uh, ul = split(upd[...])
    updh[...] = uh
    updl[...] = ul
    M = mm3(cpl[...], sinv[...])
    M3[...] = stacked(M)
    MT3[...] = stacked(M.T)
    N3[...] = stacked(mm3(sinv[...], sinv[...], 0, 0))

    for d in range(1, nsep):

        @pl.when(q - d >= 0)
        def _():
            ag(d).wait_recv()

    yT[...] = mm3(inv[...], S[...]).T

    def rs(j, d):
        to = lax.rem(q + d, nsep)
        return rcopy(
            TT.at[j, pl.ds(pl.multiple_of(to * cols, 8), cols), :],
            rsb.at[j, d],
            rsS.at[j, d],
            rsR.at[j, d],
            at_sep(d),
        )

    yh, yl = split(yT[...])
    for j in range(depth):
        bh = updh[j * cap : (j + 1) * cap, :]
        bl = updl[j * cap : (j + 1) * cap, :]
        TT[j] = mm(yh, bh, 1, 1) + (mm(yl, bh, 1, 1) + mm(yh, bl, 1, 1))
        for d in (2, 1, 3):
            rs(j, d).start()

    for d in range(1, nsep):
        ssx(d).wait_recv()
    sT = jnp.concatenate([ssb[i][:, :cols] for i in range(nsep)], axis=1)

    def to_pair(j):
        return rcopy(D.at[j], up.at[0, j], eS.at[j], upR.at[0, j], (pair, q))

    def to_parent(j):
        return rcopy(uo.at[j], up.at[right, j], pS.at[j], upR.at[right, j], (parent, q))

    def wait_up(side, j):
        rcopy(D.at[0], up.at[side, j], eS.at[0], upR.at[side, j], (pair, q)).wait_recv()

    for j in range(1, depth + 1):
        for d in range(1, nsep):
            rs(j - 1, d).wait_recv()
        t = (TT[j - 1, mine, :] + rsb[j - 1, 1]) + (rsb[j - 1, 2] + rsb[j - 1, 3])
        th, tl = split(t)
        Dj = mm(th, pick[j - 1], 1, 1) + mm(tl, pick[j - 1], 1, 1)

        @pl.when(even)
        def _():
            D[j] = Dj
            to_pair(j).start()

        @pl.when(odd)
        def _():
            wait_up(0, j)
            total = up[0, j] + Dj
            if j == 1:
                R[...] = sT - total
                U[...] = chain(R[...], MT3[...])
            else:
                uo[j] = total + U[...] if j == 2 else total
                to_parent(j).start()

    @pl.when(even_owner)
    def _():
        wait_up(0, lam)
        wait_up(1, lam)
        R[...] = sT - (up[0, lam] + up[1, lam])

        @pl.when(has_parent)
        def _():
            U[...] = chain(R[...], MT3[...])

        for i in range(1, depth - 1):
            j = lam + i

            @pl.when(j <= depth)
            def _():
                wait_up(0, j)
                wait_up(1, j)
                total = up[0, j] + up[1, j]
                uo[j] = total + U[...] if i == 1 else total
                to_parent(j).start()

    @pl.when(is_owner)
    def _():
        V[...] = chain(R[...], N3[...])

    def to_child(j, side):
        device = (l - low_half + half * side, q)
        return rcopy(dn.at[j], dn.at[j], dS.at[side, j], dnR.at[j], device)

    def down_pair(j):
        return rcopy(dn.at[j], dn.at[j], dS.at[0, j], dnR.at[j], (pair, q))

    def forward(j):
        @pl.when(even_owner)
        def _():
            to_child(j, 0).start()
            to_child(j, 1).start()

        @pl.when(jnp.logical_and(odd, j < lam_pair))
        def _():
            down_pair(j).start()

    def pk(j, d):
        place = pkb.at[mine, (j - 1) * cap : j * cap]
        return rcopy(place, place, pkS.at[j, d], pkR.at[j, d], at_sep(d))

    for j in range(depth, 0, -1):

        @pl.when(j != lam)
        def _():
            down_pair(j).wait_recv()

        if j == depth:

            @pl.when(lam == depth)
            def _():
                dn[j] = V[...]
                forward(j)

        if j > 1:

            @pl.when(j == lam + 1)
            def _():
                dn[j - 1] = V[...] - chain(dn[j], M3[...])
                forward(j - 1)

        @pl.when(j > lam)
        def _():
            forward(j)

        xh, xl = split(dn[j])
        pkb[mine, (j - 1) * cap : j * cap] = mm(xh, pick[j - 1]) + mm(xl, pick[j - 1])
        for d in (2, 1, 3):
            pk(j, d).start()

    def xo(d):
        to = lax.rem(q + d, nsep)
        return rcopy(
            xp.at[pl.ds(pl.multiple_of(to * cols, 8), cols), :],
            xob.at[q],
            xS.at[d],
            xR.at[d],
            at_sep(d),
        )

    xp[...] = jnp.zeros_like(xp)

    @pl.when(is_owner)
    def _():
        xp[:, :cols] = dn[lam].T

    xob[q] = xp[mine, :]
    for d in range(1, nsep):
        xo(d).start()

    for j in range(depth, 0, -1):
        for d in range(1, nsep):
            pk(j, d).wait_recv()
    ph, pw = split(pkb[...])
    wT = yT[...] - (mm(ph, updh[...]) + (mm(pw, updh[...]) + mm(ph, updl[...])))
    XB[...] = mm3(inv[...], wT.T, 0, 0)

    def fin(d):
        to = q - d
        return rcopy(
            XB.at[pl.ds(pl.multiple_of(to * rows, 8), rows), :],
            fb.at[d],
            fS.at[d],
            fR.at[d],
            (l, to),
        )

    for d in (2, 1, 3):

        @pl.when(q - d >= 0)
        def _():
            fin(d).start()

    for d in range(1, nsep):
        xo(d).wait_recv()
    sol[...] = jnp.concatenate([xob[i][:, :cols] for i in range(nsep)], axis=1)
    out[...] = XB[own, :]
    for d in range(1, nsep):

        @pl.when(q + d < nsep)
        def _():
            rcopy(XB.at[own, :], fb.at[d], fS.at[d], fR.at[d], at_sep(d)).wait_recv()
            out[...] += fb[d]

    for d in range(1, nsep):

        @pl.when(q + d < nsep)
        def _():
            ag(d).wait_send()

        @pl.when(q - d >= 0)
        def _():
            fin(d).wait_send()

        ssx(d).wait_send()
        xo(d).wait_send()
        for j in range(1, depth + 1):
            rs(j - 1, d).wait_send()
            pk(j, d).wait_send()
    for j in range(1, depth + 1):

        @pl.when(even)
        def _():
            to_pair(j).wait_send()

        @pl.when(jnp.logical_and(is_owner, j > lam))
        def _():
            to_parent(j).wait_send()

        @pl.when(jnp.logical_and(even_owner, j >= lam))
        def _():
            to_child(j, 0).wait_send()
            to_child(j, 1).wait_send()

        @pl.when(jnp.logical_and(odd, j < lam_pair))
        def _():
            down_pair(j).wait_send()


def per_device(src, inv, upd, lists, counts, ssrc, sinv, cpl):
    depth = counts.shape[1]
    rows, n = src.shape[1:]
    order = inv.shape[2]
    urows = upd.shape[1]
    cols = ssrc.shape[1]
    w = sinv.shape[1]
    cap = urows // depth
    nsep = 4
    slots = depth + 1
    dma = pltpu.SemaphoreType.DMA
    vm = pl.BlockSpec(memory_space=pltpu.VMEM)
    out, sol = pl.pallas_call(
        functools.partial(kernel, depth),
        out_shape=(
            jax.ShapeDtypeStruct((rows, n), F32),
            jax.ShapeDtypeStruct((cols, n), F32),
        ),
        in_specs=[pl.BlockSpec(memory_space=pltpu.SMEM)] + [vm] * 7,
        out_specs=(vm, vm),
        scratch_shapes=[
            pltpu.VMEM((order, n), F32),
            pltpu.VMEM((n, 128), F32),
            pltpu.VMEM((nsep, cols, 128), F32),
            pltpu.VMEM((3 * w, w), BF16),
            pltpu.VMEM((3 * w, w), BF16),
            pltpu.VMEM((3 * w, w), BF16),
            pltpu.VMEM((depth, w, cap), BF16),
            pltpu.VMEM((n, rows), F32),
            pltpu.VMEM((urows, rows), BF16),
            pltpu.VMEM((urows, rows), BF16),
            pltpu.VMEM((depth, n, cap), F32),
            pltpu.VMEM((depth, nsep, cols, cap), F32),
            pltpu.VMEM((slots, cols, w), F32),
            pltpu.VMEM((2, slots, cols, w), F32),
            pltpu.VMEM((slots, cols, w), F32),
            pltpu.VMEM((cols, w), F32),
            pltpu.VMEM((cols, w), F32),
            pltpu.VMEM((cols, w), F32),
            pltpu.VMEM((slots, cols, w), F32),
            pltpu.VMEM((n, urows), F32),
            pltpu.VMEM((order, n), F32),
            pltpu.VMEM((nsep, rows, n), F32),
            pltpu.VMEM((n, 128), F32),
            pltpu.VMEM((nsep, cols, 128), F32),
            dma((nsep,)),
            dma((nsep,)),
            dma((nsep,)),
            dma((nsep,)),
            dma((depth, nsep)),
            dma((depth, nsep)),
            dma((slots,)),
            dma((slots,)),
            dma((2, slots)),
            dma((2, slots)),
            dma((slots,)),
            dma((slots, nsep)),
            dma((slots, nsep)),
            dma((nsep,)),
            dma((nsep,)),
            dma((nsep,)),
            dma((nsep,)),
        ],
        compiler_params=pltpu.CompilerParams(
            collective_id=0, has_side_effects=True, vmem_limit_bytes=48 * 2**20
        ),
    )(counts, src[0], inv[0], upd[0], lists, ssrc[0], sinv[0], cpl[0])
    return out[None], sol[None]


def solution(mesh):
    placed = (
        P("leaf", "sep", None),
        P("leaf", "sep", None),
        P("leaf", None, "sep"),
        P("leaf", None),
        P("leaf", None),
        P("leaf", "sep", None),
        P("leaf", None, None),
        P("leaf", None, None),
    )
    return jax.shard_map(
        per_device,
        mesh=mesh,
        in_specs=placed,
        out_specs=(P("leaf", "sep", None), P("leaf", "sep", None)),
        check_vma=False,
    )
```

```python
import functools
import types

import jax
import jax.numpy as jnp
from jax import lax
from jax.experimental import pallas as pl
from jax.experimental.pallas import tpu as pltpu
from jax.sharding import PartitionSpec as P

MESH = pl.DeviceIdType.MESH
F32 = jnp.float32
BF16 = jnp.bfloat16
NSEP = 4


def split(x):
    high = x.astype(BF16)
    return high, (x - high.astype(F32)).astype(BF16)


def mm(a, b, ca=1, cb=0):
    return lax.dot_general(a, b, (((ca,), (cb,)), ((), ())), preferred_element_type=F32)


def mm3(a, b, ca=1, cb=0):
    ah, al = split(a)
    bh, bl = split(b)
    return mm(ah, bh, ca, cb) + (mm(al, bh, ca, cb) + mm(ah, bl, ca, cb))


def chain(rows, wh, wl):
    high, low = split(rows)
    m = rows.shape[0]
    both = mm(jnp.concatenate([high, low], axis=0), wh)
    return both[:m] + (both[m:] + mm(high, wl))


def picked_by(rows, picker, cb):
    high, low = split(rows)
    m = rows.shape[0]
    both = mm(jnp.concatenate([high, low], axis=0), picker, 1, cb)
    return both[:m] + both[m:]


def level_of(index, depth):
    level = jnp.int32(1)
    for k in range(1, depth + 1):
        level = level + (lax.rem(index, 2**k) == 0).astype(jnp.int32)
    return level


def kernel(dims, names, *refs):
    ny, nz, depth = dims
    b = types.SimpleNamespace(**dict(zip(names, refs)))
    kp = depth - nz.bit_length() + 1
    l = lax.axis_index("leaf")
    q = lax.axis_index("sep")
    c = lax.rem(l, 2)
    y = lax.rem(lax.div(l, 2), ny)
    z = lax.div(l, 2 * ny)
    pair = l + 1 - 2 * c
    rows = b.src.shape[0]
    cols = b.ssrc.shape[0]
    w = b.sinv.shape[0]
    cap = b.lists.shape[1] // depth
    rb = cols // ny
    mb = w // ny
    lam = level_of(l, depth)
    plane = level_of(z * 2 * ny, depth)
    core0 = c == 0
    core1 = c == 1
    owner = l > 0

    def when(*conditions):
        return pl.when(functools.reduce(jnp.logical_and, conditions))

    def at_sep(d):
        return (l, lax.rem(q + d, NSEP))

    def y_of(d):
        return lax.rem(y + d, ny)

    def z_of(d):
        return lax.rem(z + d, nz)

    def at_y(d):
        return (l - 2 * y + 2 * y_of(d), q)

    def at_z(d):
        return (l + 2 * ny * (z_of(d) - z), q)

    at_pair = (pair, q)

    def rcopy(a, dst, ss, rs, device):
        return pltpu.make_async_remote_copy(
            src_ref=a, dst_ref=dst, send_sem=ss, recv_sem=rs, device_id=device, device_id_type=MESH
        )

    drains = []

    def later(copy, *conditions):
        drains.append((copy, conditions))

    def ds(index, size):
        return pl.ds(pl.multiple_of(index * size, 8), size)

    barrier = pltpu.get_barrier_semaphore()
    greeted = [at_sep(d) for d in range(1, NSEP)] + [at_pair]
    greeted += [at_y(d) for d in range(1, ny)] + [at_z(d) for d in range(1, nz)]
    for device in greeted:
        pl.semaphore_signal(barrier, inc=1, device_id=device, device_id_type=MESH)

    own = ds(q, rows)
    mine = ds(q, cols)
    b.S[own, :] = b.src[...]
    for j in range(1, NSEP):

        @pl.when(j > q)
        def _():
            b.S[j * rows : (j + 1) * rows, :] = jnp.zeros((rows, b.S.shape[1]), F32)

    b.sp[...] = jnp.zeros_like(b.sp)
    b.sp[:, :cols] = b.ssrc[...].T
    b.ssb[q] = b.sp[mine, :]
    pl.semaphore_wait(barrier, len(greeted))

    def ag(d):
        return rcopy(b.S.at[own, :], b.S.at[own, :], b.agS.at[d], b.agR.at[d], at_sep(d))

    for d in (2, 1, 3):

        @pl.when(q + d < NSEP)
        def _():
            ag(d).start()

        later(functools.partial(ag, d), q + d < NSEP)

    def ssx(d):
        to = lax.rem(q + d, NSEP)
        return rcopy(b.sp.at[ds(to, cols), :], b.ssb.at[q], b.ssS.at[d], b.ssR.at[d], at_sep(d))

    for d in range(1, NSEP):
        ssx(d).start()
        later(functools.partial(ssx, d))

    sinv = b.sinv[...]
    b.Mo[...] = mm3(b.cpl[...], sinv)
    b.No[...] = mm3(sinv, sinv, 0, 0)

    def low_of(k, device, slot, m):
        src, dst = ((b.Mo, b.MB), (b.No, b.NB))[m]
        return rcopy(src, dst.at[k], b.moS.at[m, slot], b.mlR.at[m, k], device)

    def start_both(k, device, slot, *conditions):
        @when(*conditions)
        def _():
            for m in range(2):
                low_of(k, device, slot, m).start()

        for m in range(2):
            later(functools.partial(low_of, k, device, slot, m), *conditions)

    start_both(1, at_pair, 0, core1)
    for k in range(2, kp):
        reach = 2 ** (k - 2)
        slot = 0
        for o in range(-reach, reach):
            if o:
                start_both(k, (l + 2 * o, q), slot, core0, lam == k)
                slot += 1

    for k in range(1, kp):

        @when(lam == k)
        def _():
            b.MB[k] = b.Mo[...]
            b.NB[k] = b.No[...]

    def sc(m, d):
        src, dst = ((b.Mo, b.PM), (b.No, b.PN))[m]
        return rcopy(
            src.at[ds(y_of(d), mb), :], dst.at[lam], b.scS.at[m, d], b.scR.at[m, lam], at_y(d)
        )

    def wait_sc(m, k):
        dst = (b.PM, b.PN)[m]
        rcopy(dst.at[k], dst.at[k], b.scS.at[m, 0], b.scR.at[m, k], at_pair).wait_recv()

    high = jnp.logical_and(core0, jnp.logical_and(lam >= kp, owner))
    for m in range(2):
        has = (high, lam < depth) if m == 0 else (high,)

        @when(*has)
        def _():
            for d in range(1, ny):
                sc(m, d).start()
            dst, src = ((b.PM, b.Mo), (b.PN, b.No))[m]
            dst[lam] = src[ds(y, mb), :]

        for d in range(1, ny):
            later(functools.partial(sc, m, d), *has)

    wi = lax.broadcasted_iota(jnp.int32, (w, cap), 0)
    pi = lax.broadcasted_iota(jnp.int32, (w, cap), 1)
    for j in range(depth):
        hit = jnp.logical_and(wi == b.lists[0:1, j * cap : (j + 1) * cap], pi < b.counts[0, j])
        b.pick[j] = jnp.where(hit, 1.0, 0.0).astype(BF16)
    uh, ul = split(b.upd[...])
    b.updh[...] = uh
    b.updl[...] = ul

    def zm(m, d):
        dst = (b.PM, b.PN)[m]
        return rcopy(dst.at[plane], dst.at[plane], b.zmS.at[m, d], b.zmR.at[m, plane], at_z(d))

    def wait_zm(m, k):
        dst = (b.PM, b.PN)[m]
        rcopy(dst.at[k], dst.at[k], b.zmS.at[m, 0], b.zmR.at[m, k], at_pair).wait_recv()

    size = jnp.int32(1)
    for k in range(kp + 1, depth + 1):
        size = size + (plane >= k).astype(jnp.int32) * 2 ** (k - kp - 1)
    base = z - lax.div(size, 2)

    def in_node(d):
        zd = z_of(d)
        return jnp.logical_and(zd >= base, zd < base + size)

    for m in range(2):
        top = depth - 1 if m == 0 else depth

        @when(core0, y != ny // 2)
        def _():
            wait_sc(m, kp)

        @when(core0, y != 0, plane <= top)
        def _():
            wait_sc(m, plane)

        for d in range(1, nz):
            sends = (core0, plane <= top, in_node(d))

            @when(*sends)
            def _():
                zm(m, d).start()

            later(functools.partial(zm, m, d), *sends)

    def wait_low(k):
        for m, dst in enumerate((b.MB, b.NB)):
            rcopy(dst.at[k], dst.at[k], b.moS.at[m, 0], b.mlR.at[m, k], at_pair).wait_recv()

    def fw(m, lo, hi, i):
        dst = (b.MB, b.NB)[m]
        place = dst.at[lo:hi]
        return rcopy(place, place, b.fwS.at[m, i], b.fwR.at[m, i], at_pair)

    def forward(m, lo, hi, i):
        @when(core0)
        def _():
            fw(m, lo, hi, i).start()

        later(functools.partial(fw, m, lo, hi, i), core0)

    for k in range(2, kp):

        @when(core0, lam != k)
        def _():
            wait_low(k)

    if kp > 2:
        for m in range(2):
            forward(m, 2, kp, 0)

    for d in range(1, NSEP):

        @pl.when(q - d >= 0)
        def _():
            ag(d).wait_recv()

    b.yT[...] = mm3(b.inv[...], b.S[...]).T

    def rs(j, d):
        to = lax.rem(q + d, NSEP)
        return rcopy(
            b.TT.at[j, ds(to, cols), :], b.rsb.at[j, d], b.rsS.at[j, d], b.rsR.at[j, d], at_sep(d)
        )

    yh, yl = split(b.yT[...])
    for j in range(depth):
        bh = b.updh[:, j * cap : (j + 1) * cap]
        bl = b.updl[:, j * cap : (j + 1) * cap]
        b.TT[j] = mm(yh, bh) + (mm(yl, bh) + mm(yh, bl))
        for d in (2, 1, 3):
            rs(j, d).start()
            later(functools.partial(rs, j, d))

    def yg(m, d):
        dst, src = ((b.MB, b.PM), (b.NB, b.PN))[m]
        hi = depth if m == 0 else depth + 1
        return rcopy(
            src.at[kp:hi], dst.at[kp:hi, ds(y, mb), :], b.ygS.at[m, d], b.ygR.at[m, d], at_y(d)
        )

    for m in range(2):
        hi = depth if m == 0 else depth + 1

        @when(core0)
        def _():
            for k in range(kp + 1, hi):

                @pl.when(plane != k)
                def _():
                    wait_zm(m, k)

            for d in range(1, ny):
                yg(m, d).start()
            dst, src = ((b.MB, b.PM), (b.NB, b.PN))[m]
            dst[kp:hi, ds(y, mb), :] = src[kp:hi]

        for d in range(1, ny):
            later(functools.partial(yg, m, d), core0)

    for d in range(1, NSEP):
        ssx(d).wait_recv()
    sT = jnp.concatenate([b.ssb[i][:, :cols] for i in range(NSEP)], axis=1)
    b.sT[...] = sT

    def prepare(k):
        if k < depth:
            mh, ml = split(b.MB[k])
            b.Mh[k] = mh
            b.Ml[k] = ml
            th, tl = split(b.MB[k].T)
            b.Th[k] = th
            b.Tl[k] = tl

    def prepare_n(k):
        nh, nl = split(b.NB[k])
        b.Nh[k] = nh
        b.Nl[k] = nl

    @when(core0)
    def _():
        wait_low(1)

    if kp > 2:

        @when(core1)
        def _():
            for m in range(2):
                fw(m, 2, kp, 0).wait_recv()

    for k in range(1, kp):
        prepare(k)

    half = pl.ds(pl.multiple_of(c * 128, 128), 128)
    other = pl.ds(pl.multiple_of((1 - c) * 128, 128), 128)

    def own_part(k):
        for d in range(1, NSEP):
            rs(k - 1, d).wait_recv()
        t = (b.TT[k - 1, mine, :] + b.rsb[k - 1, 1]) + (b.rsb[k - 1, 2] + b.rsb[k - 1, 3])
        part = jnp.where(lam == k, b.sT[...], 0.0) - picked_by(t, b.pick[k - 1], 1)
        if k > 1:
            part = part - chain(b.RP[k - 1], b.Th[k - 1], b.Tl[k - 1])
        b.RP[k] = part

    def cx(i):
        if i == 0:
            return rcopy(b.RP.at[1], b.R1, b.cxS.at[0], b.cxR.at[0], at_pair)
        lo, hi = ((2, kp + 1), (kp + 1, depth + 1))[i - 1]
        return rcopy(
            b.RP.at[lo:hi, :, other], b.CX.at[lo:hi], b.cxS.at[i], b.cxR.at[i], at_pair
        )

    def hr(i, d):
        lo, hi = ((2, kp + 1), (kp + 1, depth + 1))[i]
        return rcopy(
            b.H.at[lo:hi, ds(y_of(d), rb), :],
            b.HR.at[y, lo:hi],
            b.hrS.at[i, d],
            b.hrR.at[i, d],
            at_y(d),
        )

    def plane_sums(i):
        lo, hi = ((2, kp + 1), (kp + 1, depth + 1))[i]
        cx(i + 1).wait_recv()
        b.H[lo:hi] = b.RP[lo:hi, :, half] + b.CX[lo:hi]
        for d in range(1, ny):
            hr(i, d).start()
            later(functools.partial(hr, i, d))
        b.HR[y, lo:hi] = b.H[lo:hi, ds(y, rb), :]

    own_part(1)
    cx(0).start()
    later(functools.partial(cx, 0))
    for k in range(2, kp + 1):
        own_part(k)
    cx(1).start()
    later(functools.partial(cx, 1))
    plane_sums(0)

    def high_matrices(m):
        hi = depth if m == 0 else depth + 1

        @when(core0)
        def _():
            for d in range(1, ny):
                yg(m, d).wait_recv()

        forward(m, kp, hi, 1)

        @when(core1)
        def _():
            fw(m, kp, hi, 1).wait_recv()

    high_matrices(0)
    for k in range(kp, depth):
        prepare(k)
    for k in range(kp + 1, depth + 1):
        own_part(k)
    cx(2).start()
    later(functools.partial(cx, 2))
    plane_sums(1)

    def br(d):
        return rcopy(
            b.B.at[y_of(d)],
            b.RF.at[2 : kp + 1, ds(y, rb), half],
            b.brS.at[0, d],
            b.brR.at[0, d],
            at_y(d),
        )

    def zr(d):
        return rcopy(b.ZT, b.ZR.at[z], b.zrS.at[d], b.zrR.at[d], at_z(d))

    def bz(d):
        return rcopy(
            b.BZ,
            b.RF.at[kp + 1 : depth + 1, ds(y, rb), half],
            b.brS.at[1, d],
            b.brR.at[1, d],
            at_y(d),
        )

    def back(i):
        lo, hi = ((2, kp + 1), (kp + 1, depth + 1))[i]
        place = b.RF.at[lo:hi, :, half]
        return rcopy(place, place, b.bkS.at[i], b.bkR.at[i], at_pair)

    for d in range(1, ny):
        hr(0, d).wait_recv()
    for k in range(2, kp + 1):
        step = 2 ** (k - 1)
        for g in range(0, ny, step):
            total = b.HR[g, k]
            for i in range(1, step):
                total = total + b.HR[g + i, k]
            for i in range(step):
                b.B[g + i, k - 2] = total
    for d in range(1, ny):
        br(d).start()
        later(functools.partial(br, d))
    b.RF[2 : kp + 1, ds(y, rb), half] = b.B[y]

    for d in range(1, ny):
        hr(1, d).wait_recv()
    total = b.HR[0, kp + 1 : depth + 1]
    for i in range(1, ny):
        total = total + b.HR[i, kp + 1 : depth + 1]
    b.ZT[...] = total
    for d in range(1, nz):
        zr(d).start()
        later(functools.partial(zr, d))
    b.ZR[z] = total

    cx(0).wait_recv()
    for d in range(1, ny):
        br(d).wait_recv()
    back(0).start()
    later(functools.partial(back, 0))
    for k in range(1, kp):
        prepare_n(k)
    high_matrices(1)
    for k in range(kp, depth + 1):
        prepare_n(k)
    back(0).wait_recv()
    b.RF[1] = b.RP[1] + b.R1[...]
    for k in range(1, kp + 1):
        b.V[k] = chain(b.RF[k], b.Nh[k], b.Nl[k])

    for d in range(1, nz):
        zr(d).wait_recv()
    for k in range(kp + 1, depth + 1):
        step = 2 ** (k - kp)
        first = z - lax.rem(z, step)
        total = b.ZR[first, k - kp - 1]
        for i in range(1, step):
            total = total + b.ZR[first + i, k - kp - 1]
        b.BZ[k - kp - 1] = total
    for d in range(1, ny):
        bz(d).start()
        later(functools.partial(bz, d))
    b.RF[kp + 1 : depth + 1, ds(y, rb), half] = b.BZ[...]
    for d in range(1, ny):
        bz(d).wait_recv()
    back(1).start()
    later(functools.partial(back, 1))
    back(1).wait_recv()

    def pk(j, d):
        place = b.pkb.at[mine, (j - 1) * cap : j * cap]
        return rcopy(place, place, b.pkS.at[j, d], b.pkR.at[j, d], at_sep(d))

    for k in range(kp + 1, depth + 1):
        b.V[k] = chain(b.RF[k], b.Nh[k], b.Nl[k])
    for j in range(depth, 0, -1):
        x = b.V[j]
        if j < depth:
            x = x - chain(b.X[j + 1], b.Mh[j], b.Ml[j])
        b.X[j] = x
        b.pkb[mine, (j - 1) * cap : j * cap] = picked_by(x, b.pick[j - 1], 0)
        for d in (2, 1, 3):
            pk(j, d).start()
            later(functools.partial(pk, j, d))

    def xo(d):
        to = lax.rem(q + d, NSEP)
        return rcopy(b.xp.at[ds(to, cols), :], b.xob.at[q], b.xS.at[d], b.xR.at[d], at_sep(d))

    b.xp[...] = jnp.zeros_like(b.xp)

    @when(owner)
    def _():
        b.xp[:, :cols] = b.X[lam].T

    b.xob[q] = b.xp[mine, :]
    for d in range(1, NSEP):
        xo(d).start()
        later(functools.partial(xo, d))

    for j in range(depth, 0, -1):
        for d in range(1, NSEP):
            pk(j, d).wait_recv()
    ph, pw = split(b.pkb[...])
    uh = b.updh[...]
    wT = b.yT[...] - (mm(ph, uh, 1, 1) + (mm(pw, uh, 1, 1) + mm(ph, b.updl[...], 1, 1)))
    b.XB[...] = mm3(b.inv[...], wT.T, 0, 0)

    def fin(d):
        to = q - d
        return rcopy(b.XB.at[ds(to, rows), :], b.fb.at[d], b.fS.at[d], b.fR.at[d], (l, to))

    for d in (2, 1, 3):

        @pl.when(q - d >= 0)
        def _():
            fin(d).start()

        later(functools.partial(fin, d), q - d >= 0)

    for d in range(1, NSEP):
        xo(d).wait_recv()
    b.sol[...] = jnp.concatenate([b.xob[i][:, :cols] for i in range(NSEP)], axis=1)
    b.out[...] = b.XB[own, :]
    for d in range(1, NSEP):

        @pl.when(q + d < NSEP)
        def _():
            rcopy(b.XB.at[own, :], b.fb.at[d], b.fS.at[d], b.fR.at[d], at_sep(d)).wait_recv()
            b.out[...] += b.fb[d]

    for copy, conditions in drains:
        if conditions:

            @when(*conditions)
            def _():
                copy().wait_send()

        else:
            copy().wait_send()


def per_device(ny, nz, src, inv, upd, lists, counts, ssrc, sinv, cpl):
    depth = counts.shape[1]
    rows, n = src.shape[1:]
    order = inv.shape[2]
    urows = upd.shape[1]
    cols = ssrc.shape[1]
    w = sinv.shape[1]
    cap = urows // depth
    s = depth + 1
    kp = depth - nz.bit_length() + 1
    rb = cols // ny
    mb = w // ny
    f = lambda *shape: pltpu.VMEM(shape, F32)
    h = lambda *shape: pltpu.VMEM(shape, BF16)
    dma = lambda *shape: pltpu.SemaphoreType.DMA(shape)
    vm = pl.BlockSpec(memory_space=pltpu.VMEM)
    scratch = dict(
        S=f(order, n),
        sp=f(n, 128),
        ssb=f(NSEP, cols, 128),
        sT=f(cols, w),
        Mo=f(w, w),
        No=f(w, w),
        MB=f(s, w, w),
        NB=f(s, w, w),
        PM=f(s, mb, w),
        PN=f(s, mb, w),
        Mh=h(s, w, w),
        Ml=h(s, w, w),
        Th=h(s, w, w),
        Tl=h(s, w, w),
        Nh=h(s, w, w),
        Nl=h(s, w, w),
        pick=h(depth, w, cap),
        yT=f(n, rows),
        updh=h(rows, urows),
        updl=h(rows, urows),
        TT=f(depth, n, cap),
        rsb=f(depth, NSEP, cols, cap),
        RP=f(s, cols, w),
        R1=f(cols, w),
        CX=f(s, cols, 128),
        H=f(s, cols, 128),
        HR=f(ny, s, rb, 128),
        B=f(ny, kp - 1, rb, 128),
        ZT=f(depth - kp, rb, 128),
        ZR=f(nz, depth - kp, rb, 128),
        BZ=f(depth - kp, rb, 128),
        RF=f(s, cols, w),
        V=f(s, cols, w),
        X=f(s, cols, w),
        pkb=f(n, urows),
        XB=f(order, n),
        fb=f(NSEP, rows, n),
        xp=f(n, 128),
        xob=f(NSEP, cols, 128),
        agS=dma(NSEP),
        agR=dma(NSEP),
        ssS=dma(NSEP),
        ssR=dma(NSEP),
        moS=dma(2, 8),
        mlR=dma(2, s),
        scS=dma(2, ny),
        scR=dma(2, s),
        zmS=dma(2, nz),
        zmR=dma(2, s),
        ygS=dma(2, ny),
        ygR=dma(2, ny),
        fwS=dma(2, 2),
        fwR=dma(2, 2),
        rsS=dma(depth, NSEP),
        rsR=dma(depth, NSEP),
        cxS=dma(3),
        cxR=dma(3),
        hrS=dma(2, ny),
        hrR=dma(2, ny),
        brS=dma(2, ny),
        brR=dma(2, ny),
        zrS=dma(nz),
        zrR=dma(nz),
        bkS=dma(2),
        bkR=dma(2),
        pkS=dma(s, NSEP),
        pkR=dma(s, NSEP),
        xS=dma(NSEP),
        xR=dma(NSEP),
        fS=dma(NSEP),
        fR=dma(NSEP),
    )
    operands = ["counts", "src", "inv", "upd", "lists", "ssrc", "sinv", "cpl", "out", "sol"]
    out, sol = pl.pallas_call(
        functools.partial(kernel, (ny, nz, depth), operands + list(scratch)),
        out_shape=(
            jax.ShapeDtypeStruct((rows, n), F32),
            jax.ShapeDtypeStruct((cols, n), F32),
        ),
        in_specs=[pl.BlockSpec(memory_space=pltpu.SMEM)] + [vm] * 7,
        out_specs=(vm, vm),
        scratch_shapes=list(scratch.values()),
        compiler_params=pltpu.CompilerParams(
            collective_id=0, has_side_effects=True, vmem_limit_bytes=48 * 2**20
        ),
    )(counts, src[0], inv[0], upd[0].T, lists, ssrc[0], sinv[0], cpl[0])
    return out[None], sol[None]


def solution(mesh):
    leaves = mesh.shape["leaf"]
    ny = nz = 8
    if leaves != 2 * ny * nz:
        ny, nz = (leaves // 4, 2)
    placed = (
        P("leaf", "sep", None),
        P("leaf", "sep", None),
        P("leaf", None, "sep"),
        P("leaf", None),
        P("leaf", None),
        P("leaf", "sep", None),
        P("leaf", None, None),
        P("leaf", None, None),
    )
    return jax.shard_map(
        functools.partial(per_device, ny, nz),
        mesh=mesh,
        in_specs=placed,
        out_specs=(P("leaf", "sep", None), P("leaf", "sep", None)),
        check_vma=False,
    )
```

```python
import functools
import types

import jax
import jax.numpy as jnp
from jax import lax
from jax.experimental import pallas as pl
from jax.experimental.pallas import tpu as pltpu
from jax.sharding import PartitionSpec as P

MESH = pl.DeviceIdType.MESH
F32 = jnp.float32
BF16 = jnp.bfloat16
NSEP = 4


def split(x):
    high = x.astype(BF16)
    return high, (x - high.astype(F32)).astype(BF16)


def mm(a, b, ca=1, cb=0):
    return lax.dot_general(a, b, (((ca,), (cb,)), ((), ())), preferred_element_type=F32)


def mm3(a, b, ca=1, cb=0):
    ah, al = split(a)
    bh, bl = split(b)
    return mm(ah, bh, ca, cb) + (mm(al, bh, ca, cb) + mm(ah, bl, ca, cb))


def chain(rows, wh, wl):
    high, low = split(rows)
    m = rows.shape[0]
    both = mm(jnp.concatenate([high, low], axis=0), wh)
    return both[:m] + (both[m:] + mm(high, wl))


def picked_by(rows, picker, cb):
    high, low = split(rows)
    m = rows.shape[0]
    both = mm(jnp.concatenate([high, low], axis=0), picker, 1, cb)
    return both[:m] + both[m:]


def level_of(index, depth):
    level = jnp.int32(1)
    for k in range(1, depth + 1):
        level = level + (lax.rem(index, 2**k) == 0).astype(jnp.int32)
    return level


def kernel(dims, names, *refs):
    ny, nz, depth = dims
    b = types.SimpleNamespace(**dict(zip(names, refs)))
    kp = depth - nz.bit_length() + 1
    l = lax.axis_index("leaf")
    q = lax.axis_index("sep")
    c = lax.rem(l, 2)
    y = lax.rem(lax.div(l, 2), ny)
    z = lax.div(l, 2 * ny)
    pair = l + 1 - 2 * c
    rows = b.xsrc.shape[0]
    cols = b.xssrc.shape[0]
    w = b.xsinv.shape[0]
    cap = b.lists.shape[1] // depth
    rb = cols // ny
    mb = w // ny
    lam = level_of(l, depth)
    plane = level_of(z * 2 * ny, depth)
    core0 = c == 0
    core1 = c == 1
    owner = l > 0

    def when(*conditions):
        return pl.when(functools.reduce(jnp.logical_and, conditions))

    def at_sep(d):
        return (l, lax.rem(q + d, NSEP))

    def y_of(d):
        return lax.rem(y + d, ny)

    def z_of(d):
        return lax.rem(z + d, nz)

    def at_y(d):
        return (l - 2 * y + 2 * y_of(d), q)

    def at_z(d):
        return (l + 2 * ny * (z_of(d) - z), q)

    at_pair = (pair, q)

    def rcopy(a, dst, ss, rs, device):
        return pltpu.make_async_remote_copy(
            src_ref=a, dst_ref=dst, send_sem=ss, recv_sem=rs, device_id=device, device_id_type=MESH
        )

    drains = []

    def later(copy, *conditions):
        drains.append((copy, conditions))

    def ds(index, size):
        return pl.ds(pl.multiple_of(index * size, 8), size)

    own = ds(q, rows)
    mine = ds(q, cols)
    loads = {}
    for i, (name, dst) in enumerate(
        (
            ("src", b.S.at[own, :]),
            ("ssrc", b.ssrc),
            ("sinv", b.sinv),
            ("cpl", b.cpl),
            ("inv", b.inv),
            ("upd", b.upd),
        )
    ):
        loads[name] = pltpu.make_async_copy(getattr(b, "x" + name), dst, b.ldS.at[i])
        loads[name].start()

    barrier = pltpu.get_barrier_semaphore()
    greeted = [at_sep(d) for d in range(1, NSEP)] + [at_pair]
    greeted += [at_y(d) for d in range(1, ny)] + [at_z(d) for d in range(1, nz)]
    for device in greeted:
        pl.semaphore_signal(barrier, inc=1, device_id=device, device_id_type=MESH)

    for j in range(1, NSEP):

        @pl.when(j > q)
        def _():
            b.S[j * rows : (j + 1) * rows, :] = jnp.zeros((rows, b.S.shape[1]), F32)

    b.sp[...] = jnp.zeros_like(b.sp)
    loads["src"].wait()
    pl.semaphore_wait(barrier, len(greeted))

    def ag(d):
        return rcopy(b.S.at[own, :], b.S.at[own, :], b.agS.at[d], b.agR.at[d], at_sep(d))

    for d in (2, 1, 3):

        @pl.when(q + d < NSEP)
        def _():
            ag(d).start()

        later(functools.partial(ag, d), q + d < NSEP)

    def ssx(d):
        to = lax.rem(q + d, NSEP)
        return rcopy(b.sp.at[ds(to, cols), :], b.ssb.at[q], b.ssS.at[d], b.ssR.at[d], at_sep(d))

    loads["ssrc"].wait()
    b.sp[:, :cols] = b.ssrc[...].T
    b.ssb[q] = b.sp[mine, :]
    for d in range(1, NSEP):
        ssx(d).start()
        later(functools.partial(ssx, d))

    loads["sinv"].wait()
    loads["cpl"].wait()
    sinv = b.sinv[...]
    b.Mo[...] = mm3(b.cpl[...], sinv)
    b.No[...] = mm3(sinv, sinv, 0, 0)

    def low_of(k, device, slot, m):
        src, dst = ((b.Mo, b.MB), (b.No, b.NB))[m]
        return rcopy(src, dst.at[k], b.moS.at[m, slot], b.mlR.at[m, k], device)

    def start_both(k, device, slot, *conditions):
        @when(*conditions)
        def _():
            for m in range(2):
                low_of(k, device, slot, m).start()

        for m in range(2):
            later(functools.partial(low_of, k, device, slot, m), *conditions)

    start_both(1, at_pair, 0, core1)
    for k in range(2, kp):
        reach = 2 ** (k - 2)
        slot = 0
        for o in range(-reach, reach):
            if o:
                start_both(k, (l + 2 * o, q), slot, core0, lam == k)
                slot += 1

    for k in range(1, kp):

        @when(lam == k)
        def _():
            b.MB[k] = b.Mo[...]
            b.NB[k] = b.No[...]

    def sc(m, d):
        src, dst = ((b.Mo, b.PM), (b.No, b.PN))[m]
        return rcopy(
            src.at[ds(y_of(d), mb), :], dst.at[lam], b.scS.at[m, d], b.scR.at[m, lam], at_y(d)
        )

    def wait_sc(m, k):
        dst = (b.PM, b.PN)[m]
        rcopy(dst.at[k], dst.at[k], b.scS.at[m, 0], b.scR.at[m, k], at_pair).wait_recv()

    high = jnp.logical_and(core0, jnp.logical_and(lam >= kp, owner))
    for m in range(2):
        has = (high, lam < depth) if m == 0 else (high,)

        @when(*has)
        def _():
            for d in range(1, ny):
                sc(m, d).start()
            dst, src = ((b.PM, b.Mo), (b.PN, b.No))[m]
            dst[lam] = src[ds(y, mb), :]

        for d in range(1, ny):
            later(functools.partial(sc, m, d), *has)

    wi = lax.broadcasted_iota(jnp.int32, (w, cap), 0)
    pi = lax.broadcasted_iota(jnp.int32, (w, cap), 1)
    for j in range(depth):
        hit = jnp.logical_and(wi == b.lists[0:1, j * cap : (j + 1) * cap], pi < b.counts[0, j])
        b.pick[j] = jnp.where(hit, 1.0, 0.0).astype(BF16)
    loads["upd"].wait()
    uh, ul = split(b.upd[...])
    b.updh[...] = uh
    b.updl[...] = ul

    def zm(m, d):
        dst = (b.PM, b.PN)[m]
        return rcopy(dst.at[plane], dst.at[plane], b.zmS.at[m, d], b.zmR.at[m, plane], at_z(d))

    def wait_zm(m, k):
        dst = (b.PM, b.PN)[m]
        rcopy(dst.at[k], dst.at[k], b.zmS.at[m, 0], b.zmR.at[m, k], at_pair).wait_recv()

    size = jnp.int32(1)
    for k in range(kp + 1, depth + 1):
        size = size + (plane >= k).astype(jnp.int32) * 2 ** (k - kp - 1)
    base = z - lax.div(size, 2)

    def in_node(d):
        zd = z_of(d)
        return jnp.logical_and(zd >= base, zd < base + size)

    for m in range(2):
        top = depth - 1 if m == 0 else depth

        @when(core0, y != ny // 2)
        def _():
            wait_sc(m, kp)

        @when(core0, y != 0, plane <= top)
        def _():
            wait_sc(m, plane)

        for d in range(1, nz):
            sends = (core0, plane <= top, in_node(d))

            @when(*sends)
            def _():
                zm(m, d).start()

            later(functools.partial(zm, m, d), *sends)

    def wait_low(k):
        for m, dst in enumerate((b.MB, b.NB)):
            rcopy(dst.at[k], dst.at[k], b.moS.at[m, 0], b.mlR.at[m, k], at_pair).wait_recv()

    def fw(m):
        place = (b.MB, b.NB)[m].at[2:kp]
        return rcopy(place, place, b.fwS.at[m], b.fwR.at[m], at_pair)

    for k in range(2, kp):

        @when(core0, lam != k)
        def _():
            wait_low(k)

    if kp > 2:

        @when(core0)
        def _():
            for m in range(2):
                fw(m).start()

        for m in range(2):
            later(functools.partial(fw, m), core0)

    for d in range(1, NSEP):

        @pl.when(q - d >= 0)
        def _():
            ag(d).wait_recv()

    loads["inv"].wait()
    b.yT[...] = mm3(b.inv[...], b.S[...]).T

    def rs(j, d):
        to = lax.rem(q + d, NSEP)
        return rcopy(
            b.TT.at[j, ds(to, cols), :], b.rsb.at[j, d], b.rsS.at[j, d], b.rsR.at[j, d], at_sep(d)
        )

    yh, yl = split(b.yT[...])
    for j in range(depth):
        bh = b.updh[:, j * cap : (j + 1) * cap]
        bl = b.updl[:, j * cap : (j + 1) * cap]
        b.TT[j] = mm(yh, bh) + (mm(yl, bh) + mm(yh, bl))
        for d in (2, 1, 3):
            rs(j, d).start()
            later(functools.partial(rs, j, d))

    def yg(m, d):
        dst, src = ((b.MB, b.PM), (b.NB, b.PN))[m]
        hi = depth if m == 0 else depth + 1
        return rcopy(
            src.at[kp:hi], dst.at[kp:hi, ds(y, mb), :], b.ygS.at[m, d], b.ygR.at[m, d], at_y(d)
        )

    def gather_high(m):
        hi = depth if m == 0 else depth + 1

        @when(core0)
        def _():
            for k in range(kp + 1, hi):

                @pl.when(plane != k)
                def _():
                    wait_zm(m, k)

            for d in range(1, ny):
                yg(m, d).start()
            dst, src = ((b.MB, b.PM), (b.NB, b.PN))[m]
            dst[kp:hi, ds(y, mb), :] = src[kp:hi]

        for d in range(1, ny):
            later(functools.partial(yg, m, d), core0)

    gather_high(0)
    for d in range(1, NSEP):
        ssx(d).wait_recv()
    sT = jnp.concatenate([b.ssb[i][:, :cols] for i in range(NSEP)], axis=1)
    b.sT[...] = sT

    def prepare(k):
        if k < depth:
            mh, ml = split(b.MB[k])
            b.Mh[k] = mh
            b.Ml[k] = ml
            th, tl = split(b.MB[k].T)
            b.Th[k] = th
            b.Tl[k] = tl

    def prepare_n(k):
        nh, nl = split(b.NB[k])
        b.Nh[k] = nh
        b.Nl[k] = nl

    @when(core0)
    def _():
        wait_low(1)

    if kp > 2:

        @when(core1)
        def _():
            for m in range(2):
                fw(m).wait_recv()

    for k in range(1, kp):
        prepare(k)


    def own_part(k):
        for d in range(1, NSEP):
            rs(k - 1, d).wait_recv()
        t = (b.TT[k - 1, mine, :] + b.rsb[k - 1, 1]) + (b.rsb[k - 1, 2] + b.rsb[k - 1, 3])
        part = jnp.where(lam == k, b.sT[...], 0.0) - picked_by(t, b.pick[k - 1], 1)
        if 1 < k <= kp:
            part = part - chain(b.RP[k - 1], b.Th[k - 1], b.Tl[k - 1])
        b.RP[k] = part

    groups = ((2, kp), (kp, depth), (depth, depth + 1))
    sums_on = (core1, core0, core0)
    sends_to_pair = (core0, core1, core1)

    def r1():
        return rcopy(b.RP.at[1], b.R1, b.cxS.at[3], b.cxR.at[3], at_pair)

    def cx(i):
        lo, hi = groups[i]
        return rcopy(b.RP.at[lo:hi], b.CX.at[lo:hi], b.cxS.at[i], b.cxR.at[i], at_pair)

    def hr(i, d):
        lo, hi = groups[i]
        return rcopy(
            b.H.at[lo:hi, ds(y_of(d), rb), :],
            b.HR.at[y, lo:hi],
            b.hrS.at[i, d],
            b.hrR.at[i, d],
            at_y(d),
        )

    def share(i):
        @when(sends_to_pair[i])
        def _():
            cx(i).start()

        later(functools.partial(cx, i), sends_to_pair[i])

        @when(sums_on[i])
        def _():
            lo, hi = groups[i]
            cx(i).wait_recv()
            b.H[lo:hi] = b.RP[lo:hi] + b.CX[lo:hi]
            for d in range(1, ny):
                hr(i, d).start()
            b.HR[y, lo:hi] = b.H[lo:hi, ds(y, rb), :]

        for d in range(1, ny):
            later(functools.partial(hr, i, d), sums_on[i])

    own_part(1)
    r1().start()
    later(r1)
    for k in range(2, kp):
        own_part(k)
    share(0)
    for k in range(kp, depth):
        own_part(k)
    share(1)
    own_part(depth)
    share(2)
    gather_high(1)

    def br(d):
        place = b.RF.at[2:kp, ds(y, rb), :]
        return rcopy(b.B.at[y_of(d)], place, b.brS.at[d], b.brR.at[d], at_y(d))

    def zr(d):
        return rcopy(b.ZT, b.ZR.at[z], b.zrS.at[d], b.zrR.at[d], at_z(d))

    def bz(d):
        place = b.X.at[kp : depth + 1, ds(y, rb), :]
        return rcopy(b.BZ, place, b.bzS.at[d], b.bzR.at[d], at_y(d))

    def back_low():
        place = b.RF.at[2:kp]
        return rcopy(place, place, b.bkS.at[0], b.bkR.at[0], at_pair)

    def back_high():
        place = b.X.at[kp : depth + 1]
        return rcopy(place, place, b.bkS.at[1], b.bkR.at[1], at_pair)

    @when(core1)
    def _():
        for d in range(1, ny):
            hr(0, d).wait_recv()
        for k in range(2, kp):
            step = 2 ** (k - 1)
            for g in range(0, ny, step):
                total = b.HR[g, k]
                for i in range(1, step):
                    total = total + b.HR[g + i, k]
                for i in range(step):
                    b.B[g + i, k - 2] = total
        for d in range(1, ny):
            br(d).start()
        b.RF[2:kp, ds(y, rb), :] = b.B[y]
        for d in range(1, ny):
            br(d).wait_recv()
        back_low().start()

    for d in range(1, ny):
        later(functools.partial(br, d), core1)
    later(back_low, core1)

    @when(core0)
    def _():
        for d in range(1, ny):
            yg(0, d).wait_recv()
        for k in range(kp, depth):
            prepare(k)
        for i in (1, 2):
            for d in range(1, ny):
                hr(i, d).wait_recv()
        for k in range(kp, depth + 1):
            total = b.HR[0, k]
            for i in range(1, ny):
                total = total + b.HR[i, k]
            if k > kp:
                total = total - chain(b.RZ[k - 1], b.Th[k - 1], b.Tl[k - 1])
                b.ZT[k - kp - 1] = total
            b.RZ[k] = total
        for d in range(1, nz):
            zr(d).start()
        b.ZR[z] = b.ZT[...]

    for d in range(1, nz):
        later(functools.partial(zr, d), core0)

    for k in range(1, kp):
        prepare_n(k)
    r1().wait_recv()
    b.RF[1] = b.RP[1] + b.R1[...]

    @when(core0)
    def _():
        back_low().wait_recv()

    for k in range(1, kp):
        b.V[k] = chain(b.RF[k], b.Nh[k], b.Nl[k])

    @when(core0)
    def _():
        for d in range(1, ny):
            yg(1, d).wait_recv()
        for k in range(kp, depth + 1):
            prepare_n(k)
        for d in range(1, nz):
            zr(d).wait_recv()
        for k in range(kp + 1, depth + 1):
            step = 2 ** (k - kp)
            first = z - lax.rem(z, step)
            total = b.ZR[first, k - kp - 1]
            for i in range(1, step):
                total = total + b.ZR[first + i, k - kp - 1]
            b.RZ[k] = total
        for k in range(kp, depth + 1):
            b.BZ[k - kp] = chain(b.RZ[k], b.Nh[k], b.Nl[k])
        for k in range(depth - 1, kp - 1, -1):
            b.BZ[k - kp] = b.BZ[k - kp] - chain(b.BZ[k + 1 - kp], b.Mh[k], b.Ml[k])
        for d in range(1, ny):
            bz(d).start()
        b.X[kp : depth + 1, ds(y, rb), :] = b.BZ[...]
        for d in range(1, ny):
            bz(d).wait_recv()
        back_high().start()

    for d in range(1, ny):
        later(functools.partial(bz, d), core0)
    later(back_high, core0)

    @when(core1)
    def _():
        back_high().wait_recv()

    def pk(j, d):
        place = b.pkb.at[mine, (j - 1) * cap : j * cap]
        return rcopy(place, place, b.pkS.at[j, d], b.pkR.at[j, d], at_sep(d))

    for j in list(range(kp - 1, 0, -1)) + list(range(depth, kp - 1, -1)):
        if j < kp:
            b.X[j] = b.V[j] - chain(b.X[j + 1], b.Mh[j], b.Ml[j])
        x = b.X[j]
        b.pkb[mine, (j - 1) * cap : j * cap] = picked_by(x, b.pick[j - 1], 0)
        for d in (2, 1, 3):
            pk(j, d).start()
            later(functools.partial(pk, j, d))

    def xo(d):
        to = lax.rem(q + d, NSEP)
        return rcopy(b.xp.at[ds(to, cols), :], b.xob.at[q], b.xS.at[d], b.xR.at[d], at_sep(d))

    b.xp[...] = jnp.zeros_like(b.xp)

    @when(owner)
    def _():
        b.xp[:, :cols] = b.X[lam].T

    b.xob[q] = b.xp[mine, :]
    for d in range(1, NSEP):
        xo(d).start()
        later(functools.partial(xo, d))

    for j in range(depth, 0, -1):
        for d in range(1, NSEP):
            pk(j, d).wait_recv()
    ph, pw = split(b.pkb[...])
    uh = b.updh[...]
    wT = b.yT[...] - (mm(ph, uh, 1, 1) + (mm(pw, uh, 1, 1) + mm(ph, b.updl[...], 1, 1)))
    b.XB[...] = mm3(b.inv[...], wT.T, 0, 0)

    def fin(d):
        to = q - d
        return rcopy(b.XB.at[ds(to, rows), :], b.fb.at[d], b.fS.at[d], b.fR.at[d], (l, to))

    for d in (2, 1, 3):

        @pl.when(q - d >= 0)
        def _():
            fin(d).start()

        later(functools.partial(fin, d), q - d >= 0)

    for d in range(1, NSEP):
        xo(d).wait_recv()
    b.sol[...] = jnp.concatenate([b.xob[i][:, :cols] for i in range(NSEP)], axis=1)
    b.out[...] = b.XB[own, :]
    for d in range(1, NSEP):

        @pl.when(q + d < NSEP)
        def _():
            rcopy(b.XB.at[own, :], b.fb.at[d], b.fS.at[d], b.fR.at[d], at_sep(d)).wait_recv()
            b.out[...] += b.fb[d]

    for copy, conditions in drains:
        if conditions:

            @when(*conditions)
            def _():
                copy().wait_send()

        else:
            copy().wait_send()


def per_device(ny, nz, src, inv, upd, lists, counts, ssrc, sinv, cpl):
    depth = counts.shape[1]
    rows, n = src.shape[1:]
    order = inv.shape[2]
    urows = upd.shape[1]
    cols = ssrc.shape[1]
    w = sinv.shape[1]
    cap = urows // depth
    s = depth + 1
    kp = depth - nz.bit_length() + 1
    rb = cols // ny
    mb = w // ny
    f = lambda *shape: pltpu.VMEM(shape, F32)
    h = lambda *shape: pltpu.VMEM(shape, BF16)
    dma = lambda *shape: pltpu.SemaphoreType.DMA(shape)
    vm = pl.BlockSpec(memory_space=pltpu.VMEM)
    hbm = pl.BlockSpec(memory_space=pl.ANY)
    scratch = dict(
        ssrc=f(cols, n),
        sinv=f(w, w),
        cpl=f(w, w),
        inv=f(rows, order),
        upd=f(rows, urows),
        ldS=dma(6),
        S=f(order, n),
        sp=f(n, 128),
        ssb=f(NSEP, cols, 128),
        sT=f(cols, w),
        Mo=f(w, w),
        No=f(w, w),
        MB=f(s, w, w),
        NB=f(s, w, w),
        PM=f(s, mb, w),
        PN=f(s, mb, w),
        Mh=h(s, w, w),
        Ml=h(s, w, w),
        Th=h(s, w, w),
        Tl=h(s, w, w),
        Nh=h(s, w, w),
        Nl=h(s, w, w),
        pick=h(depth, w, cap),
        yT=f(n, rows),
        updh=h(rows, urows),
        updl=h(rows, urows),
        TT=f(depth, n, cap),
        rsb=f(depth, NSEP, cols, cap),
        RP=f(s, cols, w),
        R1=f(cols, w),
        CX=f(s, cols, w),
        H=f(s, cols, w),
        HR=f(ny, s, rb, w),
        B=f(ny, kp - 2, rb, w),
        RZ=f(s, rb, w),
        ZT=f(depth - kp, rb, w),
        ZR=f(nz, depth - kp, rb, w),
        BZ=f(depth - kp + 1, rb, w),
        RF=f(kp, cols, w),
        V=f(kp, cols, w),
        X=f(s, cols, w),
        pkb=f(n, urows),
        XB=f(order, n),
        fb=f(NSEP, rows, n),
        xp=f(n, 128),
        xob=f(NSEP, cols, 128),
        agS=dma(NSEP),
        agR=dma(NSEP),
        ssS=dma(NSEP),
        ssR=dma(NSEP),
        moS=dma(2, 8),
        mlR=dma(2, s),
        scS=dma(2, ny),
        scR=dma(2, s),
        zmS=dma(2, nz),
        zmR=dma(2, s),
        ygS=dma(2, ny),
        ygR=dma(2, ny),
        fwS=dma(2),
        fwR=dma(2),
        rsS=dma(depth, NSEP),
        rsR=dma(depth, NSEP),
        cxS=dma(4),
        cxR=dma(4),
        hrS=dma(3, ny),
        hrR=dma(3, ny),
        brS=dma(ny),
        brR=dma(ny),
        bzS=dma(ny),
        bzR=dma(ny),
        zrS=dma(nz),
        zrR=dma(nz),
        bkS=dma(2),
        bkR=dma(2),
        pkS=dma(s, NSEP),
        pkR=dma(s, NSEP),
        xS=dma(NSEP),
        xR=dma(NSEP),
        fS=dma(NSEP),
        fR=dma(NSEP),
    )
    operands = ["counts", "xsrc", "xinv", "xupd", "lists", "xssrc", "xsinv", "xcpl", "out", "sol"]
    out, sol = pl.pallas_call(
        functools.partial(kernel, (ny, nz, depth), operands + list(scratch)),
        out_shape=(
            jax.ShapeDtypeStruct((rows, n), F32),
            jax.ShapeDtypeStruct((cols, n), F32),
        ),
        in_specs=[pl.BlockSpec(memory_space=pltpu.SMEM)] + [hbm] * 3 + [vm] + [hbm] * 3,
        out_specs=(vm, vm),
        scratch_shapes=list(scratch.values()),
        compiler_params=pltpu.CompilerParams(
            collective_id=0, has_side_effects=True, vmem_limit_bytes=62 * 2**20
        ),
    )(counts, src[0], inv[0], upd[0].T, lists, ssrc[0], sinv[0], cpl[0])
    return out[None], sol[None]


def solution(mesh):
    leaves = mesh.shape["leaf"]
    ny = nz = 8
    if leaves != 2 * ny * nz:
        ny, nz = (leaves // 4, 2)
    placed = (
        P("leaf", "sep", None),
        P("leaf", "sep", None),
        P("leaf", None, "sep"),
        P("leaf", None),
        P("leaf", None),
        P("leaf", "sep", None),
        P("leaf", None, None),
        P("leaf", None, None),
    )
    return jax.shard_map(
        functools.partial(per_device, ny, nz),
        mesh=mesh,
        in_specs=placed,
        out_specs=(P("leaf", "sep", None), P("leaf", "sep", None)),
        check_vma=False,
    )
```

```python
import functools
import types

import jax
import jax.numpy as jnp
from jax import lax
from jax.experimental import pallas as pl
from jax.experimental.pallas import tpu as pltpu
from jax.sharding import PartitionSpec as P

MESH = pl.DeviceIdType.MESH
F32 = jnp.float32
BF16 = jnp.bfloat16
NSEP = 4


def split(x):
    high = x.astype(BF16)
    return high, (x - high.astype(F32)).astype(BF16)


def mm(a, b, ca=1, cb=0):
    return lax.dot_general(a, b, (((ca,), (cb,)), ((), ())), preferred_element_type=F32)


def mm3(a, b, ca=1, cb=0):
    ah, al = split(a)
    bh, bl = split(b)
    return mm(ah, bh, ca, cb) + (mm(al, bh, ca, cb) + mm(ah, bl, ca, cb))


def chain(rows, wh, wl):
    high, low = split(rows)
    m = rows.shape[0]
    both = mm(jnp.concatenate([high, low], axis=0), wh)
    return both[:m] + (both[m:] + mm(high, wl))


def picked_by(rows, picker, cb):
    high, low = split(rows)
    m = rows.shape[0]
    both = mm(jnp.concatenate([high, low], axis=0), picker, 1, cb)
    return both[:m] + both[m:]


def level_of(index, depth):
    level = jnp.int32(1)
    for k in range(1, depth + 1):
        level = level + (lax.rem(index, 2**k) == 0).astype(jnp.int32)
    return level


def kernel(dims, names, *refs):
    ny, nz, depth = dims
    b = types.SimpleNamespace(**dict(zip(names, refs)))
    kp = depth - nz.bit_length() + 1
    l = lax.axis_index("leaf")
    q = lax.axis_index("sep")
    c = lax.rem(l, 2)
    y = lax.rem(lax.div(l, 2), ny)
    z = lax.div(l, 2 * ny)
    pair = l + 1 - 2 * c
    rows = b.xsrc.shape[0]
    cols = b.xssrc.shape[0]
    w = b.xsinv.shape[0]
    cap = b.lists.shape[1] // depth
    rb = cols // ny
    rh = 2 * rb
    mb = w // ny
    lam = level_of(l, depth)
    plane = level_of(z * 2 * ny, depth)
    core0 = c == 0
    core1 = c == 1
    owner = l > 0
    even_y = lax.rem(y, 2) == 0
    solver = jnp.logical_and(core0, even_y)

    def when(*conditions):
        return pl.when(functools.reduce(jnp.logical_and, conditions))

    def at_sep(d):
        return (l, lax.rem(q + d, NSEP))

    def y_of(d):
        return lax.rem(y + d, ny)

    def z_of(d):
        return lax.rem(z + d, nz)

    def even_at(d):
        return lax.rem(y + d, 2) == 0

    def at_y(d):
        return (l - 2 * y + 2 * y_of(d), q)

    def at_z(d):
        return (l + 2 * ny * (z_of(d) - z), q)

    at_pair = (pair, q)

    def rcopy(a, dst, ss, rs, device):
        return pltpu.make_async_remote_copy(
            src_ref=a, dst_ref=dst, send_sem=ss, recv_sem=rs, device_id=device, device_id_type=MESH
        )

    drains = []

    def later(copy, *conditions):
        drains.append((copy, conditions))

    def ds(index, size):
        return pl.ds(pl.multiple_of(index * size, 8), size)

    own = ds(q, rows)
    mine = ds(q, cols)
    loads = {}
    for i, (name, dst) in enumerate(
        (
            ("src", b.S.at[own, :]),
            ("ssrc", b.ssrc),
            ("sinv", b.sinv),
            ("cpl", b.cpl),
            ("inv", b.inv),
            ("upd", b.upd),
        )
    ):
        loads[name] = pltpu.make_async_copy(getattr(b, "x" + name), dst, b.ldS.at[i])
        loads[name].start()

    barrier = pltpu.get_barrier_semaphore()
    greeted = [at_sep(d) for d in range(1, NSEP)] + [at_pair]
    greeted += [at_y(d) for d in range(1, ny)] + [at_z(d) for d in range(1, nz)]
    for device in greeted:
        pl.semaphore_signal(barrier, inc=1, device_id=device, device_id_type=MESH)

    for j in range(1, NSEP):

        @pl.when(j > q)
        def _():
            b.S[j * rows : (j + 1) * rows, :] = jnp.zeros((rows, b.S.shape[1]), F32)

    b.sp[...] = jnp.zeros_like(b.sp)
    loads["src"].wait()
    pl.semaphore_wait(barrier, len(greeted))

    def ag(d):
        return rcopy(b.S.at[own, :], b.S.at[own, :], b.agS.at[d], b.agR.at[d], at_sep(d))

    for d in (2, 1, 3):

        @pl.when(q + d < NSEP)
        def _():
            ag(d).start()

        later(functools.partial(ag, d), q + d < NSEP)

    def ssx(d):
        to = lax.rem(q + d, NSEP)
        return rcopy(b.sp.at[ds(to, cols), :], b.ssb.at[q], b.ssS.at[d], b.ssR.at[d], at_sep(d))

    loads["ssrc"].wait()
    b.sp[:, :cols] = b.ssrc[...].T
    b.ssb[q] = b.sp[mine, :]
    for d in range(1, NSEP):
        ssx(d).start()
        later(functools.partial(ssx, d))

    loads["sinv"].wait()
    loads["cpl"].wait()
    sinv = b.sinv[...]
    b.Mo[...] = mm3(b.cpl[...], sinv)
    b.No[...] = mm3(sinv, sinv, 0, 0)

    def low_of(k, device, slot, m):
        src, dst = ((b.Mo, b.MB), (b.No, b.NB))[m]
        return rcopy(src, dst.at[k], b.moS.at[m, slot], b.mlR.at[m, k], device)

    def start_both(k, device, slot, *conditions):
        @when(*conditions)
        def _():
            for m in range(2):
                low_of(k, device, slot, m).start()

        for m in range(2):
            later(functools.partial(low_of, k, device, slot, m), *conditions)

    start_both(1, at_pair, 0, core1)
    for k in range(2, kp):
        reach = 2 ** (k - 2)
        slot = 0
        for o in range(-reach, reach):
            if o:
                start_both(k, (l + 2 * o, q), slot, core0, lam == k)
                slot += 1

    for k in range(1, kp):

        @when(lam == k)
        def _():
            b.MB[k] = b.Mo[...]
            b.NB[k] = b.No[...]

    def sc(m, d):
        src, dst = ((b.Mo, b.PM), (b.No, b.PN))[m]
        return rcopy(
            src.at[ds(y_of(d), mb), :], dst.at[lam], b.scS.at[m, d], b.scR.at[m, lam], at_y(d)
        )

    def wait_sc(m, k):
        dst = (b.PM, b.PN)[m]
        rcopy(dst.at[k], dst.at[k], b.scS.at[m, 0], b.scR.at[m, k], at_pair).wait_recv()

    high = jnp.logical_and(core0, jnp.logical_and(lam >= kp, owner))
    for m in range(2):
        has = (high, lam < depth) if m == 0 else (high,)

        @when(*has)
        def _():
            for d in range(1, ny):
                sc(m, d).start()
            dst, src = ((b.PM, b.Mo), (b.PN, b.No))[m]
            dst[lam] = src[ds(y, mb), :]

        for d in range(1, ny):
            later(functools.partial(sc, m, d), *has)

    wi = lax.broadcasted_iota(jnp.int32, (w, cap), 0)
    pi = lax.broadcasted_iota(jnp.int32, (w, cap), 1)
    for j in range(depth):
        hit = jnp.logical_and(wi == b.lists[0:1, j * cap : (j + 1) * cap], pi < b.counts[0, j])
        b.pick[j] = jnp.where(hit, 1.0, 0.0).astype(BF16)
    loads["upd"].wait()
    uh, ul = split(b.upd[...])
    b.updh[...] = uh
    b.updl[...] = ul

    def zm(m, d):
        dst = (b.PM, b.PN)[m]
        return rcopy(dst.at[plane], dst.at[plane], b.zmS.at[m, d], b.zmR.at[m, plane], at_z(d))

    def wait_zm(m, k):
        dst = (b.PM, b.PN)[m]
        rcopy(dst.at[k], dst.at[k], b.zmS.at[m, 0], b.zmR.at[m, k], at_pair).wait_recv()

    size = jnp.int32(1)
    for k in range(kp + 1, depth + 1):
        size = size + (plane >= k).astype(jnp.int32) * 2 ** (k - kp - 1)
    base = z - lax.div(size, 2)

    def in_node(d):
        zd = z_of(d)
        return jnp.logical_and(zd >= base, zd < base + size)

    for m in range(2):
        top = depth - 1 if m == 0 else depth

        @when(core0, y != ny // 2)
        def _():
            wait_sc(m, kp)

        @when(core0, y != 0, plane <= top)
        def _():
            wait_sc(m, plane)

        for d in range(1, nz):
            sends = (core0, plane <= top, in_node(d))

            @when(*sends)
            def _():
                zm(m, d).start()

            later(functools.partial(zm, m, d), *sends)

    def wait_low(k):
        for m, dst in enumerate((b.MB, b.NB)):
            rcopy(dst.at[k], dst.at[k], b.moS.at[m, 0], b.mlR.at[m, k], at_pair).wait_recv()

    def fw(m):
        place = (b.MB, b.NB)[m].at[2:kp]
        return rcopy(place, place, b.fwS.at[m], b.fwR.at[m], at_pair)

    for k in range(2, kp):

        @when(core0, lam != k)
        def _():
            wait_low(k)

    if kp > 2:

        @when(core0)
        def _():
            for m in range(2):
                fw(m).start()

        for m in range(2):
            later(functools.partial(fw, m), core0)

    for d in range(1, NSEP):

        @pl.when(q - d >= 0)
        def _():
            ag(d).wait_recv()

    loads["inv"].wait()
    b.yT[...] = mm3(b.inv[...], b.S[...]).T

    def rs(j, d):
        to = lax.rem(q + d, NSEP)
        return rcopy(
            b.TT.at[j, ds(to, cols), :], b.rsb.at[j, d], b.rsS.at[j, d], b.rsR.at[j, d], at_sep(d)
        )

    yh, yl = split(b.yT[...])
    for j in range(depth):
        bh = b.updh[:, j * cap : (j + 1) * cap]
        bl = b.updl[:, j * cap : (j + 1) * cap]
        b.TT[j] = mm(yh, bh) + (mm(yl, bh) + mm(yh, bl))
        for d in (2, 1, 3):
            rs(j, d).start()
            later(functools.partial(rs, j, d))

    def yg(m, d):
        dst, src = ((b.MB, b.PM), (b.NB, b.PN))[m]
        hi = depth if m == 0 else depth + 1
        return rcopy(
            src.at[kp:hi], dst.at[kp:hi, ds(y, mb), :], b.ygS.at[m, d], b.ygR.at[m, d], at_y(d)
        )

    def gather_high(m):
        hi = depth if m == 0 else depth + 1

        @when(core0)
        def _():
            for k in range(kp + 1, hi):

                @pl.when(plane != k)
                def _():
                    wait_zm(m, k)

            for d in range(1, ny):

                @pl.when(even_at(d))
                def _():
                    yg(m, d).start()

        for d in range(1, ny):
            later(functools.partial(yg, m, d), core0, even_at(d))

        @when(solver)
        def _():
            dst, src = ((b.MB, b.PM), (b.NB, b.PN))[m]
            dst[kp:hi, ds(y, mb), :] = src[kp:hi]

    gather_high(0)
    for d in range(1, NSEP):
        ssx(d).wait_recv()
    sT = jnp.concatenate([b.ssb[i][:, :cols] for i in range(NSEP)], axis=1)
    b.sT[...] = sT

    def prepare(k):
        if k < depth:
            mh, ml = split(b.MB[k])
            b.Mh[k] = mh
            b.Ml[k] = ml
            th, tl = split(b.MB[k].T)
            b.Th[k] = th
            b.Tl[k] = tl

    def prepare_n(k):
        nh, nl = split(b.NB[k])
        b.Nh[k] = nh
        b.Nl[k] = nl

    @when(core0)
    def _():
        wait_low(1)

    if kp > 2:

        @when(core1)
        def _():
            for m in range(2):
                fw(m).wait_recv()

    for k in range(1, kp):
        prepare(k)


    def own_part(k):
        for d in range(1, NSEP):
            rs(k - 1, d).wait_recv()
        t = (b.TT[k - 1, mine, :] + b.rsb[k - 1, 1]) + (b.rsb[k - 1, 2] + b.rsb[k - 1, 3])
        part = jnp.where(lam == k, b.sT[...], 0.0) - picked_by(t, b.pick[k - 1], 1)
        if 1 < k <= kp:
            part = part - chain(b.RP[k - 1], b.Th[k - 1], b.Tl[k - 1])
        b.RP[k] = part

    groups = ((2, kp), (kp, depth), (depth, depth + 1))
    sums_on = (core1, core0, core0)
    sends_to_pair = (core0, core1, core1)

    def r1():
        return rcopy(b.RP.at[1], b.R1, b.cxS.at[3], b.cxR.at[3], at_pair)

    def cx(i):
        lo, hi = groups[i]
        return rcopy(b.RP.at[lo:hi], b.CX.at[lo:hi], b.cxS.at[i], b.cxR.at[i], at_pair)

    def hr(i, d):
        lo, hi = groups[i]
        if i == 0:
            src, dst = b.H.at[lo:hi, ds(y_of(d), rb), :], b.HR.at[y]
        else:
            src = b.H.at[lo:hi, ds(lax.div(y_of(d), 2), rh), :]
            dst = b.HH.at[y, lo - kp : hi - kp]
        return rcopy(src, dst, b.hrS.at[i, d], b.hrR.at[i, d], at_y(d))

    def share(i):
        lo, hi = groups[i]

        @when(sends_to_pair[i])
        def _():
            cx(i).start()

        later(functools.partial(cx, i), sends_to_pair[i])

        @when(sums_on[i])
        def _():
            cx(i).wait_recv()
            b.H[lo:hi] = b.RP[lo:hi] + b.CX[lo:hi]
            for d in range(1, ny):
                if i == 0:
                    hr(i, d).start()
                else:

                    @pl.when(even_at(d))
                    def _():
                        hr(i, d).start()

            if i == 0:
                b.HR[y] = b.H[lo:hi, ds(y, rb), :]

        if i:

            @when(solver)
            def _():
                b.HH[y, lo - kp : hi - kp] = b.H[lo:hi, ds(lax.div(y, 2), rh), :]

        for d in range(1, ny):
            later(functools.partial(hr, i, d), sums_on[i], *((even_at(d),) if i else ()))

    own_part(1)
    r1().start()
    later(r1)
    for k in range(2, kp):
        own_part(k)
    share(0)
    for k in range(kp, depth):
        own_part(k)
    share(1)
    own_part(depth)
    share(2)
    gather_high(1)

    def br(d):
        place = b.RF.at[2:kp, ds(y, rb), :]
        return rcopy(b.B.at[y_of(d)], place, b.brS.at[d], b.brR.at[d], at_y(d))

    def z_xor(i):
        other = z
        for bit in range(nz.bit_length() - 1):
            if i >> bit & 1:
                other = other + 2**bit - 2 ** (bit + 1) * lax.rem(lax.div(z, 2**bit), 2)
        return other

    def zr(k, i):
        device = (l + 2 * ny * (z_xor(i) - z), q)
        at = k - kp - 1
        return rcopy(b.ZT.at[at], b.ZR.at[at, z], b.zrS.at[at, i], b.zrR.at[at, i], device)

    def bz(k, d):
        place = b.X.at[k, ds(lax.div(y, 2), rh), :]
        return rcopy(b.BZ.at[k - kp], place, b.bzS.at[k - kp, d], b.bzR.at[k - kp, d], at_y(d))

    def back_low():
        place = b.RF.at[2:kp]
        return rcopy(place, place, b.bkS.at[0], b.bkR.at[0], at_pair)

    def back_high(k):
        place = b.X.at[k]
        return rcopy(place, place, b.bkS.at[k], b.bkR.at[k], at_pair)

    @when(core1)
    def _():
        for d in range(1, ny):
            hr(0, d).wait_recv()
        for k in range(2, kp):
            step = 2 ** (k - 1)
            for g in range(0, ny, step):
                total = b.HR[g, k - 2]
                for i in range(1, step):
                    total = total + b.HR[g + i, k - 2]
                for i in range(step):
                    b.B[g + i, k - 2] = total
        for d in range(1, ny):
            br(d).start()
        b.RF[2:kp, ds(y, rb), :] = b.B[y]
        for d in range(1, ny):
            br(d).wait_recv()
        back_low().start()

    for d in range(1, ny):
        later(functools.partial(br, d), core1)
    later(back_low, core1)

    @when(solver)
    def _():
        for d in range(1, ny):
            yg(0, d).wait_recv()
        for k in range(kp, depth):
            prepare(k)
        for k in range(kp, depth + 1):
            if k == kp or k == depth:
                for d in range(1, ny):
                    hr(1 if k == kp else 2, d).wait_recv()
            total = b.HH[0, k - kp]
            for i in range(1, ny):
                total = total + b.HH[i, k - kp]
            if k > kp:
                total = total - chain(b.RZ[k - 1], b.Th[k - 1], b.Tl[k - 1])
                b.ZT[k - kp - 1] = total
                for i in range(1, 2 ** (k - kp)):
                    zr(k, i).start()
                b.ZR[k - kp - 1, z] = total
            b.RZ[k] = total

    for k in range(kp + 1, depth + 1):
        for i in range(1, 2 ** (k - kp)):
            later(functools.partial(zr, k, i), solver)

    for k in range(1, kp):
        prepare_n(k)
    r1().wait_recv()
    b.RF[1] = b.RP[1] + b.R1[...]

    @when(core0)
    def _():
        back_low().wait_recv()

    for k in range(1, kp):
        b.V[k] = chain(b.RF[k], b.Nh[k], b.Nl[k])

    @when(solver)
    def _():
        for d in range(1, ny):
            yg(1, d).wait_recv()
        for k in range(kp, depth + 1):
            prepare_n(k)
        for k in range(kp, depth + 1):
            total = b.RZ[k]
            if k > kp:
                step = 2 ** (k - kp)
                for i in range(1, step):
                    zr(k, i).wait_recv()
                first = z - lax.rem(z, step)
                total = b.ZR[k - kp - 1, first]
                for i in range(1, step):
                    total = total + b.ZR[k - kp - 1, first + i]
            b.BZ[k - kp] = chain(total, b.Nh[k], b.Nl[k])
        for k in range(depth, kp - 1, -1):
            if k < depth:
                b.BZ[k - kp] = b.BZ[k - kp] - chain(b.BZ[k + 1 - kp], b.Mh[k], b.Ml[k])
            for d in range(1, ny):
                bz(k, d).start()
            b.X[k, ds(lax.div(y, 2), rh), :] = b.BZ[k - kp]

    def arrive(k):
        @when(core0)
        def _():
            for d in range(1, ny):

                @pl.when(even_at(d))
                def _():
                    bz(k, d).wait_recv()

            back_high(k).start()

        @when(core1)
        def _():
            back_high(k).wait_recv()

    for k in range(kp, depth + 1):
        for d in range(1, ny):
            later(functools.partial(bz, k, d), solver)
        later(functools.partial(back_high, k), core0)

    def pk(j, d):
        place = b.pkb.at[mine, (j - 1) * cap : j * cap]
        return rcopy(place, place, b.pkS.at[j, d], b.pkR.at[j, d], at_sep(d))

    def send_picked(j):
        b.pkb[mine, (j - 1) * cap : j * cap] = picked_by(b.X[j], b.pick[j - 1], 0)
        for d in (2, 1, 3):
            pk(j, d).start()
            later(functools.partial(pk, j, d))

    for j in range(depth, 0, -1):
        if j >= kp:
            arrive(j)
        if j <= kp and j > 1:
            b.X[j - 1] = b.V[j - 1] - chain(b.X[j], b.Mh[j - 1], b.Ml[j - 1])
        send_picked(j)

    def xo(d):
        to = lax.rem(q + d, NSEP)
        return rcopy(b.xp.at[ds(to, cols), :], b.xob.at[q], b.xS.at[d], b.xR.at[d], at_sep(d))

    b.xp[...] = jnp.zeros_like(b.xp)

    @when(owner)
    def _():
        b.xp[:, :cols] = b.X[lam].T

    b.xob[q] = b.xp[mine, :]
    for d in range(1, NSEP):
        xo(d).start()
        later(functools.partial(xo, d))

    for j in range(depth, 0, -1):
        for d in range(1, NSEP):
            pk(j, d).wait_recv()
    ph, pw = split(b.pkb[...])
    uh = b.updh[...]
    wT = b.yT[...] - (mm(ph, uh, 1, 1) + (mm(pw, uh, 1, 1) + mm(ph, b.updl[...], 1, 1)))
    b.XB[...] = mm3(b.inv[...], wT.T, 0, 0)

    def fin(d):
        to = q - d
        return rcopy(b.XB.at[ds(to, rows), :], b.fb.at[d], b.fS.at[d], b.fR.at[d], (l, to))

    for d in (2, 1, 3):

        @pl.when(q - d >= 0)
        def _():
            fin(d).start()

        later(functools.partial(fin, d), q - d >= 0)

    for d in range(1, NSEP):
        xo(d).wait_recv()
    b.sol[...] = jnp.concatenate([b.xob[i][:, :cols] for i in range(NSEP)], axis=1)
    b.out[...] = b.XB[own, :]
    for d in range(1, NSEP):

        @pl.when(q + d < NSEP)
        def _():
            rcopy(b.XB.at[own, :], b.fb.at[d], b.fS.at[d], b.fR.at[d], at_sep(d)).wait_recv()
            b.out[...] += b.fb[d]

    for copy, conditions in drains:
        if conditions:

            @when(*conditions)
            def _():
                copy().wait_send()

        else:
            copy().wait_send()


def per_device(ny, nz, src, inv, upd, lists, counts, ssrc, sinv, cpl):
    depth = counts.shape[1]
    rows, n = src.shape[1:]
    order = inv.shape[2]
    urows = upd.shape[1]
    cols = ssrc.shape[1]
    w = sinv.shape[1]
    cap = urows // depth
    s = depth + 1
    kp = depth - nz.bit_length() + 1
    rb = cols // ny
    mb = w // ny
    f = lambda *shape: pltpu.VMEM(shape, F32)
    h = lambda *shape: pltpu.VMEM(shape, BF16)
    dma = lambda *shape: pltpu.SemaphoreType.DMA(shape)
    vm = pl.BlockSpec(memory_space=pltpu.VMEM)
    hbm = pl.BlockSpec(memory_space=pl.ANY)
    scratch = dict(
        ssrc=f(cols, n),
        sinv=f(w, w),
        cpl=f(w, w),
        inv=f(rows, order),
        upd=f(rows, urows),
        ldS=dma(6),
        S=f(order, n),
        sp=f(n, 128),
        ssb=f(NSEP, cols, 128),
        sT=f(cols, w),
        Mo=f(w, w),
        No=f(w, w),
        MB=f(s, w, w),
        NB=f(s, w, w),
        PM=f(s, mb, w),
        PN=f(s, mb, w),
        Mh=h(s, w, w),
        Ml=h(s, w, w),
        Th=h(s, w, w),
        Tl=h(s, w, w),
        Nh=h(s, w, w),
        Nl=h(s, w, w),
        pick=h(depth, w, cap),
        yT=f(n, rows),
        updh=h(rows, urows),
        updl=h(rows, urows),
        TT=f(depth, n, cap),
        rsb=f(depth, NSEP, cols, cap),
        RP=f(s, cols, w),
        R1=f(cols, w),
        CX=f(s, cols, w),
        H=f(s, cols, w),
        HR=f(ny, kp - 2, rb, w),
        HH=f(ny, depth - kp + 1, 2 * rb, w),
        B=f(ny, kp - 2, rb, w),
        RZ=f(s, 2 * rb, w),
        ZT=f(depth - kp, 2 * rb, w),
        ZR=f(depth - kp, nz, 2 * rb, w),
        BZ=f(depth - kp + 1, 2 * rb, w),
        RF=f(kp, cols, w),
        V=f(kp, cols, w),
        X=f(s, cols, w),
        pkb=f(n, urows),
        XB=f(order, n),
        fb=f(NSEP, rows, n),
        xp=f(n, 128),
        xob=f(NSEP, cols, 128),
        agS=dma(NSEP),
        agR=dma(NSEP),
        ssS=dma(NSEP),
        ssR=dma(NSEP),
        moS=dma(2, 8),
        mlR=dma(2, s),
        scS=dma(2, ny),
        scR=dma(2, s),
        zmS=dma(2, nz),
        zmR=dma(2, s),
        ygS=dma(2, ny),
        ygR=dma(2, ny),
        fwS=dma(2),
        fwR=dma(2),
        rsS=dma(depth, NSEP),
        rsR=dma(depth, NSEP),
        cxS=dma(4),
        cxR=dma(4),
        hrS=dma(3, ny),
        hrR=dma(3, ny),
        brS=dma(ny),
        brR=dma(ny),
        bzS=dma(depth - kp + 1, ny),
        bzR=dma(depth - kp + 1, ny),
        zrS=dma(depth - kp, nz),
        zrR=dma(depth - kp, nz),
        bkS=dma(s),
        bkR=dma(s),
        pkS=dma(s, NSEP),
        pkR=dma(s, NSEP),
        xS=dma(NSEP),
        xR=dma(NSEP),
        fS=dma(NSEP),
        fR=dma(NSEP),
    )
    operands = ["counts", "xsrc", "xinv", "xupd", "lists", "xssrc", "xsinv", "xcpl", "out", "sol"]
    out, sol = pl.pallas_call(
        functools.partial(kernel, (ny, nz, depth), operands + list(scratch)),
        out_shape=(
            jax.ShapeDtypeStruct((rows, n), F32),
            jax.ShapeDtypeStruct((cols, n), F32),
        ),
        in_specs=[pl.BlockSpec(memory_space=pltpu.SMEM)] + [hbm] * 3 + [vm] + [hbm] * 3,
        out_specs=(vm, vm),
        scratch_shapes=list(scratch.values()),
        compiler_params=pltpu.CompilerParams(
            collective_id=0, has_side_effects=True, vmem_limit_bytes=62 * 2**20
        ),
    )(counts, src[0], inv[0], upd[0].T, lists, ssrc[0], sinv[0], cpl[0])
    return out[None], sol[None]


def solution(mesh):
    leaves = mesh.shape["leaf"]
    ny = nz = 8
    if leaves != 2 * ny * nz:
        ny, nz = (leaves // 4, 2)
    placed = (
        P("leaf", "sep", None),
        P("leaf", "sep", None),
        P("leaf", None, "sep"),
        P("leaf", None),
        P("leaf", None),
        P("leaf", "sep", None),
        P("leaf", None, None),
        P("leaf", None, None),
    )
    return jax.shard_map(
        functools.partial(per_device, ny, nz),
        mesh=mesh,
        in_specs=placed,
        out_specs=(P("leaf", "sep", None), P("leaf", "sep", None)),
        check_vma=False,
    )
```

```python
import functools
import types

import jax
import jax.numpy as jnp
from jax import lax
from jax.experimental import pallas as pl
from jax.experimental.pallas import tpu as pltpu
from jax.sharding import PartitionSpec as P

MESH = pl.DeviceIdType.MESH
F32 = jnp.float32
BF16 = jnp.bfloat16
NSEP = 4
HALVES = range(2)


def split(x):
    high = x.astype(BF16)
    return high, (x - high.astype(F32)).astype(BF16)


def mm(a, b, ca=1, cb=0):
    return lax.dot_general(a, b, (((ca,), (cb,)), ((), ())), preferred_element_type=F32)


def mm3(a, b, ca=1, cb=0):
    ah, al = split(a)
    bh, bl = split(b)
    return mm(ah, bh, ca, cb) + (mm(al, bh, ca, cb) + mm(ah, bl, ca, cb))


def chain(rows, wh, wl):
    high, low = split(rows)
    m = rows.shape[0]
    both = mm(jnp.concatenate([high, low], axis=0), wh)
    return both[:m] + (both[m:] + mm(high, wl))


def picked_by(rows, picker, cb):
    high, low = split(rows)
    m = rows.shape[0]
    both = mm(jnp.concatenate([high, low], axis=0), picker, 1, cb)
    return both[:m] + both[m:]


def level_of(index, depth):
    level = jnp.int32(1)
    for k in range(1, depth + 1):
        level = level + (lax.rem(index, 2**k) == 0).astype(jnp.int32)
    return level


def kernel(dims, names, *refs):
    ny, nz, depth = dims
    b = types.SimpleNamespace(**dict(zip(names, refs)))
    kp = depth - nz.bit_length() + 1
    l = lax.axis_index("leaf")
    q = lax.axis_index("sep")
    c = lax.rem(l, 2)
    y = lax.rem(lax.div(l, 2), ny)
    z = lax.div(l, 2 * ny)
    pair = l + 1 - 2 * c
    rows = b.xsrc.shape[0]
    cols = b.xssrc.shape[0]
    w = b.xsinv.shape[0]
    cap = b.lists.shape[1] // depth
    rb = cols // ny
    rh = 2 * rb
    mb = w // ny
    lam = level_of(l, depth)
    plane = level_of(z * 2 * ny, depth)
    core0 = c == 0
    core1 = c == 1
    owner = l > 0
    even_y = lax.rem(y, 2) == 0
    solver = jnp.logical_and(core0, even_y)

    def when(*conditions):
        return pl.when(functools.reduce(jnp.logical_and, conditions))

    def at_sep(d):
        return (l, lax.rem(q + d, NSEP))

    def y_of(d):
        return lax.rem(y + d, ny)

    def z_of(d):
        return lax.rem(z + d, nz)

    def even_at(d):
        return lax.rem(y + d, 2) == 0

    def at_y(d):
        return (l - 2 * y + 2 * y_of(d), q)

    def at_z(d):
        return (l + 2 * ny * (z_of(d) - z), q)

    at_pair = (pair, q)

    def rcopy(a, dst, ss, rs, device):
        return pltpu.make_async_remote_copy(
            src_ref=a, dst_ref=dst, send_sem=ss, recv_sem=rs, device_id=device, device_id_type=MESH
        )

    drains = []

    def later(copy, *conditions):
        drains.append((copy, conditions))

    def ds(index, size):
        return pl.ds(pl.multiple_of(index * size, 8), size)

    own = ds(q, rows)
    mine = ds(q, cols)
    n = b.S.shape[1]
    nh = n // 2
    ch = cols // 2

    def lanes(h):
        return pl.ds(h * nh, nh)

    def part(h):
        return pl.ds(h * ch, ch)

    def chunk(h, index):
        return pl.ds(pl.multiple_of(h * nh + index * ch, 8), ch)

    def in_half(index, h):
        return lax.div(index, ny // 2) == h

    loads = {}
    for i, (name, dst) in enumerate(
        (
            ("src", b.S.at[own, :]),
            ("ssrc", b.ssrc),
            ("sinv", b.sinv),
            ("cpl", b.cpl),
            ("inv", b.inv),
            ("upd", b.upd),
        )
    ):
        loads[name] = pltpu.make_async_copy(getattr(b, "x" + name), dst, b.ldS.at[i])
        loads[name].start()

    barrier = pltpu.get_barrier_semaphore()
    greeted = [at_sep(d) for d in range(1, NSEP)] + [at_pair]
    greeted += [at_y(d) for d in range(1, ny)] + [at_z(d) for d in range(1, nz)]
    for device in greeted:
        pl.semaphore_signal(barrier, inc=1, device_id=device, device_id_type=MESH)

    for j in range(1, NSEP):

        @pl.when(j > q)
        def _():
            b.S[j * rows : (j + 1) * rows, :] = jnp.zeros((rows, b.S.shape[1]), F32)

    b.sp[...] = jnp.zeros_like(b.sp)
    loads["src"].wait()
    pl.semaphore_wait(barrier, len(greeted))

    def ag(h, d):
        place = b.S.at[own, lanes(h)]
        return rcopy(place, place, b.agS.at[h, d], b.agR.at[h, d], at_sep(d))

    for h in HALVES:
        for d in (2, 1, 3):

            @pl.when(q + d < NSEP)
            def _():
                ag(h, d).start()

            later(functools.partial(ag, h, d), q + d < NSEP)

    def ssx(d):
        to = lax.rem(q + d, NSEP)
        return rcopy(b.sp.at[ds(to, cols), :], b.ssb.at[q], b.ssS.at[d], b.ssR.at[d], at_sep(d))

    loads["ssrc"].wait()
    turned = b.ssrc[...].T
    for i in range(NSEP):
        for h in HALVES:
            block = turned[h * nh + i * ch : h * nh + (i + 1) * ch]
            b.sp[i * cols + h * ch : i * cols + (h + 1) * ch, :cols] = block
    b.ssb[q] = b.sp[mine, :]
    for d in range(1, NSEP):
        ssx(d).start()
        later(functools.partial(ssx, d))

    loads["sinv"].wait()
    loads["cpl"].wait()
    sinv = b.sinv[...]
    b.Mo[...] = mm3(b.cpl[...], sinv)
    b.No[...] = mm3(sinv, sinv, 0, 0)

    def low_of(k, device, slot, m):
        src, dst = ((b.Mo, b.MB), (b.No, b.NB))[m]
        return rcopy(src, dst.at[k], b.moS.at[m, slot], b.mlR.at[m, k], device)

    def start_both(k, device, slot, *conditions):
        @when(*conditions)
        def _():
            for m in range(2):
                low_of(k, device, slot, m).start()

        for m in range(2):
            later(functools.partial(low_of, k, device, slot, m), *conditions)

    start_both(1, at_pair, 0, core1)
    for k in range(2, kp):
        reach = 2 ** (k - 2)
        slot = 0
        for o in range(-reach, reach):
            if o:
                start_both(k, (l + 2 * o, q), slot, core0, lam == k)
                slot += 1

    for k in range(1, kp):

        @when(lam == k)
        def _():
            b.MB[k] = b.Mo[...]
            b.NB[k] = b.No[...]

    def sc(m, d):
        src, dst = ((b.Mo, b.PM), (b.No, b.PN))[m]
        return rcopy(
            src.at[ds(y_of(d), mb), :], dst.at[lam], b.scS.at[m, d], b.scR.at[m, lam], at_y(d)
        )

    def wait_sc(m, k):
        dst = (b.PM, b.PN)[m]
        rcopy(dst.at[k], dst.at[k], b.scS.at[m, 0], b.scR.at[m, k], at_pair).wait_recv()

    high = jnp.logical_and(core0, jnp.logical_and(lam >= kp, owner))
    for m in range(2):
        has = (high, lam < depth) if m == 0 else (high,)

        @when(*has)
        def _():
            for d in range(1, ny):
                sc(m, d).start()
            dst, src = ((b.PM, b.Mo), (b.PN, b.No))[m]
            dst[lam] = src[ds(y, mb), :]

        for d in range(1, ny):
            later(functools.partial(sc, m, d), *has)

    wi = lax.broadcasted_iota(jnp.int32, (w, cap), 0)
    pi = lax.broadcasted_iota(jnp.int32, (w, cap), 1)
    for j in range(depth):
        hit = jnp.logical_and(wi == b.lists[0:1, j * cap : (j + 1) * cap], pi < b.counts[0, j])
        b.pick[j] = jnp.where(hit, 1.0, 0.0).astype(BF16)
    loads["upd"].wait()
    uh, ul = split(b.upd[...])
    b.updh[...] = uh
    b.updl[...] = ul

    def zm(m, d):
        dst = (b.PM, b.PN)[m]
        return rcopy(dst.at[plane], dst.at[plane], b.zmS.at[m, d], b.zmR.at[m, plane], at_z(d))

    def wait_zm(m, k):
        dst = (b.PM, b.PN)[m]
        rcopy(dst.at[k], dst.at[k], b.zmS.at[m, 0], b.zmR.at[m, k], at_pair).wait_recv()

    size = jnp.int32(1)
    for k in range(kp + 1, depth + 1):
        size = size + (plane >= k).astype(jnp.int32) * 2 ** (k - kp - 1)
    base = z - lax.div(size, 2)

    def in_node(d):
        zd = z_of(d)
        return jnp.logical_and(zd >= base, zd < base + size)

    for m in range(2):
        top = depth - 1 if m == 0 else depth

        @when(core0, y != ny // 2)
        def _():
            wait_sc(m, kp)

        @when(core0, y != 0, plane <= top)
        def _():
            wait_sc(m, plane)

        for d in range(1, nz):
            sends = (core0, plane <= top, in_node(d))

            @when(*sends)
            def _():
                zm(m, d).start()

            later(functools.partial(zm, m, d), *sends)

    def wait_low(k):
        for m, dst in enumerate((b.MB, b.NB)):
            rcopy(dst.at[k], dst.at[k], b.moS.at[m, 0], b.mlR.at[m, k], at_pair).wait_recv()

    def fw(m):
        place = (b.MB, b.NB)[m].at[2:kp]
        return rcopy(place, place, b.fwS.at[m], b.fwR.at[m], at_pair)

    for k in range(2, kp):

        @when(core0, lam != k)
        def _():
            wait_low(k)

    if kp > 2:

        @when(core0)
        def _():
            for m in range(2):
                fw(m).start()

        for m in range(2):
            later(functools.partial(fw, m), core0)

    def rs(h, j, d):
        to = lax.rem(q + d, NSEP)
        return rcopy(
            b.TT.at[j, chunk(h, to), :],
            b.rsb.at[j, d, part(h)],
            b.rsS.at[h, j, d],
            b.rsR.at[h, j, d],
            at_sep(d),
        )

    loads["inv"].wait()
    ih, il = split(b.inv[...])
    b.ih[...] = ih
    b.il[...] = il
    for h in HALVES:
        for d in range(1, NSEP):

            @pl.when(q - d >= 0)
            def _():
                ag(h, d).wait_recv()

        sh, sl = split(b.S[:, lanes(h)])
        ih = b.ih[...]
        yT = (mm(ih, sh) + (mm(b.il[...], sh) + mm(ih, sl))).T
        b.yT[lanes(h), :] = yT
        yh, yl = split(yT)
        for j in range(depth):
            bh = b.updh[:, j * cap : (j + 1) * cap]
            bl = b.updl[:, j * cap : (j + 1) * cap]
            b.TT[j, lanes(h), :] = mm(yh, bh) + (mm(yl, bh) + mm(yh, bl))
            for d in (2, 1, 3):
                rs(h, j, d).start()
                later(functools.partial(rs, h, j, d))

    def yg(m, d):
        dst, src = ((b.MB, b.PM), (b.NB, b.PN))[m]
        hi = depth if m == 0 else depth + 1
        return rcopy(
            src.at[kp:hi], dst.at[kp:hi, ds(y, mb), :], b.ygS.at[m, d], b.ygR.at[m, d], at_y(d)
        )

    def gather_high(m):
        hi = depth if m == 0 else depth + 1

        @when(core0)
        def _():
            for k in range(kp + 1, hi):

                @pl.when(plane != k)
                def _():
                    wait_zm(m, k)

            for d in range(1, ny):

                @pl.when(even_at(d))
                def _():
                    yg(m, d).start()

        for d in range(1, ny):
            later(functools.partial(yg, m, d), core0, even_at(d))

        @when(solver)
        def _():
            dst, src = ((b.MB, b.PM), (b.NB, b.PN))[m]
            dst[kp:hi, ds(y, mb), :] = src[kp:hi]

    gather_high(0)
    gather_high(1)
    for d in range(1, NSEP):
        ssx(d).wait_recv()
    sT = jnp.concatenate([b.ssb[i][:, :cols] for i in range(NSEP)], axis=1)
    b.sT[...] = sT

    def prepare(k):
        if k < depth:
            mh, ml = split(b.MB[k])
            b.Mh[k] = mh
            b.Ml[k] = ml
            th, tl = split(b.MB[k].T)
            b.Th[k] = th
            b.Tl[k] = tl

    def prepare_n(k):
        nh, nl = split(b.NB[k])
        b.Nh[k] = nh
        b.Nl[k] = nl

    @when(core0)
    def _():
        wait_low(1)

    if kp > 2:

        @when(core1)
        def _():
            for m in range(2):
                fw(m).wait_recv()

    for k in range(1, kp):
        prepare(k)


    def own_part(h, k):
        for d in range(1, NSEP):
            rs(h, k - 1, d).wait_recv()
        r = part(h)
        t = (b.TT[k - 1, chunk(h, q), :] + b.rsb[k - 1, 1, r]) + (
            b.rsb[k - 1, 2, r] + b.rsb[k - 1, 3, r]
        )
        mine_k = jnp.where(lam == k, b.sT[r, :], 0.0) - picked_by(t, b.pick[k - 1], 1)
        if 1 < k <= kp:
            mine_k = mine_k - chain(b.RP[k - 1, r], b.Th[k - 1], b.Tl[k - 1])
        b.RP[k, r] = mine_k

    groups = ((2, kp), (kp, depth), (depth, depth + 1))
    sums_on = (core1, core0, core0)
    sends_to_pair = (core0, core1, core1)

    def r1():
        return rcopy(b.RP.at[1], b.R1, b.cxS.at[0, 3], b.cxR.at[0, 3], at_pair)

    def cx(h, i):
        lo, hi = groups[i]
        return rcopy(
            b.RP.at[lo:hi, part(h)],
            b.CX.at[lo:hi, part(h)],
            b.cxS.at[h, i],
            b.cxR.at[h, i],
            at_pair,
        )

    def hr(i, d):
        lo, hi = groups[i]
        if i == 0:
            src, dst = b.H.at[lo:hi, ds(y_of(d), rb), :], b.HR.at[y]
        else:
            src = b.H.at[lo:hi, ds(lax.div(y_of(d), 2), rh), :]
            dst = b.HH.at[y, lo - kp : hi - kp]
        return rcopy(src, dst, b.hrS.at[i, d], b.hrR.at[i, d], at_y(d))

    def share(h, i):
        lo, hi = groups[i]

        @when(sends_to_pair[i])
        def _():
            cx(h, i).start()

        later(functools.partial(cx, h, i), sends_to_pair[i])

        @when(sums_on[i])
        def _():
            cx(h, i).wait_recv()
            r = part(h)
            b.H[lo:hi, r] = b.RP[lo:hi, r] + b.CX[lo:hi, r]
            for d in range(1, ny):
                goes = in_half(y_of(d), h)

                @pl.when(jnp.logical_and(goes, even_at(d)) if i else goes)
                def _():
                    hr(i, d).start()

        if i:

            @when(solver, in_half(y, h))
            def _():
                b.HH[y, lo - kp : hi - kp] = b.H[lo:hi, ds(lax.div(y, 2), rh), :]

        else:

            @when(core1, in_half(y, h))
            def _():
                b.HR[y] = b.H[lo:hi, ds(y, rb), :]

    for i in range(3):
        for d in range(1, ny):
            later(functools.partial(hr, i, d), sums_on[i], *((even_at(d),) if i else ()))

    for h in HALVES:
        for k in range(1, kp):
            own_part(h, k)
        if h == 1:
            r1().start()
            later(r1)
        share(h, 0)
        for k in range(kp, depth):
            own_part(h, k)
        share(h, 1)
        own_part(h, depth)
        share(h, 2)

    def br(d):
        place = b.RF.at[2:kp, ds(y, rb), :]
        return rcopy(b.B.at[y_of(d)], place, b.brS.at[d], b.brR.at[d], at_y(d))

    def z_xor(i):
        other = z
        for bit in range(nz.bit_length() - 1):
            if i >> bit & 1:
                other = other + 2**bit - 2 ** (bit + 1) * lax.rem(lax.div(z, 2**bit), 2)
        return other

    def zr(k, i):
        device = (l + 2 * ny * (z_xor(i) - z), q)
        at = k - kp - 1
        return rcopy(b.ZT.at[at], b.ZR.at[at, z], b.zrS.at[at, i], b.zrR.at[at, i], device)

    def bz(k, d):
        place = b.X.at[k, ds(lax.div(y, 2), rh), :]
        return rcopy(b.BZ.at[k - kp], place, b.bzS.at[k - kp, d], b.bzR.at[k - kp, d], at_y(d))

    def back_low():
        place = b.RF.at[2:kp]
        return rcopy(place, place, b.bkS.at[0], b.bkR.at[0], at_pair)

    def back_high(h, k):
        place = b.X.at[k, part(h)]
        return rcopy(place, place, b.bhS.at[h, k], b.bhR.at[h, k], at_pair)

    @when(core1)
    def _():
        for d in range(1, ny):
            hr(0, d).wait_recv()
        for k in range(2, kp):
            step = 2 ** (k - 1)
            for g in range(0, ny, step):
                total = b.HR[g, k - 2]
                for i in range(1, step):
                    total = total + b.HR[g + i, k - 2]
                for i in range(step):
                    b.B[g + i, k - 2] = total
        for d in range(1, ny):
            br(d).start()
        b.RF[2:kp, ds(y, rb), :] = b.B[y]
        for d in range(1, ny):
            br(d).wait_recv()
        back_low().start()

    for d in range(1, ny):
        later(functools.partial(br, d), core1)
    later(back_low, core1)

    @when(solver)
    def _():
        for d in range(1, ny):
            yg(0, d).wait_recv()
        for k in range(kp, depth):
            prepare(k)
        for k in range(kp, depth + 1):
            if k == kp or k == depth:
                for d in range(1, ny):
                    hr(1 if k == kp else 2, d).wait_recv()
            total = b.HH[0, k - kp]
            for i in range(1, ny):
                total = total + b.HH[i, k - kp]
            if k > kp:
                total = total - chain(b.RZ[k - 1], b.Th[k - 1], b.Tl[k - 1])
                b.ZT[k - kp - 1] = total
                for i in range(1, 2 ** (k - kp)):
                    zr(k, i).start()
                b.ZR[k - kp - 1, z] = total
            b.RZ[k] = total

    for k in range(kp + 1, depth + 1):
        for i in range(1, 2 ** (k - kp)):
            later(functools.partial(zr, k, i), solver)

    for k in range(1, kp):
        prepare_n(k)
    r1().wait_recv()
    b.RF[1] = b.RP[1] + b.R1[...]

    @when(core0)
    def _():
        back_low().wait_recv()

    for k in range(1, kp):
        b.V[k] = chain(b.RF[k], b.Nh[k], b.Nl[k])

    @when(solver)
    def _():
        for d in range(1, ny):
            yg(1, d).wait_recv()
        for k in range(kp, depth + 1):
            prepare_n(k)
        for k in range(kp, depth + 1):
            total = b.RZ[k]
            if k > kp:
                step = 2 ** (k - kp)
                for i in range(1, step):
                    zr(k, i).wait_recv()
                first = z - lax.rem(z, step)
                total = b.ZR[k - kp - 1, first]
                for i in range(1, step):
                    total = total + b.ZR[k - kp - 1, first + i]
            b.BZ[k - kp] = chain(total, b.Nh[k], b.Nl[k])
        for k in range(depth, kp - 1, -1):
            if k < depth:
                b.BZ[k - kp] = b.BZ[k - kp] - chain(b.BZ[k + 1 - kp], b.Mh[k], b.Ml[k])
            for d in range(1, ny):
                bz(k, d).start()
            b.X[k, ds(lax.div(y, 2), rh), :] = b.BZ[k - kp]

    def arrive(h, k):
        @when(core0)
        def _():
            for d in range(1, ny):

                @when(even_at(d), in_half(y_of(ny - d), h))
                def _():
                    bz(k, d).wait_recv()

            back_high(h, k).start()

        @when(core1)
        def _():
            back_high(h, k).wait_recv()

    for k in range(kp, depth + 1):
        for d in range(1, ny):
            later(functools.partial(bz, k, d), solver)
        for h in HALVES:
            later(functools.partial(back_high, h, k), core0)

    def pk(h, j, d):
        place = b.pkb.at[chunk(h, q), (j - 1) * cap : j * cap]
        return rcopy(place, place, b.pkS.at[h, j, d], b.pkR.at[h, j, d], at_sep(d))

    for h in HALVES:
        r = part(h)
        for j in range(depth, 0, -1):
            if j >= kp:
                arrive(h, j)
            if j <= kp and j > 1:
                b.X[j - 1, r] = b.V[j - 1, r] - chain(b.X[j, r], b.Mh[j - 1], b.Ml[j - 1])
            b.pkb[chunk(h, q), (j - 1) * cap : j * cap] = picked_by(b.X[j, r], b.pick[j - 1], 0)
            for d in (2, 1, 3):
                pk(h, j, d).start()
                later(functools.partial(pk, h, j, d))

    def xo(d):
        to = lax.rem(q + d, NSEP)
        return rcopy(b.xp.at[ds(to, cols), :], b.xob.at[q], b.xS.at[d], b.xR.at[d], at_sep(d))

    b.xp[...] = jnp.zeros_like(b.xp)

    @when(owner)
    def _():
        b.xp[:, :cols] = b.X[lam].T

    b.xob[q] = b.xp[mine, :]
    for d in range(1, NSEP):
        xo(d).start()
        later(functools.partial(xo, d))

    def fin(h, d):
        to = q - d
        return rcopy(
            b.XB.at[ds(to, rows), lanes(h)],
            b.fb.at[d, :, lanes(h)],
            b.fS.at[h, d],
            b.fR.at[h, d],
            (l, to),
        )

    def wait_fin(h, d):
        place = b.fb.at[d, :, lanes(h)]
        rcopy(place, place, b.fS.at[h, d], b.fR.at[h, d], at_sep(d)).wait_recv()

    for h in HALVES:
        for j in range(depth, 0, -1):
            for d in range(1, NSEP):
                pk(h, j, d).wait_recv()
        ph, pw = split(b.pkb[lanes(h), :])
        uh = b.updh[...]
        wT = b.yT[lanes(h), :] - (mm(ph, uh, 1, 1) + (mm(pw, uh, 1, 1) + mm(ph, b.updl[...], 1, 1)))
        wh, wl = split(wT.T)
        ih = b.ih[...]
        b.XB[:, lanes(h)] = mm(ih, wh, 0, 0) + (mm(b.il[...], wh, 0, 0) + mm(ih, wl, 0, 0))
        for d in (2, 1, 3):

            @pl.when(q - d >= 0)
            def _():
                fin(h, d).start()

            later(functools.partial(fin, h, d), q - d >= 0)

    for d in range(1, NSEP):
        xo(d).wait_recv()
    b.sol[...] = jnp.concatenate(
        [b.xob[i][:, h * ch : (h + 1) * ch] for h in HALVES for i in range(NSEP)], axis=1
    )
    for h in HALVES:
        b.out[:, lanes(h)] = b.XB[own, lanes(h)]
        for d in range(1, NSEP):

            @pl.when(q + d < NSEP)
            def _():
                wait_fin(h, d)
                b.out[:, lanes(h)] += b.fb[d, :, lanes(h)]

    for copy, conditions in drains:
        if conditions:

            @when(*conditions)
            def _():
                copy().wait_send()

        else:
            copy().wait_send()


def per_device(ny, nz, src, inv, upd, lists, counts, ssrc, sinv, cpl):
    depth = counts.shape[1]
    rows, n = src.shape[1:]
    order = inv.shape[2]
    urows = upd.shape[1]
    cols = ssrc.shape[1]
    w = sinv.shape[1]
    cap = urows // depth
    s = depth + 1
    kp = depth - nz.bit_length() + 1
    rb = cols // ny
    mb = w // ny
    f = lambda *shape: pltpu.VMEM(shape, F32)
    h = lambda *shape: pltpu.VMEM(shape, BF16)
    dma = lambda *shape: pltpu.SemaphoreType.DMA(shape)
    vm = pl.BlockSpec(memory_space=pltpu.VMEM)
    hbm = pl.BlockSpec(memory_space=pl.ANY)
    scratch = dict(
        ssrc=f(cols, n),
        sinv=f(w, w),
        cpl=f(w, w),
        inv=f(rows, order),
        upd=f(rows, urows),
        ldS=dma(6),
        S=f(order, n),
        sp=f(n, 128),
        ssb=f(NSEP, cols, 128),
        sT=f(cols, w),
        Mo=f(w, w),
        No=f(w, w),
        MB=f(s, w, w),
        NB=f(s, w, w),
        PM=f(s, mb, w),
        PN=f(s, mb, w),
        Mh=h(s, w, w),
        Ml=h(s, w, w),
        Th=h(s, w, w),
        Tl=h(s, w, w),
        Nh=h(s, w, w),
        Nl=h(s, w, w),
        pick=h(depth, w, cap),
        yT=f(n, rows),
        updh=h(rows, urows),
        updl=h(rows, urows),
        TT=f(depth, n, cap),
        rsb=f(depth, NSEP, cols, cap),
        RP=f(s, cols, w),
        R1=f(cols, w),
        CX=f(s, cols, w),
        H=f(s, cols, w),
        HR=f(ny, kp - 2, rb, w),
        HH=f(ny, depth - kp + 1, 2 * rb, w),
        B=f(ny, kp - 2, rb, w),
        RZ=f(s, 2 * rb, w),
        ZT=f(depth - kp, 2 * rb, w),
        ZR=f(depth - kp, nz, 2 * rb, w),
        BZ=f(depth - kp + 1, 2 * rb, w),
        RF=f(kp, cols, w),
        V=f(kp, cols, w),
        X=f(s, cols, w),
        pkb=f(n, urows),
        XB=f(order, n),
        fb=f(NSEP, rows, n),
        xp=f(n, 128),
        xob=f(NSEP, cols, 128),
        ih=h(rows, order),
        il=h(rows, order),
        agS=dma(2, NSEP),
        agR=dma(2, NSEP),
        ssS=dma(NSEP),
        ssR=dma(NSEP),
        moS=dma(2, 8),
        mlR=dma(2, s),
        scS=dma(2, ny),
        scR=dma(2, s),
        zmS=dma(2, nz),
        zmR=dma(2, s),
        ygS=dma(2, ny),
        ygR=dma(2, ny),
        fwS=dma(2),
        fwR=dma(2),
        rsS=dma(2, depth, NSEP),
        rsR=dma(2, depth, NSEP),
        cxS=dma(2, 4),
        cxR=dma(2, 4),
        hrS=dma(3, ny),
        hrR=dma(3, ny),
        brS=dma(ny),
        brR=dma(ny),
        bzS=dma(depth - kp + 1, ny),
        bzR=dma(depth - kp + 1, ny),
        zrS=dma(depth - kp, nz),
        zrR=dma(depth - kp, nz),
        bkS=dma(1),
        bkR=dma(1),
        bhS=dma(2, s),
        bhR=dma(2, s),
        pkS=dma(2, s, NSEP),
        pkR=dma(2, s, NSEP),
        xS=dma(NSEP),
        xR=dma(NSEP),
        fS=dma(2, NSEP),
        fR=dma(2, NSEP),
    )
    operands = ["counts", "xsrc", "xinv", "xupd", "lists", "xssrc", "xsinv", "xcpl", "out", "sol"]
    out, sol = pl.pallas_call(
        functools.partial(kernel, (ny, nz, depth), operands + list(scratch)),
        out_shape=(
            jax.ShapeDtypeStruct((rows, n), F32),
            jax.ShapeDtypeStruct((cols, n), F32),
        ),
        in_specs=[pl.BlockSpec(memory_space=pltpu.SMEM)] + [hbm] * 3 + [vm] + [hbm] * 3,
        out_specs=(vm, vm),
        scratch_shapes=list(scratch.values()),
        compiler_params=pltpu.CompilerParams(
            collective_id=0, has_side_effects=True, vmem_limit_bytes=62 * 2**20
        ),
    )(counts, src[0], inv[0], upd[0].T, lists, ssrc[0], sinv[0], cpl[0])
    return out[None], sol[None]


def solution(mesh):
    leaves = mesh.shape["leaf"]
    ny = nz = 8
    if leaves != 2 * ny * nz:
        ny, nz = (leaves // 4, 2)
    placed = (
        P("leaf", "sep", None),
        P("leaf", "sep", None),
        P("leaf", None, "sep"),
        P("leaf", None),
        P("leaf", None),
        P("leaf", "sep", None),
        P("leaf", None, None),
        P("leaf", None, None),
    )
    return jax.shard_map(
        functools.partial(per_device, ny, nz),
        mesh=mesh,
        in_specs=placed,
        out_specs=(P("leaf", "sep", None), P("leaf", "sep", None)),
        check_vma=False,
    )
```

```python
import functools
import types

import jax
import jax.numpy as jnp
from jax import lax
from jax.experimental import pallas as pl
from jax.experimental.pallas import tpu as pltpu
from jax.sharding import PartitionSpec as P

MESH = pl.DeviceIdType.MESH
F32 = jnp.float32
BF16 = jnp.bfloat16
NSEP = 4
HALVES = range(2)


def split(x):
    high = x.astype(BF16)
    return high, (x - high.astype(F32)).astype(BF16)


def mm(a, b, ca=1, cb=0):
    return lax.dot_general(a, b, (((ca,), (cb,)), ((), ())), preferred_element_type=F32)


def mm3(a, b, ca=1, cb=0):
    ah, al = split(a)
    bh, bl = split(b)
    return mm(ah, bh, ca, cb) + (mm(al, bh, ca, cb) + mm(ah, bl, ca, cb))


def chain(rows, wh, wl):
    high, low = split(rows)
    m = rows.shape[0]
    both = mm(jnp.concatenate([high, low], axis=0), wh)
    return both[:m] + (both[m:] + mm(high, wl))


def picked_by(rows, picker, cb):
    high, low = split(rows)
    m = rows.shape[0]
    both = mm(jnp.concatenate([high, low], axis=0), picker, 1, cb)
    return both[:m] + both[m:]


def level_of(index, depth):
    level = jnp.int32(1)
    for k in range(1, depth + 1):
        level = level + (lax.rem(index, 2**k) == 0).astype(jnp.int32)
    return level


def kernel(dims, names, *refs):
    ny, nz, depth = dims
    b = types.SimpleNamespace(**dict(zip(names, refs)))
    kp = depth - nz.bit_length() + 1
    l = lax.axis_index("leaf")
    q = lax.axis_index("sep")
    c = lax.rem(l, 2)
    y = lax.rem(lax.div(l, 2), ny)
    z = lax.div(l, 2 * ny)
    pair = l + 1 - 2 * c
    rows = b.xsrc.shape[0]
    cols = b.xssrc.shape[0]
    w = b.xsinv.shape[0]
    cap = b.lists.shape[1] // depth
    rb = cols // ny
    rh = 2 * rb
    mb = w // ny
    lam = level_of(l, depth)
    plane = level_of(z * 2 * ny, depth)
    core0 = c == 0
    core1 = c == 1
    owner = l > 0
    even_y = lax.rem(y, 2) == 0
    solver = jnp.logical_and(core0, even_y)

    def when(*conditions):
        return pl.when(functools.reduce(jnp.logical_and, conditions))

    def at_sep(d):
        return (l, lax.rem(q + d, NSEP))

    def y_of(d):
        return lax.rem(y + d, ny)

    def z_of(d):
        return lax.rem(z + d, nz)

    def even_at(d):
        return lax.rem(y + d, 2) == 0

    def at_y(d):
        return (l - 2 * y + 2 * y_of(d), q)

    def at_z(d):
        return (l + 2 * ny * (z_of(d) - z), q)

    at_pair = (pair, q)

    def rcopy(a, dst, ss, rs, device):
        return pltpu.make_async_remote_copy(
            src_ref=a, dst_ref=dst, send_sem=ss, recv_sem=rs, device_id=device, device_id_type=MESH
        )

    drains = []

    def later(copy, *conditions):
        drains.append((copy, conditions))

    def ds(index, size):
        return pl.ds(pl.multiple_of(index * size, 8), size)

    own = ds(q, rows)
    mine = ds(q, cols)
    n = b.S.shape[1]
    nh = n // 2
    ch = cols // 2

    def lanes(h):
        return pl.ds(h * nh, nh)

    def part(h):
        return pl.ds(h * ch, ch)

    def chunk(h, index):
        return pl.ds(pl.multiple_of(h * nh + index * ch, 8), ch)

    def in_half(index, h):
        return lax.div(index, ny // 2) == h

    loads = {}
    for i, (name, dst) in enumerate(
        (
            ("src", b.S.at[own, :]),
            ("ssrc", b.ssrc),
            ("sinv", b.sinv),
            ("cpl", b.cpl),
            ("inv", b.inv),
            ("upd", b.upd),
        )
    ):
        loads[name] = pltpu.make_async_copy(getattr(b, "x" + name), dst, b.ldS.at[i])
        loads[name].start()

    barrier = pltpu.get_barrier_semaphore()
    greeted = [at_sep(d) for d in range(1, NSEP)] + [at_pair]
    greeted += [at_y(d) for d in range(1, ny)] + [at_z(d) for d in range(1, nz)]
    for device in greeted:
        pl.semaphore_signal(barrier, inc=1, device_id=device, device_id_type=MESH)

    for j in range(1, NSEP):

        @pl.when(j > q)
        def _():
            b.S[j * rows : (j + 1) * rows, :] = jnp.zeros((rows, b.S.shape[1]), F32)

    b.sp[...] = jnp.zeros_like(b.sp)
    loads["src"].wait()
    pl.semaphore_wait(barrier, len(greeted))

    def ag(h, d):
        place = b.S.at[own, lanes(h)]
        return rcopy(place, place, b.agS.at[h, d], b.agR.at[h, d], at_sep(d))

    for h in HALVES:
        for d in (2, 1, 3):

            @pl.when(q + d < NSEP)
            def _():
                ag(h, d).start()

            later(functools.partial(ag, h, d), q + d < NSEP)

    def ssx(d):
        to = lax.rem(q + d, NSEP)
        return rcopy(b.sp.at[ds(to, cols), :], b.ssb.at[q], b.ssS.at[d], b.ssR.at[d], at_sep(d))

    loads["ssrc"].wait()
    turned = b.ssrc[...].T
    for i in range(NSEP):
        for h in HALVES:
            block = turned[h * nh + i * ch : h * nh + (i + 1) * ch]
            b.sp[i * cols + h * ch : i * cols + (h + 1) * ch, :cols] = block
    b.ssb[q] = b.sp[mine, :]
    for d in range(1, NSEP):
        ssx(d).start()
        later(functools.partial(ssx, d))

    loads["sinv"].wait()
    loads["cpl"].wait()
    def low_of(k, device, slot, m):
        src, dst = ((b.Mo, b.MB), (b.No, b.NB))[m]
        return rcopy(src, dst.at[k], b.moS.at[m, slot], b.mlR.at[m, k], device)

    def send_low(m):
        targets = [(1, at_pair, 0, (core1,))]
        for k in range(2, kp):
            reach = 2 ** (k - 2)
            offsets = [o for o in range(-reach, reach) if o]
            for slot, o in enumerate(offsets):
                targets.append((k, (l + 2 * o, q), slot, (core0, lam == k)))
        for k, device, slot, conditions in targets:

            @when(*conditions)
            def _():
                low_of(k, device, slot, m).start()

            later(functools.partial(low_of, k, device, slot, m), *conditions)
        for k in range(1, kp):

            @when(lam == k)
            def _():
                if m == 0:
                    b.MB[k] = b.Mo[...]
                else:
                    b.NB[k] = b.No[...]

    def sc(m, d):
        src, dst = ((b.Mo, b.PM), (b.No, b.PN))[m]
        return rcopy(
            src.at[ds(y_of(d), mb), :], dst.at[lam], b.scS.at[m, d], b.scR.at[m, lam], at_y(d)
        )

    def wait_sc(m, k):
        dst = (b.PM, b.PN)[m]
        rcopy(dst.at[k], dst.at[k], b.scS.at[m, 0], b.scR.at[m, k], at_pair).wait_recv()

    high = jnp.logical_and(core0, jnp.logical_and(lam >= kp, owner))

    def send_high(m):
        has = (high, lam < depth) if m == 0 else (high,)

        @when(*has)
        def _():
            for d in range(1, ny):
                sc(m, d).start()
            dst, src = ((b.PM, b.Mo), (b.PN, b.No))[m]
            dst[lam] = src[ds(y, mb), :]

        for d in range(1, ny):
            later(functools.partial(sc, m, d), *has)

    sinv = b.sinv[...]
    b.Mo[...] = mm3(b.cpl[...], sinv)
    send_high(0)
    send_low(0)
    b.No[...] = mm3(sinv, sinv, 0, 0)
    send_high(1)
    send_low(1)

    wi = lax.broadcasted_iota(jnp.int32, (w, cap), 0)
    pi = lax.broadcasted_iota(jnp.int32, (w, cap), 1)
    for j in range(depth):
        hit = jnp.logical_and(wi == b.lists[0:1, j * cap : (j + 1) * cap], pi < b.counts[0, j])
        b.pick[j] = jnp.where(hit, 1.0, 0.0).astype(BF16)
    loads["upd"].wait()
    uh, ul = split(b.upd[...])
    b.updh[...] = uh
    b.updl[...] = ul

    def zm(m, d):
        dst = (b.PM, b.PN)[m]
        return rcopy(dst.at[plane], dst.at[plane], b.zmS.at[m, d], b.zmR.at[m, plane], at_z(d))

    def wait_zm(m, k):
        dst = (b.PM, b.PN)[m]
        rcopy(dst.at[k], dst.at[k], b.zmS.at[m, 0], b.zmR.at[m, k], at_pair).wait_recv()

    size = jnp.int32(1)
    for k in range(kp + 1, depth + 1):
        size = size + (plane >= k).astype(jnp.int32) * 2 ** (k - kp - 1)
    base = z - lax.div(size, 2)

    def in_node(d):
        zd = z_of(d)
        return jnp.logical_and(zd >= base, zd < base + size)

    def along_z(m):
        top = depth - 1 if m == 0 else depth

        @when(core0, y != ny // 2)
        def _():
            wait_sc(m, kp)

        @when(core0, y != 0, plane <= top)
        def _():
            wait_sc(m, plane)

        for d in range(1, nz):
            sends = (core0, plane <= top, in_node(d))

            @when(*sends)
            def _():
                zm(m, d).start()

            later(functools.partial(zm, m, d), *sends)

    def wait_low(m, k):
        dst = (b.MB, b.NB)[m]
        rcopy(dst.at[k], dst.at[k], b.moS.at[m, 0], b.mlR.at[m, k], at_pair).wait_recv()

    def fw(m):
        place = (b.MB, b.NB)[m].at[2:kp]
        return rcopy(place, place, b.fwS.at[m], b.fwR.at[m], at_pair)

    def pass_low(m):
        if kp > 2:
            for k in range(2, kp):

                @when(core0, lam != k)
                def _():
                    wait_low(m, k)

            @when(core0)
            def _():
                fw(m).start()

            later(functools.partial(fw, m), core0)

    def have_low(m):
        @when(core0)
        def _():
            wait_low(m, 1)

        if kp > 2:

            @when(core1)
            def _():
                fw(m).wait_recv()

    def rs(h, j, d):
        to = lax.rem(q + d, NSEP)
        return rcopy(
            b.TT.at[j, chunk(h, to), :],
            b.rsb.at[j, d, part(h)],
            b.rsS.at[h, j, d],
            b.rsR.at[h, j, d],
            at_sep(d),
        )

    loads["inv"].wait()
    ih, il = split(b.inv[...])
    b.ih[...] = ih
    b.il[...] = il
    for h in HALVES:
        for d in range(1, NSEP):

            @pl.when(q - d >= 0)
            def _():
                ag(h, d).wait_recv()

        sh, sl = split(b.S[:, lanes(h)])
        ih = b.ih[...]
        yT = (mm(ih, sh) + (mm(b.il[...], sh) + mm(ih, sl))).T
        b.yT[lanes(h), :] = yT
        yh, yl = split(yT)
        for j in range(depth):
            bh = b.updh[:, j * cap : (j + 1) * cap]
            bl = b.updl[:, j * cap : (j + 1) * cap]
            b.TT[j, lanes(h), :] = mm(yh, bh) + (mm(yl, bh) + mm(yh, bl))
            for d in (2, 1, 3):
                rs(h, j, d).start()
                later(functools.partial(rs, h, j, d))
        if h == 0:
            along_z(0)

    pass_low(0)
    along_z(1)

    def yg(m, d):
        dst, src = ((b.MB, b.PM), (b.NB, b.PN))[m]
        hi = depth if m == 0 else depth + 1
        return rcopy(
            src.at[kp:hi], dst.at[kp:hi, ds(y, mb), :], b.ygS.at[m, d], b.ygR.at[m, d], at_y(d)
        )

    def gather_high(m):
        hi = depth if m == 0 else depth + 1

        @when(core0)
        def _():
            for k in range(kp + 1, hi):

                @pl.when(plane != k)
                def _():
                    wait_zm(m, k)

            for d in range(1, ny):

                @pl.when(even_at(d))
                def _():
                    yg(m, d).start()

        for d in range(1, ny):
            later(functools.partial(yg, m, d), core0, even_at(d))

        @when(solver)
        def _():
            dst, src = ((b.MB, b.PM), (b.NB, b.PN))[m]
            dst[kp:hi, ds(y, mb), :] = src[kp:hi]

    gather_high(0)
    for d in range(1, NSEP):
        ssx(d).wait_recv()
    sT = jnp.concatenate([b.ssb[i][:, :cols] for i in range(NSEP)], axis=1)
    b.sT[...] = sT

    def prepare(k):
        if k < depth:
            mh, ml = split(b.MB[k])
            b.Mh[k] = mh
            b.Ml[k] = ml
            th, tl = split(b.MB[k].T)
            b.Th[k] = th
            b.Tl[k] = tl

    def prepare_n(k):
        nh, nl = split(b.NB[k])
        b.Nh[k] = nh
        b.Nl[k] = nl

    have_low(0)
    for k in range(1, kp):
        prepare(k)


    def own_part(h, k):
        for d in range(1, NSEP):
            rs(h, k - 1, d).wait_recv()
        r = part(h)
        t = (b.TT[k - 1, chunk(h, q), :] + b.rsb[k - 1, 1, r]) + (
            b.rsb[k - 1, 2, r] + b.rsb[k - 1, 3, r]
        )
        mine_k = jnp.where(lam == k, b.sT[r, :], 0.0) - picked_by(t, b.pick[k - 1], 1)
        if 1 < k <= kp:
            mine_k = mine_k - chain(b.RP[k - 1, r], b.Th[k - 1], b.Tl[k - 1])
        b.RP[k, r] = mine_k

    groups = ((2, kp), (kp, depth), (depth, depth + 1))
    sums_on = (core1, core0, core0)
    sends_to_pair = (core0, core1, core1)

    def r1():
        return rcopy(b.RP.at[1], b.R1, b.cxS.at[0, 3], b.cxR.at[0, 3], at_pair)

    def cx(h, i):
        lo, hi = groups[i]
        return rcopy(
            b.RP.at[lo:hi, part(h)],
            b.CX.at[lo:hi, part(h)],
            b.cxS.at[h, i],
            b.cxR.at[h, i],
            at_pair,
        )

    def hr(i, d):
        lo, hi = groups[i]
        if i == 0:
            src, dst = b.H.at[lo:hi, ds(y_of(d), rb), :], b.HR.at[y]
        else:
            src = b.H.at[lo:hi, ds(lax.div(y_of(d), 2), rh), :]
            dst = b.HH.at[y, lo - kp : hi - kp]
        return rcopy(src, dst, b.hrS.at[i, d], b.hrR.at[i, d], at_y(d))

    def share(h, i):
        lo, hi = groups[i]

        @when(sends_to_pair[i])
        def _():
            cx(h, i).start()

        later(functools.partial(cx, h, i), sends_to_pair[i])

        @when(sums_on[i])
        def _():
            cx(h, i).wait_recv()
            r = part(h)
            b.H[lo:hi, r] = b.RP[lo:hi, r] + b.CX[lo:hi, r]
            for d in range(1, ny):
                goes = in_half(y_of(d), h)

                @pl.when(jnp.logical_and(goes, even_at(d)) if i else goes)
                def _():
                    hr(i, d).start()

        if i:

            @when(solver, in_half(y, h))
            def _():
                b.HH[y, lo - kp : hi - kp] = b.H[lo:hi, ds(lax.div(y, 2), rh), :]

        else:

            @when(core1, in_half(y, h))
            def _():
                b.HR[y] = b.H[lo:hi, ds(y, rb), :]

    for i in range(3):
        for d in range(1, ny):
            later(functools.partial(hr, i, d), sums_on[i], *((even_at(d),) if i else ()))

    for h in HALVES:
        for k in range(1, kp):
            own_part(h, k)
        if h == 1:
            r1().start()
            later(r1)
        share(h, 0)
        for k in range(kp, depth):
            own_part(h, k)
        share(h, 1)
        own_part(h, depth)
        share(h, 2)
        if h == 0:
            gather_high(1)
    pass_low(1)

    def br(d):
        place = b.RF.at[2:kp, ds(y, rb), :]
        return rcopy(b.B.at[y_of(d)], place, b.brS.at[d], b.brR.at[d], at_y(d))

    def z_xor(i):
        other = z
        for bit in range(nz.bit_length() - 1):
            if i >> bit & 1:
                other = other + 2**bit - 2 ** (bit + 1) * lax.rem(lax.div(z, 2**bit), 2)
        return other

    def zr(k, i):
        device = (l + 2 * ny * (z_xor(i) - z), q)
        at = k - kp - 1
        return rcopy(b.ZT.at[at], b.ZR.at[at, z], b.zrS.at[at, i], b.zrR.at[at, i], device)

    def bz(k, d):
        place = b.X.at[k, ds(lax.div(y, 2), rh), :]
        return rcopy(b.BZ.at[k - kp], place, b.bzS.at[k - kp, d], b.bzR.at[k - kp, d], at_y(d))

    def back_low():
        place = b.RF.at[2:kp]
        return rcopy(place, place, b.bkS.at[0], b.bkR.at[0], at_pair)

    def back_high(h, k):
        place = b.X.at[k, part(h)]
        return rcopy(place, place, b.bhS.at[h, k], b.bhR.at[h, k], at_pair)

    @when(core1)
    def _():
        for d in range(1, ny):
            hr(0, d).wait_recv()
        for k in range(2, kp):
            step = 2 ** (k - 1)
            for g in range(0, ny, step):
                total = b.HR[g, k - 2]
                for i in range(1, step):
                    total = total + b.HR[g + i, k - 2]
                for i in range(step):
                    b.B[g + i, k - 2] = total
        for d in range(1, ny):
            br(d).start()
        b.RF[2:kp, ds(y, rb), :] = b.B[y]
        for d in range(1, ny):
            br(d).wait_recv()
        back_low().start()

    for d in range(1, ny):
        later(functools.partial(br, d), core1)
    later(back_low, core1)

    @when(solver)
    def _():
        for d in range(1, ny):
            yg(0, d).wait_recv()
        for k in range(kp, depth):
            prepare(k)
        for k in range(kp, depth + 1):
            if k == kp or k == depth:
                for d in range(1, ny):
                    hr(1 if k == kp else 2, d).wait_recv()
            total = b.HH[0, k - kp]
            for i in range(1, ny):
                total = total + b.HH[i, k - kp]
            if k > kp:
                total = total - chain(b.RZ[k - 1], b.Th[k - 1], b.Tl[k - 1])
                b.ZT[k - kp - 1] = total
                for i in range(1, 2 ** (k - kp)):
                    zr(k, i).start()
                b.ZR[k - kp - 1, z] = total
            b.RZ[k] = total

    for k in range(kp + 1, depth + 1):
        for i in range(1, 2 ** (k - kp)):
            later(functools.partial(zr, k, i), solver)

    have_low(1)
    for k in range(1, kp):
        prepare_n(k)
    r1().wait_recv()
    b.RF[1] = b.RP[1] + b.R1[...]

    @when(core0)
    def _():
        back_low().wait_recv()

    for k in range(1, kp):
        b.V[k] = chain(b.RF[k], b.Nh[k], b.Nl[k])

    @when(solver)
    def _():
        for d in range(1, ny):
            yg(1, d).wait_recv()
        for k in range(kp, depth + 1):
            prepare_n(k)
        for k in range(kp, depth + 1):
            total = b.RZ[k]
            if k > kp:
                step = 2 ** (k - kp)
                for i in range(1, step):
                    zr(k, i).wait_recv()
                first = z - lax.rem(z, step)
                total = b.ZR[k - kp - 1, first]
                for i in range(1, step):
                    total = total + b.ZR[k - kp - 1, first + i]
            b.BZ[k - kp] = chain(total, b.Nh[k], b.Nl[k])
        for k in range(depth, kp - 1, -1):
            if k < depth:
                b.BZ[k - kp] = b.BZ[k - kp] - chain(b.BZ[k + 1 - kp], b.Mh[k], b.Ml[k])
            for d in range(1, ny):
                bz(k, d).start()
            b.X[k, ds(lax.div(y, 2), rh), :] = b.BZ[k - kp]

    def arrive(h, k):
        @when(core0)
        def _():
            for d in range(1, ny):

                @when(even_at(d), in_half(y_of(ny - d), h))
                def _():
                    bz(k, d).wait_recv()

            back_high(h, k).start()

        @when(core1)
        def _():
            back_high(h, k).wait_recv()

    for k in range(kp, depth + 1):
        for d in range(1, ny):
            later(functools.partial(bz, k, d), solver)
        for h in HALVES:
            later(functools.partial(back_high, h, k), core0)

    def pk(h, j, d):
        place = b.pkb.at[chunk(h, q), (j - 1) * cap : j * cap]
        return rcopy(place, place, b.pkS.at[h, j, d], b.pkR.at[h, j, d], at_sep(d))

    for h in HALVES:
        r = part(h)
        for j in range(depth, 0, -1):
            if j >= kp:
                arrive(h, j)
            if j <= kp and j > 1:
                b.X[j - 1, r] = b.V[j - 1, r] - chain(b.X[j, r], b.Mh[j - 1], b.Ml[j - 1])
            b.pkb[chunk(h, q), (j - 1) * cap : j * cap] = picked_by(b.X[j, r], b.pick[j - 1], 0)
            for d in (2, 1, 3):
                pk(h, j, d).start()
                later(functools.partial(pk, h, j, d))

    def xo(d):
        to = lax.rem(q + d, NSEP)
        return rcopy(b.xp.at[ds(to, cols), :], b.xob.at[q], b.xS.at[d], b.xR.at[d], at_sep(d))

    b.xp[...] = jnp.zeros_like(b.xp)

    @when(owner)
    def _():
        b.xp[:, :cols] = b.X[lam].T

    b.xob[q] = b.xp[mine, :]
    for d in range(1, NSEP):
        xo(d).start()
        later(functools.partial(xo, d))

    def fin(h, d):
        to = q - d
        return rcopy(
            b.XB.at[ds(to, rows), lanes(h)],
            b.fb.at[d, :, lanes(h)],
            b.fS.at[h, d],
            b.fR.at[h, d],
            (l, to),
        )

    def wait_fin(h, d):
        place = b.fb.at[d, :, lanes(h)]
        rcopy(place, place, b.fS.at[h, d], b.fR.at[h, d], at_sep(d)).wait_recv()

    for h in HALVES:
        for j in range(depth, 0, -1):
            for d in range(1, NSEP):
                pk(h, j, d).wait_recv()
        ph, pw = split(b.pkb[lanes(h), :])
        uh = b.updh[...]
        wT = b.yT[lanes(h), :] - (mm(ph, uh, 1, 1) + (mm(pw, uh, 1, 1) + mm(ph, b.updl[...], 1, 1)))
        wh, wl = split(wT.T)
        ih = b.ih[...]
        b.XB[:, lanes(h)] = mm(ih, wh, 0, 0) + (mm(b.il[...], wh, 0, 0) + mm(ih, wl, 0, 0))
        for d in (2, 1, 3):

            @pl.when(q - d >= 0)
            def _():
                fin(h, d).start()

            later(functools.partial(fin, h, d), q - d >= 0)

    for d in range(1, NSEP):
        xo(d).wait_recv()
    b.sol[...] = jnp.concatenate(
        [b.xob[i][:, h * ch : (h + 1) * ch] for h in HALVES for i in range(NSEP)], axis=1
    )
    for h in HALVES:
        b.out[:, lanes(h)] = b.XB[own, lanes(h)]
        for d in range(1, NSEP):

            @pl.when(q + d < NSEP)
            def _():
                wait_fin(h, d)
                b.out[:, lanes(h)] += b.fb[d, :, lanes(h)]

    for copy, conditions in drains:
        if conditions:

            @when(*conditions)
            def _():
                copy().wait_send()

        else:
            copy().wait_send()


def per_device(ny, nz, src, inv, upd, lists, counts, ssrc, sinv, cpl):
    depth = counts.shape[1]
    rows, n = src.shape[1:]
    order = inv.shape[2]
    urows = upd.shape[1]
    cols = ssrc.shape[1]
    w = sinv.shape[1]
    cap = urows // depth
    s = depth + 1
    kp = depth - nz.bit_length() + 1
    rb = cols // ny
    mb = w // ny
    f = lambda *shape: pltpu.VMEM(shape, F32)
    h = lambda *shape: pltpu.VMEM(shape, BF16)
    dma = lambda *shape: pltpu.SemaphoreType.DMA(shape)
    vm = pl.BlockSpec(memory_space=pltpu.VMEM)
    hbm = pl.BlockSpec(memory_space=pl.ANY)
    scratch = dict(
        ssrc=f(cols, n),
        sinv=f(w, w),
        cpl=f(w, w),
        inv=f(rows, order),
        upd=f(rows, urows),
        ldS=dma(6),
        S=f(order, n),
        sp=f(n, 128),
        ssb=f(NSEP, cols, 128),
        sT=f(cols, w),
        Mo=f(w, w),
        No=f(w, w),
        MB=f(s, w, w),
        NB=f(s, w, w),
        PM=f(s, mb, w),
        PN=f(s, mb, w),
        Mh=h(s, w, w),
        Ml=h(s, w, w),
        Th=h(s, w, w),
        Tl=h(s, w, w),
        Nh=h(s, w, w),
        Nl=h(s, w, w),
        pick=h(depth, w, cap),
        yT=f(n, rows),
        updh=h(rows, urows),
        updl=h(rows, urows),
        TT=f(depth, n, cap),
        rsb=f(depth, NSEP, cols, cap),
        RP=f(s, cols, w),
        R1=f(cols, w),
        CX=f(s, cols, w),
        H=f(s, cols, w),
        HR=f(ny, kp - 2, rb, w),
        HH=f(ny, depth - kp + 1, 2 * rb, w),
        B=f(ny, kp - 2, rb, w),
        RZ=f(s, 2 * rb, w),
        ZT=f(depth - kp, 2 * rb, w),
        ZR=f(depth - kp, nz, 2 * rb, w),
        BZ=f(depth - kp + 1, 2 * rb, w),
        RF=f(kp, cols, w),
        V=f(kp, cols, w),
        X=f(s, cols, w),
        pkb=f(n, urows),
        XB=f(order, n),
        fb=f(NSEP, rows, n),
        xp=f(n, 128),
        xob=f(NSEP, cols, 128),
        ih=h(rows, order),
        il=h(rows, order),
        agS=dma(2, NSEP),
        agR=dma(2, NSEP),
        ssS=dma(NSEP),
        ssR=dma(NSEP),
        moS=dma(2, 8),
        mlR=dma(2, s),
        scS=dma(2, ny),
        scR=dma(2, s),
        zmS=dma(2, nz),
        zmR=dma(2, s),
        ygS=dma(2, ny),
        ygR=dma(2, ny),
        fwS=dma(2),
        fwR=dma(2),
        rsS=dma(2, depth, NSEP),
        rsR=dma(2, depth, NSEP),
        cxS=dma(2, 4),
        cxR=dma(2, 4),
        hrS=dma(3, ny),
        hrR=dma(3, ny),
        brS=dma(ny),
        brR=dma(ny),
        bzS=dma(depth - kp + 1, ny),
        bzR=dma(depth - kp + 1, ny),
        zrS=dma(depth - kp, nz),
        zrR=dma(depth - kp, nz),
        bkS=dma(1),
        bkR=dma(1),
        bhS=dma(2, s),
        bhR=dma(2, s),
        pkS=dma(2, s, NSEP),
        pkR=dma(2, s, NSEP),
        xS=dma(NSEP),
        xR=dma(NSEP),
        fS=dma(2, NSEP),
        fR=dma(2, NSEP),
    )
    operands = ["counts", "xsrc", "xinv", "xupd", "lists", "xssrc", "xsinv", "xcpl", "out", "sol"]
    out, sol = pl.pallas_call(
        functools.partial(kernel, (ny, nz, depth), operands + list(scratch)),
        out_shape=(
            jax.ShapeDtypeStruct((rows, n), F32),
            jax.ShapeDtypeStruct((cols, n), F32),
        ),
        in_specs=[pl.BlockSpec(memory_space=pltpu.SMEM)] + [hbm] * 3 + [vm] + [hbm] * 3,
        out_specs=(vm, vm),
        scratch_shapes=list(scratch.values()),
        compiler_params=pltpu.CompilerParams(
            collective_id=0, has_side_effects=True, vmem_limit_bytes=62 * 2**20
        ),
    )(counts, src[0], inv[0], upd[0].T, lists, ssrc[0], sinv[0], cpl[0])
    return out[None], sol[None]


def solution(mesh):
    leaves = mesh.shape["leaf"]
    ny = nz = 8
    if leaves != 2 * ny * nz:
        ny, nz = (leaves // 4, 2)
    placed = (
        P("leaf", "sep", None),
        P("leaf", "sep", None),
        P("leaf", None, "sep"),
        P("leaf", None),
        P("leaf", None),
        P("leaf", "sep", None),
        P("leaf", None, None),
        P("leaf", None, None),
    )
    return jax.shard_map(
        functools.partial(per_device, ny, nz),
        mesh=mesh,
        in_specs=placed,
        out_specs=(P("leaf", "sep", None), P("leaf", "sep", None)),
        check_vma=False,
    )
```

```python
import functools
import types

import jax
import jax.numpy as jnp
from jax import lax
from jax.experimental import pallas as pl
from jax.experimental.pallas import tpu as pltpu
from jax.sharding import PartitionSpec as P

MESH = pl.DeviceIdType.MESH
F32 = jnp.float32
BF16 = jnp.bfloat16
NSEP = 4
HALVES = range(2)


def split(x):
    high = x.astype(BF16)
    return high, (x - high.astype(F32)).astype(BF16)


def mm(a, b, ca=1, cb=0):
    return lax.dot_general(a, b, (((ca,), (cb,)), ((), ())), preferred_element_type=F32)


def mm3(a, b, ca=1, cb=0):
    ah, al = split(a)
    bh, bl = split(b)
    return mm(ah, bh, ca, cb) + (mm(al, bh, ca, cb) + mm(ah, bl, ca, cb))


def chain(rows, wh, wl):
    high, low = split(rows)
    m = rows.shape[0]
    both = mm(jnp.concatenate([high, low], axis=0), wh)
    return both[:m] + (both[m:] + mm(high, wl))


def picked_by(rows, picker, cb):
    high, low = split(rows)
    m = rows.shape[0]
    both = mm(jnp.concatenate([high, low], axis=0), picker, 1, cb)
    return both[:m] + both[m:]


def level_of(index, depth):
    level = jnp.int32(1)
    for k in range(1, depth + 1):
        level = level + (lax.rem(index, 2**k) == 0).astype(jnp.int32)
    return level


def kernel(dims, names, *refs):
    ny, nz, depth = dims
    b = types.SimpleNamespace(**dict(zip(names, refs)))
    kp = depth - nz.bit_length() + 1
    l = lax.axis_index("leaf")
    q = lax.axis_index("sep")
    c = lax.rem(l, 2)
    y = lax.rem(lax.div(l, 2), ny)
    z = lax.div(l, 2 * ny)
    pair = l + 1 - 2 * c
    rows = b.xsrc.shape[0]
    cols = b.xssrc.shape[0]
    w = b.xsinv.shape[0]
    cap = b.lists.shape[1] // depth
    rb = cols // ny
    rh = 2 * rb
    mb = w // ny
    lam = level_of(l, depth)
    plane = level_of(z * 2 * ny, depth)
    core0 = c == 0
    core1 = c == 1
    owner = l > 0
    even_y = lax.rem(y, 2) == 0
    solver = jnp.logical_and(core0, even_y)

    def when(*conditions):
        return pl.when(functools.reduce(jnp.logical_and, conditions))

    def at_sep(d):
        return (l, lax.rem(q + d, NSEP))

    def y_of(d):
        return lax.rem(y + d, ny)

    def z_of(d):
        return lax.rem(z + d, nz)

    def even_at(d):
        return lax.rem(y + d, 2) == 0

    def at_y(d):
        return (l - 2 * y + 2 * y_of(d), q)

    def at_z(d):
        return (l + 2 * ny * (z_of(d) - z), q)

    at_pair = (pair, q)

    def rcopy(a, dst, ss, rs, device):
        return pltpu.make_async_remote_copy(
            src_ref=a, dst_ref=dst, send_sem=ss, recv_sem=rs, device_id=device, device_id_type=MESH
        )

    drains = []

    def later(copy, *conditions):
        drains.append((copy, conditions))

    def ds(index, size):
        return pl.ds(pl.multiple_of(index * size, 8), size)

    own = ds(q, rows)
    mine = ds(q, cols)
    n = b.S.shape[1]
    nh = n // 2
    ch = cols // 2

    def lanes(h):
        return pl.ds(h * nh, nh)

    def part(h):
        return pl.ds(h * ch, ch)

    def chunk(h, index):
        return pl.ds(pl.multiple_of(h * nh + index * ch, 8), ch)

    def in_half(index, h):
        return lax.div(index, ny // 2) == h

    loads = {}
    for i, (name, dst) in enumerate(
        (
            ("src", b.S.at[own, :]),
            ("ssrc", b.ssrc),
            ("sinv", b.sinv),
            ("cpl", b.cpl),
            ("inv", b.inv),
            ("upd", b.upd),
        )
    ):
        loads[name] = pltpu.make_async_copy(getattr(b, "x" + name), dst, b.ldS.at[i])
        loads[name].start()

    barrier = pltpu.get_barrier_semaphore()
    greeted = [at_sep(d) for d in range(1, NSEP)] + [at_pair]
    greeted += [at_y(d) for d in range(1, ny)] + [at_z(d) for d in range(1, nz)]
    for device in greeted:
        pl.semaphore_signal(barrier, inc=1, device_id=device, device_id_type=MESH)

    for j in range(1, NSEP):

        @pl.when(j > q)
        def _():
            b.S[j * rows : (j + 1) * rows, :] = jnp.zeros((rows, b.S.shape[1]), F32)

    b.sp[...] = jnp.zeros_like(b.sp)
    loads["src"].wait()
    pl.semaphore_wait(barrier, len(greeted))

    def ag(h, d):
        place = b.S.at[own, lanes(h)]
        return rcopy(place, place, b.agS.at[h, d], b.agR.at[h, d], at_sep(d))

    for h in HALVES:
        for d in (2, 1, 3):

            @pl.when(q + d < NSEP)
            def _():
                ag(h, d).start()

            later(functools.partial(ag, h, d), q + d < NSEP)

    def ssx(d):
        to = lax.rem(q + d, NSEP)
        return rcopy(b.sp.at[ds(to, cols), :], b.ssb.at[q], b.ssS.at[d], b.ssR.at[d], at_sep(d))

    loads["ssrc"].wait()
    turned = b.ssrc[...].T
    for i in range(NSEP):
        for h in HALVES:
            block = turned[h * nh + i * ch : h * nh + (i + 1) * ch]
            b.sp[i * cols + h * ch : i * cols + (h + 1) * ch, :cols] = block
    b.ssb[q] = b.sp[mine, :]
    for d in range(1, NSEP):
        ssx(d).start()
        later(functools.partial(ssx, d))

    loads["sinv"].wait()
    loads["cpl"].wait()
    def low_of(k, device, slot, m):
        src, dst = ((b.Mo, b.MB), (b.No, b.NB))[m]
        return rcopy(src, dst.at[k], b.moS.at[m, slot], b.mlR.at[m, k], device)

    def send_low(m):
        targets = [(1, at_pair, 0, (core1,))]
        for k in range(2, kp):
            reach = 2 ** (k - 2)
            offsets = [o for o in range(-reach, reach) if o]
            for slot, o in enumerate(offsets):
                targets.append((k, (l + 2 * o, q), slot, (core0, lam == k)))
        for k, device, slot, conditions in targets:

            @when(*conditions)
            def _():
                low_of(k, device, slot, m).start()

            later(functools.partial(low_of, k, device, slot, m), *conditions)
        for k in range(1, kp):

            @when(lam == k)
            def _():
                if m == 0:
                    b.MB[k] = b.Mo[...]
                else:
                    b.NB[k] = b.No[...]

    def sc(m, d):
        src, dst = ((b.Mo, b.PM), (b.No, b.PN))[m]
        return rcopy(
            src.at[ds(y_of(d), mb), :], dst.at[lam], b.scS.at[m, d], b.scR.at[m, lam], at_y(d)
        )

    def wait_sc(m, k):
        dst = (b.PM, b.PN)[m]
        rcopy(dst.at[k], dst.at[k], b.scS.at[m, 0], b.scR.at[m, k], at_pair).wait_recv()

    high = jnp.logical_and(core0, jnp.logical_and(lam >= kp, owner))

    def send_high(m):
        has = (high, lam < depth) if m == 0 else (high,)

        @when(*has)
        def _():
            for d in range(1, ny):
                sc(m, d).start()
            dst, src = ((b.PM, b.Mo), (b.PN, b.No))[m]
            dst[lam] = src[ds(y, mb), :]

        for d in range(1, ny):
            later(functools.partial(sc, m, d), *has)

    sinv = b.sinv[...]
    b.Mo[...] = mm3(b.cpl[...], sinv)
    send_high(0)
    send_low(0)
    b.No[...] = mm3(sinv, sinv, 0, 0)
    send_high(1)
    send_low(1)

    wi = lax.broadcasted_iota(jnp.int32, (w, cap), 0)
    pi = lax.broadcasted_iota(jnp.int32, (w, cap), 1)
    for j in range(depth):
        hit = jnp.logical_and(wi == b.lists[0:1, j * cap : (j + 1) * cap], pi < b.counts[0, j])
        b.pick[j] = jnp.where(hit, 1.0, 0.0).astype(BF16)
    loads["upd"].wait()
    uh, ul = split(b.upd[...])
    b.updh[...] = uh
    b.updl[...] = ul

    def zm(m, d):
        dst = (b.PM, b.PN)[m]
        return rcopy(dst.at[plane], dst.at[plane], b.zmS.at[m, d], b.zmR.at[m, plane], at_z(d))

    def wait_zm(m, k):
        dst = (b.PM, b.PN)[m]
        rcopy(dst.at[k], dst.at[k], b.zmS.at[m, 0], b.zmR.at[m, k], at_pair).wait_recv()

    size = jnp.int32(1)
    for k in range(kp + 1, depth + 1):
        size = size + (plane >= k).astype(jnp.int32) * 2 ** (k - kp - 1)
    base = z - lax.div(size, 2)

    def in_node(d):
        zd = z_of(d)
        return jnp.logical_and(zd >= base, zd < base + size)

    def along_z(m):
        top = depth - 1 if m == 0 else depth

        @when(core0, y != ny // 2)
        def _():
            wait_sc(m, kp)

        @when(core0, y != 0, plane <= top)
        def _():
            wait_sc(m, plane)

        for d in range(1, nz):
            sends = (core0, plane <= top, in_node(d))

            @when(*sends)
            def _():
                zm(m, d).start()

            later(functools.partial(zm, m, d), *sends)

    def wait_low(m, k):
        dst = (b.MB, b.NB)[m]
        rcopy(dst.at[k], dst.at[k], b.moS.at[m, 0], b.mlR.at[m, k], at_pair).wait_recv()

    def fw(m):
        place = (b.MB, b.NB)[m].at[2:kp]
        return rcopy(place, place, b.fwS.at[m], b.fwR.at[m], at_pair)

    def pass_low(m):
        if kp > 2:
            for k in range(2, kp):

                @when(core0, lam != k)
                def _():
                    wait_low(m, k)

            @when(core0)
            def _():
                fw(m).start()

            later(functools.partial(fw, m), core0)

    def have_low(m):
        @when(core0)
        def _():
            wait_low(m, 1)

        if kp > 2:

            @when(core1)
            def _():
                fw(m).wait_recv()

    def yg(m, d):
        dst, src = ((b.MB, b.PM), (b.NB, b.PN))[m]
        hi = depth if m == 0 else depth + 1
        return rcopy(
            src.at[kp:hi], dst.at[kp:hi, ds(y, mb), :], b.ygS.at[m, d], b.ygR.at[m, d], at_y(d)
        )

    def gather_high(m):
        hi = depth if m == 0 else depth + 1

        @when(core0)
        def _():
            for k in range(kp + 1, hi):

                @pl.when(plane != k)
                def _():
                    wait_zm(m, k)

            for d in range(1, ny):

                @pl.when(even_at(d))
                def _():
                    yg(m, d).start()

        for d in range(1, ny):
            later(functools.partial(yg, m, d), core0, even_at(d))

        @when(solver)
        def _():
            dst, src = ((b.MB, b.PM), (b.NB, b.PN))[m]
            dst[kp:hi, ds(y, mb), :] = src[kp:hi]

    def rs(h, j, d):
        to = lax.rem(q + d, NSEP)
        return rcopy(
            b.TT.at[j, chunk(h, to), :],
            b.rsb.at[j, d, part(h)],
            b.rsS.at[h, j, d],
            b.rsR.at[h, j, d],
            at_sep(d),
        )

    loads["inv"].wait()
    ih, il = split(b.inv[...])
    b.ih[...] = ih
    b.il[...] = il
    along_z(0)
    for h in HALVES:
        for d in range(1, NSEP):

            @pl.when(q - d >= 0)
            def _():
                ag(h, d).wait_recv()

        sh, sl = split(b.S[:, lanes(h)])
        ih = b.ih[...]
        yT = (mm(ih, sh) + (mm(b.il[...], sh) + mm(ih, sl))).T
        b.yT[lanes(h), :] = yT
        yh, yl = split(yT)
        for j in range(depth):
            bh = b.updh[:, j * cap : (j + 1) * cap]
            bl = b.updl[:, j * cap : (j + 1) * cap]
            b.TT[j, lanes(h), :] = mm(yh, bh) + (mm(yl, bh) + mm(yh, bl))
            for d in (2, 1, 3):
                rs(h, j, d).start()
                later(functools.partial(rs, h, j, d))
        if h == 0:
            along_z(1)
            gather_high(0)

    pass_low(0)

    for d in range(1, NSEP):
        ssx(d).wait_recv()
    sT = jnp.concatenate([b.ssb[i][:, :cols] for i in range(NSEP)], axis=1)
    b.sT[...] = sT

    def prepare(k):
        if k < depth:
            mh, ml = split(b.MB[k])
            b.Mh[k] = mh
            b.Ml[k] = ml
            th, tl = split(b.MB[k].T)
            b.Th[k] = th
            b.Tl[k] = tl

    def prepare_n(k):
        nh, nl = split(b.NB[k])
        b.Nh[k] = nh
        b.Nl[k] = nl

    have_low(0)
    for k in range(1, kp):
        prepare(k)


    def own_part(h, k):
        for d in range(1, NSEP):
            rs(h, k - 1, d).wait_recv()
        r = part(h)
        t = (b.TT[k - 1, chunk(h, q), :] + b.rsb[k - 1, 1, r]) + (
            b.rsb[k - 1, 2, r] + b.rsb[k - 1, 3, r]
        )
        mine_k = jnp.where(lam == k, b.sT[r, :], 0.0) - picked_by(t, b.pick[k - 1], 1)
        if 1 < k <= kp:
            mine_k = mine_k - chain(b.RP[k - 1, r], b.Th[k - 1], b.Tl[k - 1])
        b.RP[k, r] = mine_k

    groups = ((2, kp), (kp, depth), (depth, depth + 1))
    sums_on = (core1, core0, core0)
    sends_to_pair = (core0, core1, core1)

    def r1():
        return rcopy(b.RP.at[1], b.R1, b.cxS.at[0, 3], b.cxR.at[0, 3], at_pair)

    def cx(h, i):
        lo, hi = groups[i]
        return rcopy(
            b.RP.at[lo:hi, part(h)],
            b.CX.at[lo:hi, part(h)],
            b.cxS.at[h, i],
            b.cxR.at[h, i],
            at_pair,
        )

    def hr(i, d):
        lo, hi = groups[i]
        if i == 0:
            src, dst = b.H.at[lo:hi, ds(y_of(d), rb), :], b.HR.at[y]
        else:
            src = b.H.at[lo:hi, ds(lax.div(y_of(d), 2), rh), :]
            dst = b.HH.at[y, lo - kp : hi - kp]
        return rcopy(src, dst, b.hrS.at[i, d], b.hrR.at[i, d], at_y(d))

    def share(h, i):
        lo, hi = groups[i]

        @when(sends_to_pair[i])
        def _():
            cx(h, i).start()

        later(functools.partial(cx, h, i), sends_to_pair[i])

        @when(sums_on[i])
        def _():
            cx(h, i).wait_recv()
            r = part(h)
            b.H[lo:hi, r] = b.RP[lo:hi, r] + b.CX[lo:hi, r]
            for d in range(1, ny):
                goes = in_half(y_of(d), h)

                @pl.when(jnp.logical_and(goes, even_at(d)) if i else goes)
                def _():
                    hr(i, d).start()

        if i:

            @when(solver, in_half(y, h))
            def _():
                b.HH[y, lo - kp : hi - kp] = b.H[lo:hi, ds(lax.div(y, 2), rh), :]

        else:

            @when(core1, in_half(y, h))
            def _():
                b.HR[y] = b.H[lo:hi, ds(y, rb), :]

    for i in range(3):
        for d in range(1, ny):
            later(functools.partial(hr, i, d), sums_on[i], *((even_at(d),) if i else ()))

    for h in HALVES:
        for k in range(1, kp):
            own_part(h, k)
        if h == 1:
            r1().start()
            later(r1)
        share(h, 0)
        for k in range(kp, depth):
            own_part(h, k)
        share(h, 1)
        own_part(h, depth)
        share(h, 2)
        if h == 1:
            gather_high(1)
    pass_low(1)

    def br(d):
        place = b.RF.at[2:kp, ds(y, rb), :]
        return rcopy(b.B.at[y_of(d)], place, b.brS.at[d], b.brR.at[d], at_y(d))

    def z_xor(i):
        other = z
        for bit in range(nz.bit_length() - 1):
            if i >> bit & 1:
                other = other + 2**bit - 2 ** (bit + 1) * lax.rem(lax.div(z, 2**bit), 2)
        return other

    def zr(k, i):
        device = (l + 2 * ny * (z_xor(i) - z), q)
        at = k - kp - 1
        return rcopy(b.ZT.at[at], b.ZR.at[at, z], b.zrS.at[at, i], b.zrR.at[at, i], device)

    def bz(k, d):
        place = b.X.at[k, ds(lax.div(y, 2), rh), :]
        return rcopy(b.BZ.at[k - kp], place, b.bzS.at[k - kp, d], b.bzR.at[k - kp, d], at_y(d))

    def back_low():
        place = b.RF.at[2:kp]
        return rcopy(place, place, b.bkS.at[0], b.bkR.at[0], at_pair)

    def back_high(h, k):
        place = b.X.at[k, part(h)]
        return rcopy(place, place, b.bhS.at[h, k], b.bhR.at[h, k], at_pair)

    @when(core1)
    def _():
        for d in range(1, ny):
            hr(0, d).wait_recv()
        for k in range(2, kp):
            step = 2 ** (k - 1)
            for g in range(0, ny, step):
                total = b.HR[g, k - 2]
                for i in range(1, step):
                    total = total + b.HR[g + i, k - 2]
                for i in range(step):
                    b.B[g + i, k - 2] = total
        for d in range(1, ny):
            br(d).start()
        b.RF[2:kp, ds(y, rb), :] = b.B[y]
        for d in range(1, ny):
            br(d).wait_recv()
        back_low().start()

    for d in range(1, ny):
        later(functools.partial(br, d), core1)
    later(back_low, core1)

    @when(solver)
    def _():
        for d in range(1, ny):
            yg(0, d).wait_recv()
        for k in range(kp, depth):
            prepare(k)
        for k in range(kp, depth + 1):
            if k == kp or k == depth:
                for d in range(1, ny):
                    hr(1 if k == kp else 2, d).wait_recv()
            total = b.HH[0, k - kp]
            for i in range(1, ny):
                total = total + b.HH[i, k - kp]
            if k > kp:
                total = total - chain(b.RZ[k - 1], b.Th[k - 1], b.Tl[k - 1])
                b.ZT[k - kp - 1] = total
                for i in range(1, 2 ** (k - kp)):
                    zr(k, i).start()
                b.ZR[k - kp - 1, z] = total
            b.RZ[k] = total

    for k in range(kp + 1, depth + 1):
        for i in range(1, 2 ** (k - kp)):
            later(functools.partial(zr, k, i), solver)

    @when(solver)
    def _():
        for d in range(1, ny):
            yg(1, d).wait_recv()
        for k in range(kp, depth + 1):
            prepare_n(k)
        for k in range(kp, depth + 1):
            total = b.RZ[k]
            if k > kp:
                step = 2 ** (k - kp)
                for i in range(1, step):
                    zr(k, i).wait_recv()
                first = z - lax.rem(z, step)
                total = b.ZR[k - kp - 1, first]
                for i in range(1, step):
                    total = total + b.ZR[k - kp - 1, first + i]
            b.BZ[k - kp] = chain(total, b.Nh[k], b.Nl[k])
        for k in range(depth, kp - 1, -1):
            if k < depth:
                b.BZ[k - kp] = b.BZ[k - kp] - chain(b.BZ[k + 1 - kp], b.Mh[k], b.Ml[k])
            for d in range(1, ny):
                bz(k, d).start()
            b.X[k, ds(lax.div(y, 2), rh), :] = b.BZ[k - kp]

    have_low(1)
    for k in range(1, kp):
        prepare_n(k)
    r1().wait_recv()
    b.RF[1] = b.RP[1] + b.R1[...]

    @when(core0)
    def _():
        back_low().wait_recv()

    for k in range(1, kp):
        b.V[k] = chain(b.RF[k], b.Nh[k], b.Nl[k])

    def arrive(h, k):
        @when(core0)
        def _():
            for d in range(1, ny):

                @when(even_at(d), in_half(y_of(ny - d), h))
                def _():
                    bz(k, d).wait_recv()

            back_high(h, k).start()

        @when(core1)
        def _():
            back_high(h, k).wait_recv()

    for k in range(kp, depth + 1):
        for d in range(1, ny):
            later(functools.partial(bz, k, d), solver)
        for h in HALVES:
            later(functools.partial(back_high, h, k), core0)

    def pk(h, j, d):
        place = b.pkb.at[chunk(h, q), (j - 1) * cap : j * cap]
        return rcopy(place, place, b.pkS.at[h, j, d], b.pkR.at[h, j, d], at_sep(d))

    for h in HALVES:
        r = part(h)
        for j in range(depth, 0, -1):
            if j >= kp:
                arrive(h, j)
            if j <= kp and j > 1:
                b.X[j - 1, r] = b.V[j - 1, r] - chain(b.X[j, r], b.Mh[j - 1], b.Ml[j - 1])
            b.pkb[chunk(h, q), (j - 1) * cap : j * cap] = picked_by(b.X[j, r], b.pick[j - 1], 0)
            for d in (2, 1, 3):
                pk(h, j, d).start()
                later(functools.partial(pk, h, j, d))

    def xo(d):
        to = lax.rem(q + d, NSEP)
        return rcopy(b.xp.at[ds(to, cols), :], b.xob.at[q], b.xS.at[d], b.xR.at[d], at_sep(d))

    b.xp[...] = jnp.zeros_like(b.xp)

    @when(owner)
    def _():
        b.xp[:, :cols] = b.X[lam].T

    b.xob[q] = b.xp[mine, :]
    for d in range(1, NSEP):
        xo(d).start()
        later(functools.partial(xo, d))

    def fin(h, d):
        to = q - d
        return rcopy(
            b.XB.at[ds(to, rows), lanes(h)],
            b.fb.at[d, :, lanes(h)],
            b.fS.at[h, d],
            b.fR.at[h, d],
            (l, to),
        )

    def wait_fin(h, d):
        place = b.fb.at[d, :, lanes(h)]
        rcopy(place, place, b.fS.at[h, d], b.fR.at[h, d], at_sep(d)).wait_recv()

    for h in HALVES:
        for j in range(depth, 0, -1):
            for d in range(1, NSEP):
                pk(h, j, d).wait_recv()
        ph, pw = split(b.pkb[lanes(h), :])
        uh = b.updh[...]
        wT = b.yT[lanes(h), :] - (mm(ph, uh, 1, 1) + (mm(pw, uh, 1, 1) + mm(ph, b.updl[...], 1, 1)))
        wh, wl = split(wT.T)
        ih = b.ih[...]
        b.XB[:, lanes(h)] = mm(ih, wh, 0, 0) + (mm(b.il[...], wh, 0, 0) + mm(ih, wl, 0, 0))
        for d in (2, 1, 3):

            @pl.when(q - d >= 0)
            def _():
                fin(h, d).start()

            later(functools.partial(fin, h, d), q - d >= 0)

    for d in range(1, NSEP):
        xo(d).wait_recv()
    b.sol[...] = jnp.concatenate(
        [b.xob[i][:, h * ch : (h + 1) * ch] for h in HALVES for i in range(NSEP)], axis=1
    )
    for h in HALVES:
        b.out[:, lanes(h)] = b.XB[own, lanes(h)]
        for d in range(1, NSEP):

            @pl.when(q + d < NSEP)
            def _():
                wait_fin(h, d)
                b.out[:, lanes(h)] += b.fb[d, :, lanes(h)]

    for copy, conditions in drains:
        if conditions:

            @when(*conditions)
            def _():
                copy().wait_send()

        else:
            copy().wait_send()


def per_device(ny, nz, src, inv, upd, lists, counts, ssrc, sinv, cpl):
    depth = counts.shape[1]
    rows, n = src.shape[1:]
    order = inv.shape[2]
    urows = upd.shape[1]
    cols = ssrc.shape[1]
    w = sinv.shape[1]
    cap = urows // depth
    s = depth + 1
    kp = depth - nz.bit_length() + 1
    rb = cols // ny
    mb = w // ny
    f = lambda *shape: pltpu.VMEM(shape, F32)
    h = lambda *shape: pltpu.VMEM(shape, BF16)
    dma = lambda *shape: pltpu.SemaphoreType.DMA(shape)
    vm = pl.BlockSpec(memory_space=pltpu.VMEM)
    hbm = pl.BlockSpec(memory_space=pl.ANY)
    scratch = dict(
        ssrc=f(cols, n),
        sinv=f(w, w),
        cpl=f(w, w),
        inv=f(rows, order),
        upd=f(rows, urows),
        ldS=dma(6),
        S=f(order, n),
        sp=f(n, 128),
        ssb=f(NSEP, cols, 128),
        sT=f(cols, w),
        Mo=f(w, w),
        No=f(w, w),
        MB=f(s, w, w),
        NB=f(s, w, w),
        PM=f(s, mb, w),
        PN=f(s, mb, w),
        Mh=h(s, w, w),
        Ml=h(s, w, w),
        Th=h(s, w, w),
        Tl=h(s, w, w),
        Nh=h(s, w, w),
        Nl=h(s, w, w),
        pick=h(depth, w, cap),
        yT=f(n, rows),
        updh=h(rows, urows),
        updl=h(rows, urows),
        TT=f(depth, n, cap),
        rsb=f(depth, NSEP, cols, cap),
        RP=f(s, cols, w),
        R1=f(cols, w),
        CX=f(s, cols, w),
        H=f(s, cols, w),
        HR=f(ny, kp - 2, rb, w),
        HH=f(ny, depth - kp + 1, 2 * rb, w),
        B=f(ny, kp - 2, rb, w),
        RZ=f(s, 2 * rb, w),
        ZT=f(depth - kp, 2 * rb, w),
        ZR=f(depth - kp, nz, 2 * rb, w),
        BZ=f(depth - kp + 1, 2 * rb, w),
        RF=f(kp, cols, w),
        V=f(kp, cols, w),
        X=f(s, cols, w),
        pkb=f(n, urows),
        XB=f(order, n),
        fb=f(NSEP, rows, n),
        xp=f(n, 128),
        xob=f(NSEP, cols, 128),
        ih=h(rows, order),
        il=h(rows, order),
        agS=dma(2, NSEP),
        agR=dma(2, NSEP),
        ssS=dma(NSEP),
        ssR=dma(NSEP),
        moS=dma(2, 8),
        mlR=dma(2, s),
        scS=dma(2, ny),
        scR=dma(2, s),
        zmS=dma(2, nz),
        zmR=dma(2, s),
        ygS=dma(2, ny),
        ygR=dma(2, ny),
        fwS=dma(2),
        fwR=dma(2),
        rsS=dma(2, depth, NSEP),
        rsR=dma(2, depth, NSEP),
        cxS=dma(2, 4),
        cxR=dma(2, 4),
        hrS=dma(3, ny),
        hrR=dma(3, ny),
        brS=dma(ny),
        brR=dma(ny),
        bzS=dma(depth - kp + 1, ny),
        bzR=dma(depth - kp + 1, ny),
        zrS=dma(depth - kp, nz),
        zrR=dma(depth - kp, nz),
        bkS=dma(1),
        bkR=dma(1),
        bhS=dma(2, s),
        bhR=dma(2, s),
        pkS=dma(2, s, NSEP),
        pkR=dma(2, s, NSEP),
        xS=dma(NSEP),
        xR=dma(NSEP),
        fS=dma(2, NSEP),
        fR=dma(2, NSEP),
    )
    operands = ["counts", "xsrc", "xinv", "xupd", "lists", "xssrc", "xsinv", "xcpl", "out", "sol"]
    out, sol = pl.pallas_call(
        functools.partial(kernel, (ny, nz, depth), operands + list(scratch)),
        out_shape=(
            jax.ShapeDtypeStruct((rows, n), F32),
            jax.ShapeDtypeStruct((cols, n), F32),
        ),
        in_specs=[pl.BlockSpec(memory_space=pltpu.SMEM)] + [hbm] * 3 + [vm] + [hbm] * 3,
        out_specs=(vm, vm),
        scratch_shapes=list(scratch.values()),
        compiler_params=pltpu.CompilerParams(
            collective_id=0, has_side_effects=True, vmem_limit_bytes=62 * 2**20
        ),
    )(counts, src[0], inv[0], upd[0].T, lists, ssrc[0], sinv[0], cpl[0])
    return out[None], sol[None]


def solution(mesh):
    leaves = mesh.shape["leaf"]
    ny = nz = 8
    if leaves != 2 * ny * nz:
        ny, nz = (leaves // 4, 2)
    placed = (
        P("leaf", "sep", None),
        P("leaf", "sep", None),
        P("leaf", None, "sep"),
        P("leaf", None),
        P("leaf", None),
        P("leaf", "sep", None),
        P("leaf", None, None),
        P("leaf", None, None),
    )
    return jax.shard_map(
        functools.partial(per_device, ny, nz),
        mesh=mesh,
        in_specs=placed,
        out_specs=(P("leaf", "sep", None), P("leaf", "sep", None)),
        check_vma=False,
    )
```

```python
import functools
import types

import jax
import jax.numpy as jnp
from jax import lax
from jax.experimental import pallas as pl
from jax.experimental.pallas import tpu as pltpu
from jax.sharding import PartitionSpec as P

MESH = pl.DeviceIdType.MESH
F32 = jnp.float32
BF16 = jnp.bfloat16
NSEP = 4
HALVES = range(2)


def split(x):
    high = x.astype(BF16)
    return high, (x - high.astype(F32)).astype(BF16)


def mm(a, b, ca=1, cb=0):
    return lax.dot_general(a, b, (((ca,), (cb,)), ((), ())), preferred_element_type=F32)


def mm3(a, b, ca=1, cb=0):
    ah, al = split(a)
    bh, bl = split(b)
    return mm(ah, bh, ca, cb) + (mm(al, bh, ca, cb) + mm(ah, bl, ca, cb))


def chain(rows, wh, wl):
    high, low = split(rows)
    m = rows.shape[0]
    both = mm(jnp.concatenate([high, low], axis=0), wh)
    return both[:m] + (both[m:] + mm(high, wl))


def picked_by(rows, picker, cb):
    high, low = split(rows)
    m = rows.shape[0]
    both = mm(jnp.concatenate([high, low], axis=0), picker, 1, cb)
    return both[:m] + both[m:]


def level_of(index, depth):
    level = jnp.int32(1)
    for k in range(1, depth + 1):
        level = level + (lax.rem(index, 2**k) == 0).astype(jnp.int32)
    return level


def kernel(dims, names, *refs):
    ny, nz, depth = dims
    b = types.SimpleNamespace(**dict(zip(names, refs)))
    kp = depth - nz.bit_length() + 1
    l = lax.axis_index("leaf")
    q = lax.axis_index("sep")
    c = lax.rem(l, 2)
    y = lax.rem(lax.div(l, 2), ny)
    z = lax.div(l, 2 * ny)
    pair = l + 1 - 2 * c
    rows = b.xsrc.shape[0]
    cols = b.xssrc.shape[0]
    w = b.xsinv.shape[0]
    cap = b.lists.shape[1] // depth
    rb = cols // ny
    rh = 2 * rb
    mb = w // ny
    lam = level_of(l, depth)
    plane = level_of(z * 2 * ny, depth)
    core0 = c == 0
    core1 = c == 1
    owner = l > 0
    even_y = lax.rem(y, 2) == 0
    solver = jnp.logical_and(core0, even_y)

    def when(*conditions):
        return pl.when(functools.reduce(jnp.logical_and, conditions))

    def at_sep(d):
        return (l, lax.rem(q + d, NSEP))

    def y_of(d):
        return lax.rem(y + d, ny)

    def z_of(d):
        return lax.rem(z + d, nz)

    def even_at(d):
        return lax.rem(y + d, 2) == 0

    def at_y(d):
        return (l - 2 * y + 2 * y_of(d), q)

    def at_z(d):
        return (l + 2 * ny * (z_of(d) - z), q)

    at_pair = (pair, q)

    def rcopy(a, dst, ss, rs, device):
        return pltpu.make_async_remote_copy(
            src_ref=a, dst_ref=dst, send_sem=ss, recv_sem=rs, device_id=device, device_id_type=MESH
        )

    drains = []

    def settle():
        for copy, conditions in drains:
            if conditions:

                @when(*conditions)
                def _():
                    copy().wait_send()

            else:
                copy().wait_send()
        drains.clear()

    def later(copy, *conditions):
        drains.append((copy, conditions))

    def ds(index, size):
        return pl.ds(pl.multiple_of(index * size, 8), size)

    own = ds(q, rows)
    mine = ds(q, cols)
    n = b.S.shape[1]
    nh = n // 2
    ch = cols // 2

    def lanes(h):
        return pl.ds(h * nh, nh)

    def part(h):
        return pl.ds(h * ch, ch)

    def chunk(h, index):
        return pl.ds(pl.multiple_of(h * nh + index * ch, 8), ch)

    def in_half(index, h):
        return lax.div(index, ny // 2) == h

    loads = {}
    for i, (name, dst) in enumerate(
        (
            ("src", b.S.at[own, :]),
            ("ssrc", b.ssrc),
            ("sinv", b.sinv),
            ("cpl", b.cpl),
            ("inv", b.inv),
            ("upd", b.upd),
        )
    ):
        loads[name] = pltpu.make_async_copy(getattr(b, "x" + name), dst, b.ldS.at[i])
        loads[name].start()

    barrier = pltpu.get_barrier_semaphore()
    greeted = [at_sep(d) for d in range(1, NSEP)] + [at_pair]
    greeted += [at_y(d) for d in range(1, ny)] + [at_z(d) for d in range(1, nz)]
    for device in greeted:
        pl.semaphore_signal(barrier, inc=1, device_id=device, device_id_type=MESH)

    for j in range(1, NSEP):

        @pl.when(j > q)
        def _():
            b.S[j * rows : (j + 1) * rows, :] = jnp.zeros((rows, b.S.shape[1]), F32)

    b.sp[...] = jnp.zeros_like(b.sp)
    loads["src"].wait()
    pl.semaphore_wait(barrier, len(greeted))

    def ag(h, d):
        place = b.S.at[own, lanes(h)]
        return rcopy(place, place, b.agS.at[h, d], b.agR.at[h, d], at_sep(d))

    for h in HALVES:
        for d in (2, 1, 3):

            @pl.when(q + d < NSEP)
            def _():
                ag(h, d).start()

            later(functools.partial(ag, h, d), q + d < NSEP)

    def ssx(d):
        to = lax.rem(q + d, NSEP)
        return rcopy(b.sp.at[ds(to, cols), :], b.ssb.at[q], b.ssS.at[d], b.ssR.at[d], at_sep(d))

    loads["ssrc"].wait()
    turned = b.ssrc[...].T
    for i in range(NSEP):
        for h in HALVES:
            block = turned[h * nh + i * ch : h * nh + (i + 1) * ch]
            b.sp[i * cols + h * ch : i * cols + (h + 1) * ch, :cols] = block
    b.ssb[q] = b.sp[mine, :]
    for d in range(1, NSEP):
        ssx(d).start()
        later(functools.partial(ssx, d))

    loads["sinv"].wait()
    loads["cpl"].wait()
    def low_of(k, device, slot, m):
        src, dst = ((b.Mo, b.MB), (b.No, b.NB))[m]
        return rcopy(src, dst.at[k], b.moS.at[m, slot], b.mlR.at[m, k], device)

    def send_low(m):
        targets = [(1, at_pair, 0, (core1,))]
        for k in range(2, kp):
            reach = 2 ** (k - 2)
            offsets = [o for o in range(-reach, reach) if o]
            for slot, o in enumerate(offsets):
                targets.append((k, (l + 2 * o, q), slot, (core0, lam == k)))
        for k, device, slot, conditions in targets:

            @when(*conditions)
            def _():
                low_of(k, device, slot, m).start()

            later(functools.partial(low_of, k, device, slot, m), *conditions)
        for k in range(1, kp):

            @when(lam == k)
            def _():
                if m == 0:
                    b.MB[k] = b.Mo[...]
                else:
                    b.NB[k] = b.No[...]

    def sc(m, d):
        src, dst = ((b.Mo, b.PM), (b.No, b.PN))[m]
        return rcopy(
            src.at[ds(y_of(d), mb), :], dst.at[lam], b.scS.at[m, d], b.scR.at[m, lam], at_y(d)
        )

    def wait_sc(m, k):
        dst = (b.PM, b.PN)[m]
        rcopy(dst.at[k], dst.at[k], b.scS.at[m, 0], b.scR.at[m, k], at_pair).wait_recv()

    high = jnp.logical_and(core0, jnp.logical_and(lam >= kp, owner))

    def send_high(m):
        has = (high, lam < depth) if m == 0 else (high,)

        @when(*has)
        def _():
            for d in range(1, ny):
                sc(m, d).start()
            dst, src = ((b.PM, b.Mo), (b.PN, b.No))[m]
            dst[lam] = src[ds(y, mb), :]

        for d in range(1, ny):
            later(functools.partial(sc, m, d), *has)

    sinv = b.sinv[...]
    b.Mo[...] = mm3(b.cpl[...], sinv)
    send_high(0)
    send_low(0)
    b.No[...] = mm3(sinv, sinv, 0, 0)
    send_high(1)
    send_low(1)

    wi = lax.broadcasted_iota(jnp.int32, (w, cap), 0)
    pi = lax.broadcasted_iota(jnp.int32, (w, cap), 1)
    for j in range(depth):
        hit = jnp.logical_and(wi == b.lists[0:1, j * cap : (j + 1) * cap], pi < b.counts[0, j])
        b.pick[j] = jnp.where(hit, 1.0, 0.0).astype(BF16)
    loads["upd"].wait()
    uh, ul = split(b.upd[...])
    b.updh[...] = uh
    b.updl[...] = ul

    def zm(m, d):
        dst = (b.PM, b.PN)[m]
        return rcopy(dst.at[plane], dst.at[plane], b.zmS.at[m, d], b.zmR.at[m, plane], at_z(d))

    def wait_zm(m, k):
        dst = (b.PM, b.PN)[m]
        rcopy(dst.at[k], dst.at[k], b.zmS.at[m, 0], b.zmR.at[m, k], at_pair).wait_recv()

    size = jnp.int32(1)
    for k in range(kp + 1, depth + 1):
        size = size + (plane >= k).astype(jnp.int32) * 2 ** (k - kp - 1)
    base = z - lax.div(size, 2)

    def in_node(d):
        zd = z_of(d)
        return jnp.logical_and(zd >= base, zd < base + size)

    def along_z(m):
        top = depth - 1 if m == 0 else depth

        @when(core0, y != ny // 2)
        def _():
            wait_sc(m, kp)

        @when(core0, y != 0, plane <= top)
        def _():
            wait_sc(m, plane)

        for d in range(1, nz):
            sends = (core0, plane <= top, in_node(d))

            @when(*sends)
            def _():
                zm(m, d).start()

            later(functools.partial(zm, m, d), *sends)

    def wait_low(m, k):
        dst = (b.MB, b.NB)[m]
        rcopy(dst.at[k], dst.at[k], b.moS.at[m, 0], b.mlR.at[m, k], at_pair).wait_recv()

    def fw(m):
        place = (b.MB, b.NB)[m].at[2:kp]
        return rcopy(place, place, b.fwS.at[m], b.fwR.at[m], at_pair)

    def pass_low(m):
        if kp > 2:
            for k in range(2, kp):

                @when(core0, lam != k)
                def _():
                    wait_low(m, k)

            @when(core0)
            def _():
                fw(m).start()

            later(functools.partial(fw, m), core0)

    def have_low(m):
        @when(core0)
        def _():
            wait_low(m, 1)

        if kp > 2:

            @when(core1)
            def _():
                fw(m).wait_recv()

    def yg(m, d):
        dst, src = ((b.MB, b.PM), (b.NB, b.PN))[m]
        hi = depth if m == 0 else depth + 1
        return rcopy(
            src.at[kp:hi], dst.at[kp:hi, ds(y, mb), :], b.ygS.at[m, d], b.ygR.at[m, d], at_y(d)
        )

    def gather_high(m):
        hi = depth if m == 0 else depth + 1

        @when(core0)
        def _():
            for k in range(kp + 1, hi):

                @pl.when(plane != k)
                def _():
                    wait_zm(m, k)

            for h in HALVES:
                for d in range(1, ny):

                    @when(even_at(d), in_half(y_of(d), h))
                    def _():
                        yg(m, d).start()

        for d in range(1, ny):
            later(functools.partial(yg, m, d), core0, even_at(d))

        @when(solver)
        def _():
            dst, src = ((b.MB, b.PM), (b.NB, b.PN))[m]
            dst[kp:hi, ds(y, mb), :] = src[kp:hi]

    def rs(h, j, d):
        to = lax.rem(q + d, NSEP)
        return rcopy(
            b.TT.at[j, chunk(h, to), :],
            b.rsb.at[j, d, part(h)],
            b.rsS.at[h, j, d],
            b.rsR.at[h, j, d],
            at_sep(d),
        )

    loads["inv"].wait()
    ih, il = split(b.inv[...])
    b.ih[...] = ih
    b.il[...] = il
    along_z(0)
    for h in HALVES:
        for d in range(1, NSEP):

            @pl.when(q - d >= 0)
            def _():
                ag(h, d).wait_recv()

        sh, sl = split(b.S[:, lanes(h)])
        ih = b.ih[...]
        yT = (mm(ih, sh) + (mm(b.il[...], sh) + mm(ih, sl))).T
        b.yT[lanes(h), :] = yT
        yh, yl = split(yT)
        for j in range(depth):
            bh = b.updh[:, j * cap : (j + 1) * cap]
            bl = b.updl[:, j * cap : (j + 1) * cap]
            b.TT[j, lanes(h), :] = mm(yh, bh) + (mm(yl, bh) + mm(yh, bl))
            for d in (2, 1, 3):
                rs(h, j, d).start()
                later(functools.partial(rs, h, j, d))
        if h == 0:
            gather_high(0)
        else:
            along_z(1)

    pass_low(0)

    for d in range(1, NSEP):
        ssx(d).wait_recv()
    sT = jnp.concatenate([b.ssb[i][:, :cols] for i in range(NSEP)], axis=1)
    b.sT[...] = sT

    def prepare(k):
        if k < depth:
            mh, ml = split(b.MB[k])
            b.Mh[k] = mh
            b.Ml[k] = ml
            th, tl = split(b.MB[k].T)
            b.Th[k] = th
            b.Tl[k] = tl

    def prepare_n(k):
        nh, nl = split(b.NB[k])
        b.Nh[k] = nh
        b.Nl[k] = nl

    have_low(0)
    for k in range(1, kp):
        prepare(k)


    def own_part(h, k):
        for d in range(1, NSEP):
            rs(h, k - 1, d).wait_recv()
        r = part(h)
        t = (b.TT[k - 1, chunk(h, q), :] + b.rsb[k - 1, 1, r]) + (
            b.rsb[k - 1, 2, r] + b.rsb[k - 1, 3, r]
        )
        mine_k = jnp.where(lam == k, b.sT[r, :], 0.0) - picked_by(t, b.pick[k - 1], 1)
        if 1 < k <= kp:
            mine_k = mine_k - chain(b.RP[k - 1, r], b.Th[k - 1], b.Tl[k - 1])
        b.RP[k, r] = mine_k

    groups = ((2, kp), (kp, depth), (depth, depth + 1))
    sums_on = (core1, core0, core0)
    sends_to_pair = (core0, core1, core1)

    def r1():
        return rcopy(b.RP.at[1], b.R1, b.cxS.at[0, 3], b.cxR.at[0, 3], at_pair)

    def cx(h, i):
        lo, hi = groups[i]
        return rcopy(
            b.RP.at[lo:hi, part(h)],
            b.CX.at[lo:hi, part(h)],
            b.cxS.at[h, i],
            b.cxR.at[h, i],
            at_pair,
        )

    def hr(i, d):
        lo, hi = groups[i]
        if i == 0:
            src, dst = b.H.at[lo:hi, ds(y_of(d), rb), :], b.HR.at[y]
        else:
            src = b.H.at[lo:hi, ds(lax.div(y_of(d), 2), rh), :]
            dst = b.HH.at[y, lo - kp : hi - kp]
        return rcopy(src, dst, b.hrS.at[i, d], b.hrR.at[i, d], at_y(d))

    def share(h, i):
        lo, hi = groups[i]

        @when(sends_to_pair[i])
        def _():
            cx(h, i).start()

        later(functools.partial(cx, h, i), sends_to_pair[i])

        @when(sums_on[i])
        def _():
            cx(h, i).wait_recv()
            r = part(h)
            b.H[lo:hi, r] = b.RP[lo:hi, r] + b.CX[lo:hi, r]
            for d in range(1, ny):
                goes = in_half(y_of(d), h)

                @pl.when(jnp.logical_and(goes, even_at(d)) if i else goes)
                def _():
                    hr(i, d).start()

        if i:

            @when(solver, in_half(y, h))
            def _():
                b.HH[y, lo - kp : hi - kp] = b.H[lo:hi, ds(lax.div(y, 2), rh), :]

        else:

            @when(core1, in_half(y, h))
            def _():
                b.HR[y] = b.H[lo:hi, ds(y, rb), :]

    for i in range(3):
        for d in range(1, ny):
            later(functools.partial(hr, i, d), sums_on[i], *((even_at(d),) if i else ()))

    for h in HALVES:
        for k in range(1, kp):
            own_part(h, k)
        if h == 1:
            r1().start()
            later(r1)
        share(h, 0)
        for k in range(kp, depth):
            own_part(h, k)
        share(h, 1)
        own_part(h, depth)
        share(h, 2)
        if h == 1:
            gather_high(1)
    pass_low(1)

    def br(d):
        place = b.RF.at[2:kp, ds(y, rb), :]
        return rcopy(b.B.at[y_of(d)], place, b.brS.at[d], b.brR.at[d], at_y(d))

    def z_xor(i):
        other = z
        for bit in range(nz.bit_length() - 1):
            if i >> bit & 1:
                other = other + 2**bit - 2 ** (bit + 1) * lax.rem(lax.div(z, 2**bit), 2)
        return other

    def zr(k, i):
        device = (l + 2 * ny * (z_xor(i) - z), q)
        at = k - kp - 1
        return rcopy(b.ZT.at[at], b.ZR.at[at, z], b.zrS.at[at, i], b.zrR.at[at, i], device)

    def bz(k, d):
        place = b.X.at[k, ds(lax.div(y, 2), rh), :]
        return rcopy(b.BZ.at[k - kp], place, b.bzS.at[k - kp, d], b.bzR.at[k - kp, d], at_y(d))

    def back_low():
        place = b.RF.at[2:kp]
        return rcopy(place, place, b.bkS.at[0], b.bkR.at[0], at_pair)

    def back_high(h, k):
        place = b.X.at[k, part(h)]
        return rcopy(place, place, b.bhS.at[h, k], b.bhR.at[h, k], at_pair)

    @when(core1)
    def _():
        for d in range(1, ny):
            hr(0, d).wait_recv()
        for k in range(2, kp):
            step = 2 ** (k - 1)
            for g in range(0, ny, step):
                total = b.HR[g, k - 2]
                for i in range(1, step):
                    total = total + b.HR[g + i, k - 2]
                for i in range(step):
                    b.B[g + i, k - 2] = total
        for d in range(1, ny):
            br(d).start()
        b.RF[2:kp, ds(y, rb), :] = b.B[y]
        for d in range(1, ny):
            br(d).wait_recv()
        back_low().start()

    for d in range(1, ny):
        later(functools.partial(br, d), core1)
    later(back_low, core1)

    @when(solver)
    def _():
        for d in range(1, ny):
            yg(0, d).wait_recv()
        for k in range(kp, depth):
            prepare(k)
        for k in range(kp, depth + 1):
            if k == kp or k == depth:
                for d in range(1, ny):
                    hr(1 if k == kp else 2, d).wait_recv()
            total = b.HH[0, k - kp]
            for i in range(1, ny):
                total = total + b.HH[i, k - kp]
            if k > kp:
                total = total - chain(b.RZ[k - 1], b.Th[k - 1], b.Tl[k - 1])
                b.ZT[k - kp - 1] = total
                for i in range(1, 2 ** (k - kp)):
                    zr(k, i).start()
                b.ZR[k - kp - 1, z] = total
            b.RZ[k] = total

    for k in range(kp + 1, depth + 1):
        for i in range(1, 2 ** (k - kp)):
            later(functools.partial(zr, k, i), solver)

    @when(solver)
    def _():
        for d in range(1, ny):
            yg(1, d).wait_recv()
        for k in range(kp, depth + 1):
            prepare_n(k)
        for k in range(kp, depth + 1):
            total = b.RZ[k]
            if k > kp:
                step = 2 ** (k - kp)
                for i in range(1, step):
                    zr(k, i).wait_recv()
                first = z - lax.rem(z, step)
                total = b.ZR[k - kp - 1, first]
                for i in range(1, step):
                    total = total + b.ZR[k - kp - 1, first + i]
            b.BZ[k - kp] = chain(total, b.Nh[k], b.Nl[k])
        for k in range(depth, kp - 1, -1):
            if k < depth:
                b.BZ[k - kp] = b.BZ[k - kp] - chain(b.BZ[k + 1 - kp], b.Mh[k], b.Ml[k])
            for d in range(1, ny):
                bz(k, d).start()
            b.X[k, ds(lax.div(y, 2), rh), :] = b.BZ[k - kp]

    have_low(1)
    for k in range(1, kp):
        prepare_n(k)
    r1().wait_recv()
    b.RF[1] = b.RP[1] + b.R1[...]

    @when(core0)
    def _():
        back_low().wait_recv()

    for k in range(1, kp):
        b.V[k] = chain(b.RF[k], b.Nh[k], b.Nl[k])

    def arrive(h, k):
        @when(core0)
        def _():
            for d in range(1, ny):

                @when(even_at(d), in_half(y_of(ny - d), h))
                def _():
                    bz(k, d).wait_recv()

            back_high(h, k).start()

        @when(core1)
        def _():
            back_high(h, k).wait_recv()

    for k in range(kp, depth + 1):
        for d in range(1, ny):
            later(functools.partial(bz, k, d), solver)
        for h in HALVES:
            later(functools.partial(back_high, h, k), core0)

    def pk(h, j, d):
        place = b.pkb.at[chunk(h, q), (j - 1) * cap : j * cap]
        return rcopy(place, place, b.pkS.at[h, j, d], b.pkR.at[h, j, d], at_sep(d))

    for h in HALVES:
        r = part(h)
        for j in range(depth, 0, -1):
            if j >= kp:
                arrive(h, j)
            if j <= kp and j > 1:
                b.X[j - 1, r] = b.V[j - 1, r] - chain(b.X[j, r], b.Mh[j - 1], b.Ml[j - 1])
            b.pkb[chunk(h, q), (j - 1) * cap : j * cap] = picked_by(b.X[j, r], b.pick[j - 1], 0)
            for d in (2, 1, 3):
                pk(h, j, d).start()

    def xo(d):
        to = lax.rem(q + d, NSEP)
        return rcopy(b.xp.at[ds(to, cols), :], b.xob.at[q], b.xS.at[d], b.xR.at[d], at_sep(d))

    b.xp[...] = jnp.zeros_like(b.xp)

    @when(owner)
    def _():
        b.xp[:, :cols] = b.X[lam].T

    b.xob[q] = b.xp[mine, :]
    for d in range(1, NSEP):
        xo(d).start()

    settle()
    for d in range(1, NSEP):
        later(functools.partial(xo, d))
        for h in HALVES:
            for j in range(1, depth + 1):
                later(functools.partial(pk, h, j, d))

    def fin(h, d):
        to = q - d
        return rcopy(
            b.XB.at[ds(to, rows), lanes(h)],
            b.fb.at[d, :, lanes(h)],
            b.fS.at[h, d],
            b.fR.at[h, d],
            (l, to),
        )

    def wait_fin(h, d):
        place = b.fb.at[d, :, lanes(h)]
        rcopy(place, place, b.fS.at[h, d], b.fR.at[h, d], at_sep(d)).wait_recv()

    for h in HALVES:
        for j in range(depth, 0, -1):
            for d in range(1, NSEP):
                pk(h, j, d).wait_recv()
        ph, pw = split(b.pkb[lanes(h), :])
        uh = b.updh[...]
        wT = b.yT[lanes(h), :] - (mm(ph, uh, 1, 1) + (mm(pw, uh, 1, 1) + mm(ph, b.updl[...], 1, 1)))
        wh, wl = split(wT.T)
        ih = b.ih[...]
        b.XB[:, lanes(h)] = mm(ih, wh, 0, 0) + (mm(b.il[...], wh, 0, 0) + mm(ih, wl, 0, 0))
        for d in (2, 1, 3):

            @pl.when(q - d >= 0)
            def _():
                fin(h, d).start()

    settle()
    for h in HALVES:
        for d in range(1, NSEP):
            later(functools.partial(fin, h, d), q - d >= 0)

    for d in range(1, NSEP):
        xo(d).wait_recv()
    b.sol[...] = jnp.concatenate(
        [b.xob[i][:, h * ch : (h + 1) * ch] for h in HALVES for i in range(NSEP)], axis=1
    )
    for h in HALVES:
        b.out[:, lanes(h)] = b.XB[own, lanes(h)]
        for d in range(1, NSEP):

            @pl.when(q + d < NSEP)
            def _():
                wait_fin(h, d)
                b.out[:, lanes(h)] += b.fb[d, :, lanes(h)]

    settle()


def per_device(ny, nz, src, inv, upd, lists, counts, ssrc, sinv, cpl):
    depth = counts.shape[1]
    rows, n = src.shape[1:]
    order = inv.shape[2]
    urows = upd.shape[1]
    cols = ssrc.shape[1]
    w = sinv.shape[1]
    cap = urows // depth
    s = depth + 1
    kp = depth - nz.bit_length() + 1
    rb = cols // ny
    mb = w // ny
    f = lambda *shape: pltpu.VMEM(shape, F32)
    h = lambda *shape: pltpu.VMEM(shape, BF16)
    dma = lambda *shape: pltpu.SemaphoreType.DMA(shape)
    vm = pl.BlockSpec(memory_space=pltpu.VMEM)
    hbm = pl.BlockSpec(memory_space=pl.ANY)
    scratch = dict(
        ssrc=f(cols, n),
        sinv=f(w, w),
        cpl=f(w, w),
        inv=f(rows, order),
        upd=f(rows, urows),
        ldS=dma(6),
        S=f(order, n),
        sp=f(n, 128),
        ssb=f(NSEP, cols, 128),
        sT=f(cols, w),
        Mo=f(w, w),
        No=f(w, w),
        MB=f(s, w, w),
        NB=f(s, w, w),
        PM=f(s, mb, w),
        PN=f(s, mb, w),
        Mh=h(s, w, w),
        Ml=h(s, w, w),
        Th=h(s, w, w),
        Tl=h(s, w, w),
        Nh=h(s, w, w),
        Nl=h(s, w, w),
        pick=h(depth, w, cap),
        yT=f(n, rows),
        updh=h(rows, urows),
        updl=h(rows, urows),
        TT=f(depth, n, cap),
        rsb=f(depth, NSEP, cols, cap),
        RP=f(s, cols, w),
        R1=f(cols, w),
        CX=f(s, cols, w),
        H=f(s, cols, w),
        HR=f(ny, kp - 2, rb, w),
        HH=f(ny, depth - kp + 1, 2 * rb, w),
        B=f(ny, kp - 2, rb, w),
        RZ=f(s, 2 * rb, w),
        ZT=f(depth - kp, 2 * rb, w),
        ZR=f(depth - kp, nz, 2 * rb, w),
        BZ=f(depth - kp + 1, 2 * rb, w),
        RF=f(kp, cols, w),
        V=f(kp, cols, w),
        X=f(s, cols, w),
        pkb=f(n, urows),
        XB=f(order, n),
        fb=f(NSEP, rows, n),
        xp=f(n, 128),
        xob=f(NSEP, cols, 128),
        ih=h(rows, order),
        il=h(rows, order),
        agS=dma(2, NSEP),
        agR=dma(2, NSEP),
        ssS=dma(NSEP),
        ssR=dma(NSEP),
        moS=dma(2, 8),
        mlR=dma(2, s),
        scS=dma(2, ny),
        scR=dma(2, s),
        zmS=dma(2, nz),
        zmR=dma(2, s),
        ygS=dma(2, ny),
        ygR=dma(2, ny),
        fwS=dma(2),
        fwR=dma(2),
        rsS=dma(2, depth, NSEP),
        rsR=dma(2, depth, NSEP),
        cxS=dma(2, 4),
        cxR=dma(2, 4),
        hrS=dma(3, ny),
        hrR=dma(3, ny),
        brS=dma(ny),
        brR=dma(ny),
        bzS=dma(depth - kp + 1, ny),
        bzR=dma(depth - kp + 1, ny),
        zrS=dma(depth - kp, nz),
        zrR=dma(depth - kp, nz),
        bkS=dma(1),
        bkR=dma(1),
        bhS=dma(2, s),
        bhR=dma(2, s),
        pkS=dma(2, s, NSEP),
        pkR=dma(2, s, NSEP),
        xS=dma(NSEP),
        xR=dma(NSEP),
        fS=dma(2, NSEP),
        fR=dma(2, NSEP),
    )
    operands = ["counts", "xsrc", "xinv", "xupd", "lists", "xssrc", "xsinv", "xcpl", "out", "sol"]
    out, sol = pl.pallas_call(
        functools.partial(kernel, (ny, nz, depth), operands + list(scratch)),
        out_shape=(
            jax.ShapeDtypeStruct((rows, n), F32),
            jax.ShapeDtypeStruct((cols, n), F32),
        ),
        in_specs=[pl.BlockSpec(memory_space=pltpu.SMEM)] + [hbm] * 3 + [vm] + [hbm] * 3,
        out_specs=(vm, vm),
        scratch_shapes=list(scratch.values()),
        compiler_params=pltpu.CompilerParams(
            collective_id=0, has_side_effects=True, vmem_limit_bytes=62 * 2**20
        ),
    )(counts, src[0], inv[0], upd[0].T, lists, ssrc[0], sinv[0], cpl[0])
    return out[None], sol[None]


def solution(mesh):
    leaves = mesh.shape["leaf"]
    ny = nz = 8
    if leaves != 2 * ny * nz:
        ny, nz = (leaves // 4, 2)
    placed = (
        P("leaf", "sep", None),
        P("leaf", "sep", None),
        P("leaf", None, "sep"),
        P("leaf", None),
        P("leaf", None),
        P("leaf", "sep", None),
        P("leaf", None, None),
        P("leaf", None, None),
    )
    return jax.shard_map(
        functools.partial(per_device, ny, nz),
        mesh=mesh,
        in_specs=placed,
        out_specs=(P("leaf", "sep", None), P("leaf", "sep", None)),
        check_vma=False,
    )
```
